32 devices in a mesh: fsdp: 2 (over core), expert: 16 (over z, y, x).
Axes of the slice: x: 2, y: 2, z: 4, core: 2. Of those that a mesh axis runs over, the one named last changes fastest.
Arguments:
- tokens: bfloat16 [16, 2048, 1024], P('expert', 'fsdp'), may hold values from -6 to 6
- out_grad: bfloat16 [16, 2048, 1024], P('expert', 'fsdp'), may hold values from -8 to 8
- routes: int32 [16, 2048, 1], P('expert', 'fsdp'), may hold values from 0 to 15; in each aligned block of 1024 rows (0 to 1023, 1024 to 2047, ..., all dimensions but the last counted through in order) at most 128 rows name the same one
- prefix: int32 [16], P('expert'), may hold values from 204 to 1024
- ln1_gain: bfloat16 [1024], P('fsdp'), may hold values from 0.5 to 1.5
- ln1_bias: bfloat16 [1024], P('fsdp'), may hold values from -0.625 to 0.625
- w_qkv: bfloat16 [1024, 3072], P('fsdp'), may hold values from -0.1875 to 0.1875
- q_bias: bfloat16 [1024], P('fsdp'), may hold values from -0.625 to 0.625
- v_bias: bfloat16 [1024], P('fsdp'), may hold values from -0.625 to 0.625
- attention_output_weight: bfloat16 [1024, 1024], P('fsdp'), may hold values from -4 to 4
- attention_output_bias: bfloat16 [1024], P('fsdp'), may hold values from -0.625 to 0.625
- ln2_gain: bfloat16 [1024], P('fsdp'), may hold values from 0.5 to 1.5
- ln2_bias: bfloat16 [1024], P('fsdp'), may hold values from -0.625 to 0.625
- w_router: bfloat16 [1024, 16], P('fsdp'), may hold values from -0.09375 to 0.09375
- moe_bias: bfloat16 [1024], P('fsdp'), may hold values from -0.625 to 0.625
- w_in: bfloat16 [16, 1024, 4096], P('expert', None, 'fsdp'), may hold values from -0.1875 to 0.1875
- w_down: bfloat16 [16, 4096, 1024], P('expert', 'fsdp'), may hold values from -1.5 to 1.5
Outputs:
- out: bfloat16 [16, 2048, 1024], P('expert', 'fsdp')
- d_tokens: bfloat16 [16, 2048, 1024], P('expert', 'fsdp')
- d_ln1_gain: float32 [1024], P(('fsdp', 'expert'))
- d_ln1_bias: float32 [1024], P(('fsdp', 'expert'))
- d_w_qkv: float32 [1024, 3072], P(('fsdp', 'expert'))
- d_q_bias: float32 [1024], P(('fsdp', 'expert'))
- d_v_bias: float32 [1024], P(('fsdp', 'expert'))
- d_w_out: float32 [1024, 1024], P(('fsdp', 'expert'))
- d_out_bias: float32 [1024], P(('fsdp', 'expert'))
- d_ln2_gain: float32 [1024], P(('fsdp', 'expert'))
- d_ln2_bias: float32 [1024], P(('fsdp', 'expert'))
- d_w_router: float32 [1024, 16], P(('fsdp', 'expert'))
- d_moe_bias: float32 [1024], P(('fsdp', 'expert'))
- d_w_in: float32 [16, 1024, 4096], P('expert', None, 'fsdp')
- d_w_down: float32 [16, 4096, 1024], P('expert', 'fsdp')
The draws below stay inside these ranges and needn't reach their ends.
Inputs may be any that keep to these rules, and one draw needn't show every extreme that they name: `routes`: in each aligned block of 1024 rows (the positions of one sequence on one device) at most 128 rows name the same expert, and some block has 128 that do.
All inputs are finite; a program needn't handle non-finite values.
Results may differ from the reference program's by a relative error of at most 0.02.
Values may be sent and summed in bfloat16 or wider, within the bound.
No kernel may reach another device: no remote copies, remote signals or barrier semaphores. Data moves between devices by JAX's collectives and lax.ppermute only.
A program may use at most 384 MiB of HBM per device.

```python
import math
from functools import partial
import jax
import jax.numpy as jnp
import numpy as np
from jax import lax

D = 1024
HEADS = 16
HEAD_DIM = 64
H = 4096
ROWS = 1024
EXPERTS = 16
LEN = 2048
SEQS = 16
MOST = 128
N_FSDP = 2


def touch_ends(array, rng, least, high):
    longest = array.shape.index(max(array.shape))
    spots = []
    for shift in (0, 1):
        where = [jax.random.randint(jax.random.fold_in(rng, axis), (), 0, length) for axis, length in enumerate(array.shape)]
        where[longest] = (where[longest] + shift) % array.shape[longest]
        spots.append(tuple(where))
    return array.at[spots[0]].set(least).at[spots[1]].set(high)


def strengthened(drawn, key, source, target, blocks, factor):
    def block_of(position):
        return (jnp.arange(drawn.shape[position]) // (drawn.shape[position] // blocks)).reshape((-1,) + (1,) * (drawn.ndim - 1 - position))

    near = jax.random.permutation(key, blocks)[block_of(target)]
    second = (block_of(target) + blocks // 2) % blocks
    return jnp.where((block_of(source) == near) | (block_of(source) == second), factor * drawn, drawn)


def shard_levels(key, extent, cuts, least, largest):
    level, own = 1.0, jax.random.fold_in(key, 6)
    for dim, parts in cuts:
        draws = jnp.exp(jax.random.uniform(jax.random.fold_in(own, dim), (parts,), jnp.float32, least / len(cuts), largest / len(cuts)))
        level = level * jnp.repeat(draws, extent[dim] // parts).reshape([-1 if axis == dim else 1 for axis in range(len(extent))])
    return level


def deal_out(rng, own, number, rows, number_of, top, limit, slope):
    order = jax.random.permutation(rng, number_of)
    packed, common = portions_of(number_of, rows * top, limit, slope, True), portions_of(number_of, rows * top, limit, slope, False)
    places = jnp.arange(number_of)

    def named(sizes, turn):
        used = int((sizes > 0).sum())
        fixed = max(1, used // 4)
        passed = fixed + (places - fixed + turn * (used - fixed)) % max(1, number_of - fixed)
        return jnp.zeros((number_of,), jnp.int32).at[order[jnp.where(places < fixed, places, passed)]].set(jnp.asarray(sizes, jnp.int32))

    sizes = jnp.where(number % 4 == 0, named(packed, number // 4), named(common, number - number // 4 - 1))
    mixed = jax.random.permutation(jax.random.fold_in(own, 3), number_of)
    donor, taker = mixed[0:number_of // 2 * 2:2], mixed[1:number_of // 2 * 2:2]
    margin = jnp.minimum(sizes[donor] - 1, limit - sizes[taker]) // 2
    margin = jnp.where((donor == order[0]) | (taker == order[0]) | (sizes[taker] == 0), 0, jnp.maximum(margin, 0))
    passed = jax.random.randint(jax.random.fold_in(own, 4), (number_of // 2,), 0, 1 << 20) % (margin + 1)
    sizes = sizes.at[donor].add(-passed).at[taker].add(passed)
    labels = jnp.searchsorted(jnp.cumsum(sizes), jnp.arange(rows * top), side="right").astype(jnp.int32)
    grid = labels.reshape(top, rows).T
    grid = grid[jax.random.permutation(jax.random.fold_in(own, 1), rows)]
    turn = jax.random.randint(jax.random.fold_in(own, 2), (rows, 1), 0, top)
    return jnp.take_along_axis(grid, (jnp.arange(top)[None, :] + turn) % top, axis=1)


def portions_of(amount, total, reach, slope, full):
    loads = [(1 << 20) // math.isqrt(rank ** slope) + 1 for rank in range(1, amount + 1)]
    largest = reach if full else min(reach, max(-(-total // amount), total * loads[0] // sum(loads)))
    least = 1 if total - largest >= amount - 1 else 0
    given, surplus = [largest] + [least] * (amount - 1), total - largest - least * (amount - 1)
    while surplus > 0:
        candidates = [i for i in range(1, amount) if given[i] < largest] or [i for i in range(1, amount) if given[i] < reach]
        mass, budget = sum([loads[i] for i in candidates]), surplus
        for i in candidates:
            addition = min(reach - given[i], max(1, budget * loads[i] // mass), surplus)
            given[i] = given[i] + addition
            surplus = surplus - addition
    return np.array(given)


def centred(own_key, shape, width, most, split=(), kind=jnp.bfloat16):
    values = jax.random.normal(own_key, shape, jnp.float32) * width
    if len(split) > 0:
        values = shard_levels(own_key, shape, split, -0.22, 0.18) * values
    return jnp.clip(values, min=-most, max=most).astype(kind)


def gaussian_with(rng, dims, width, limit, pieces, heavy, kind=jnp.bfloat16):
    values = width * jax.random.normal(rng, dims, jnp.float32)
    if pieces:
        values = values * shard_levels(rng, dims, pieces, -0.22, 0.18)
    return jnp.clip(strengthened(values, jax.random.fold_in(rng, 3), *heavy), -limit, limit).astype(kind)


def setup_inputs(seed: int = 0) -> dict:
    seeds = jax.random.split(jax.random.key(seed), 18)
    tokens = centred(seeds[0], (SEQS, LEN, D), 1.0, 6.0, ((0, 16), (1, 2)))
    out_grad = gaussian_with(seeds[1], (SEQS, LEN, D), 1.0, 8.0, ((0, 16), (1, 2)), (0, 2, 16, 2.0))
    routes_keys = jax.random.split(jax.random.fold_in(seeds[2], 1), SEQS * LEN // ROWS)
    routes_turns = jax.random.permutation(jax.random.fold_in(seeds[2], 3), SEQS * LEN // ROWS)
    routes = jax.vmap(lambda own, number: deal_out(jax.random.fold_in(seeds[2], 2), own, number, ROWS, EXPERTS, 1, MOST, 2))(routes_keys, routes_turns).reshape((SEQS, LEN, 1))
    prefix = touch_ends(jax.random.randint(seeds[3], (SEQS,), LEN // 10, LEN // 2 + 1), jax.random.fold_in(seeds[3], 1), LEN // 10, (LEN // 2 + 1) - 1).astype(jnp.int32)
    ln1_gain = jnp.clip(1.0 + 0.1 * jax.random.normal(seeds[4], (D,), jnp.float32), 0.5, 1.5).astype(jnp.bfloat16)
    ln1_bias = centred(seeds[5], (D,), 0.1, 0.625, ((0, 2),))
    w_qkv = centred(seeds[6], (D, 3 * D), D ** -0.5, 0.1875, ((0, 2),))
    q_bias = centred(seeds[7], (D,), 0.1, 0.625, ((0, 2),))
    v_bias = centred(seeds[8], (D,), 0.1, 0.625, ((0, 2),))
    attention_output_weight = centred(seeds[9], (D, D), (max(1, 4 * D // LEN)) ** -0.5, 4.0, ((0, 2),))
    attention_output_bias = centred(seeds[10], (D,), 0.1, 0.625, ((0, 2),))
    ln2_gain = jnp.clip(1.0 + 0.1 * jax.random.normal(seeds[11], (D,), jnp.float32), 0.5, 1.5).astype(jnp.bfloat16)
    ln2_bias = centred(seeds[12], (D,), 0.1, 0.625, ((0, 2),))
    w_router = centred(seeds[13], (D, EXPERTS), (4 * D) ** -0.5, 0.09375, ((0, 2),))
    moe_bias = centred(seeds[14], (D,), 0.1, 0.625, ((0, 2),))
    w_in = centred(seeds[15], (EXPERTS, D, H), D ** -0.5, 0.1875, ((0, 16), (2, 2)))
    w_down = centred(seeds[16], (EXPERTS, H, D), (max(1, H // (EXPERTS * EXPERTS))) ** -0.5, 1.5, ((0, 16), (1, 2)))
    return {"tokens": tokens, "out_grad": out_grad, "routes": routes, "prefix": prefix, "ln1_gain": ln1_gain, "ln1_bias": ln1_bias, "w_qkv": w_qkv, "q_bias": q_bias, "v_bias": v_bias, "attention_output_weight": attention_output_weight, "attention_output_bias": attention_output_bias, "ln2_gain": ln2_gain, "ln2_bias": ln2_bias, "w_router": w_router, "moe_bias": moe_bias, "w_in": w_in, "w_down": w_down}


FULL_PRECISION = lax.Precision.HIGHEST
NORM_EPSILON = 1e-05
MASK_FILL = -1e+30

@jax.custom_vjp
def low(v):
    return lax.optimization_barrier(v.astype(jnp.bfloat16)).astype(jnp.float32)

@jax.custom_vjp
def lower_backward(v):
    return v

def low_keep(v):
    return (low(v), None)

def low_pass(kept, grad):
    return (grad,)

def back_keep(v):
    return (v, None)

def back_low(kept, grad):
    return (low(grad),)
low.defvjp(low_keep, low_pass)
lower_backward.defvjp(back_keep, back_low)

def layer_norm(values, norm_gain, norm_bias):
    center = values - lax.optimization_barrier(jnp.mean(values, axis=-1, keepdims=True))
    inv_std = lax.rsqrt(lax.optimization_barrier(jnp.mean(center * center, axis=-1, keepdims=True)) + NORM_EPSILON)
    return center * inv_std * norm_gain + norm_bias

def attend(queries, key_rows, values, prefix_len):
    block_rows = math.gcd(LEN, 512)
    key_pos = jnp.arange(LEN, dtype=jnp.int32)

    def one_block(block_index):
        offset = block_index * block_rows
        query_part = lax.dynamic_slice_in_dim(queries, offset, block_rows, 0)
        scores = lower_backward(jnp.einsum('qhd,khd->hqk', query_part, key_rows, precision=FULL_PRECISION))
        query_pos = offset + jnp.arange(block_rows, dtype=jnp.int32)
        allowed = (key_pos[None, :] <= query_pos[:, None]) | (key_pos[None, :] < prefix_len)
        attention = jax.nn.softmax(jnp.where(allowed[None], scores, MASK_FILL), axis=-1)
        return jnp.einsum('hqk,khd->qhd', low(attention), values, precision=FULL_PRECISION)
    blocks = lax.map(jax.checkpoint(one_block), jnp.arange(LEN // block_rows, dtype=jnp.int32))
    return blocks.reshape(LEN, D)

def apply_experts(rows_in, token_route, w_in, w_down):
    capacity = SEQS * N_FSDP * MOST
    sorted_rows = jnp.argsort(token_route, stable=True).astype(jnp.int32)
    expert_ids = jnp.arange(EXPERTS, dtype=jnp.int32)
    counts = lax.optimization_barrier(jnp.sum((token_route[:, None] == expert_ids[None, :]).astype(jnp.int32), axis=0)).astype(jnp.int32)
    starts = (jnp.cumsum(counts) - counts).astype(jnp.int32)
    padded = jnp.concatenate([sorted_rows, jnp.zeros((capacity,), jnp.int32)])
    slot_ids = jnp.arange(capacity, dtype=jnp.int32)
    index_table = padded[(starts[:, None] + slot_ids[None, :]).astype(jnp.int32)]
    valid_table = (slot_ids[None, :] < counts[:, None]).astype(jnp.float32)

    def one_expert(inputs):
        row_index, row_valid, weight_in, weight_down = inputs
        picked = rows_in[row_index] * row_valid[:, None]
        pre_act = lower_backward(jnp.dot(picked, weight_in, precision=FULL_PRECISION))
        activation = low(jax.nn.gelu(pre_act, approximate=True))
        return jnp.dot(activation, weight_down, precision=FULL_PRECISION) * row_valid[:, None]
    results = lax.map(jax.checkpoint(one_expert), (index_table, valid_table, w_in, w_down))
    return jnp.zeros((SEQS * LEN, D), jnp.float32).at[index_table.reshape(-1)].add(results.reshape(-1, D))

def forward(token_route, prefix, tokens, ln1_gain, ln1_bias, w_qkv, q_bias, v_bias, attention_output_weight, attention_output_bias, ln2_gain, ln2_bias, w_router, moe_bias, w_in, w_down):
    query_scale = HEAD_DIM ** (-0.5)
    head_shape = (LEN, HEADS, HEAD_DIM)

    def one_sequence(carried, inputs):
        seq_tokens, prefix_len = inputs
        normed = low(layer_norm(seq_tokens, ln1_gain, ln1_bias))
        projected = jnp.dot(normed, w_qkv, precision=FULL_PRECISION)
        queries = low(lower_backward((projected[:, :D] + q_bias) * query_scale))
        key_rows = low(lower_backward(projected[:, D:2 * D]))
        values = low(lower_backward(projected[:, 2 * D:] + v_bias))
        return (carried, attend(queries.reshape(head_shape), key_rows.reshape(head_shape), values.reshape(head_shape), prefix_len))
    unused, context_vectors = lax.scan(jax.checkpoint(one_sequence), jnp.zeros((), jnp.float32), (tokens, prefix))
    context_vectors = low(lower_backward(context_vectors))
    attention_result = lower_backward(jnp.einsum('prm,mi->pri', context_vectors, attention_output_weight, precision=FULL_PRECISION) + attention_output_bias)
    hidden = tokens + attention_result
    mixed_low = low(layer_norm(hidden, ln2_gain, ln2_bias)).reshape(SEQS * LEN, D)
    logits = lower_backward(jnp.dot(mixed_low, w_router, precision=FULL_PRECISION))
    router_probs = jax.nn.softmax(logits, axis=-1)
    gate_value = jnp.take_along_axis(router_probs, token_route[:, None], axis=1)[:, 0]
    expert_value = low(lower_backward(apply_experts(lower_backward(mixed_low), token_route, w_in, w_down)))
    moe_out = gate_value[:, None] * expert_value + moe_bias
    return hidden + moe_out.reshape(SEQS, LEN, D)

def reference(tokens, out_grad, routes, prefix, ln1_gain, ln1_bias, w_qkv, q_bias, v_bias, attention_output_weight, attention_output_bias, ln2_gain, ln2_bias, w_router, moe_bias, w_in, w_down):
    token_route = routes.reshape(SEQS * LEN).astype(jnp.int32)
    floats = tuple((argument.astype(jnp.float32) for argument in (tokens, ln1_gain, ln1_bias, w_qkv, q_bias, v_bias, attention_output_weight, attention_output_bias, ln2_gain, ln2_bias, w_router, moe_bias, w_in, w_down)))
    output, pullback = jax.vjp(partial(forward, token_route, prefix), *floats)
    gradients = pullback(out_grad.astype(jnp.float32))
    return (output.astype(jnp.bfloat16), gradients[0].astype(jnp.bfloat16), gradients[1], gradients[2], gradients[3], gradients[4], gradients[5], gradients[6], gradients[7], gradients[8], gradients[9], gradients[10], gradients[11], gradients[12], gradients[13])
```

```python
from functools import partial

import jax
import jax.numpy as jnp
from jax import lax
from jax.experimental import pallas as pl
from jax.experimental.pallas import tpu as pltpu
from jax.sharding import PartitionSpec as P

HEAD_DIM = 64
NORM_EPSILON = 1e-05
MASK_FILL = -1e30
LOG2E = 1.4426950408889634
GELU_A = 0.7978845608028654
GELU_B = 0.044715
CHUNKS = 2
LANES = 128
BF16 = jnp.bfloat16
F32 = jnp.float32
VMEM_LIMIT = 56 << 20


def nn(left, right):
    return lax.dot_general(left, right, (((1,), (0,)), ((), ())), preferred_element_type=F32)


def nt(left, right):
    return lax.dot_general(left, right, (((1,), (1,)), ((), ())), preferred_element_type=F32)


def tn(left, right):
    return lax.dot_general(left, right, (((0,), (0,)), ((), ())), preferred_element_type=F32)


def lane_index(rows):
    return lax.broadcasted_iota(jnp.int32, (rows, LANES), 1)


def split_queries(queries):
    scaled = queries.astype(F32) * LOG2E
    high = scaled.astype(BF16).astype(F32)
    low = scaled - high
    first = lane_index(queries.shape[0]) < HEAD_DIM
    head_a = jnp.where(first, high, pltpu.roll(low, HEAD_DIM, 1)).astype(BF16)
    head_b = jnp.where(first, pltpu.roll(high, HEAD_DIM, 1), low).astype(BF16)
    return head_a, head_b


def twice(keys):
    wide = keys.astype(F32)
    rolled = pltpu.roll(wide, HEAD_DIM, 1)
    first = lane_index(keys.shape[0]) < HEAD_DIM
    return jnp.where(first, wide, rolled).astype(BF16), jnp.where(first, rolled, wide).astype(BF16)


def in_three(values):
    high = values.astype(BF16).astype(F32)
    rest = values - high
    middle = rest.astype(BF16).astype(F32)
    return high, middle, rest - middle


def three_columns(values, place):
    high, middle, low = in_three(values)
    return jnp.where(
        place == 0, high, jnp.where(place == 1, middle, jnp.where(place == 2, low, 0.0))
    )


def forward_kernel(
    block_q,
    block_k,
    scalars,
    q_ref,
    prev_k_ref,
    prev_v_ref,
    own_k_ref,
    own_v_ref,
    out_ref,
    lse_ref,
    key_aug,
    value_aug,
    query_aug,
    total,
    top,
):
    rows = q_ref.shape[0]
    has_prev, own_prefix = scalars[0], scalars[1]
    lane = lane_index(rows)
    first = lane < HEAD_DIM
    ones = jnp.where((lane & (HEAD_DIM - 1)) < 3, 1.0, 0.0).astype(BF16)
    head_a, head_b = split_queries(q_ref[...])
    query_aug[0, :, :LANES] = head_a
    query_aug[1, :, :LANES] = head_b

    def prepare(k_ref, v_ref, at):
        keys_a, keys_b = twice(k_ref[...])
        values = v_ref[...]
        one = jnp.ones_like(values)
        where = pl.ds(at, rows)
        key_aug[0, where, :LANES] = keys_a
        key_aug[1, where, :LANES] = keys_b
        key_aug[0, where, LANES:] = ones
        key_aug[1, where, LANES:] = ones
        value_aug[0, where] = jnp.where(first, values, one)
        value_aug[1, where] = jnp.where(first, one, values)

    @pl.when(has_prev > 0)
    def _():
        prepare(prev_k_ref, prev_v_ref, 0)

    prepare(own_k_ref, own_v_ref, rows)
    block_lane = lane_index(block_q)
    block_first = block_lane < HEAD_DIM
    place = block_lane & (HEAD_DIM - 1)
    key_blocks = rows // block_k
    for i in range(rows // block_q):
        here = slice(i * block_q, (i + 1) * block_q)
        seen = jnp.minimum(
            jnp.maximum(-(-(i + 1) * block_q // block_k), (own_prefix + block_k - 1) // block_k),
            key_blocks,
        )
        whole = jnp.minimum(jnp.maximum(i * block_q // block_k, own_prefix // block_k), seen)

        def over_keys(block):
            @pl.when(has_prev > 0)
            def _():
                for j in range(key_blocks):
                    block(j * block_k, False)

            def unmasked(j, carried):
                block(rows + j * block_k, False)
                return carried

            def masked(j, carried):
                block(rows + j * block_k, True)
                return carried

            lax.fori_loop(0, whole, unmasked, 0)
            lax.fori_loop(whole, seen, masked, 0)

        def allowed(at):
            key_pos = at - rows + lax.broadcasted_iota(jnp.int32, (block_q, block_k), 1)
            query_pos = i * block_q + lax.broadcasted_iota(jnp.int32, (block_q, block_k), 0)
            return key_pos <= jnp.maximum(query_pos, own_prefix - 1)

        top[...] = jnp.full_like(top, MASK_FILL)

        def find_top(at, masked):
            at = pl.multiple_of(at, block_k)
            visible = allowed(at) if masked else None
            for h in range(2):
                scores = nt(query_aug[h, here, :LANES], key_aug[h, pl.ds(at, block_k), :LANES])
                if masked:
                    scores = jnp.where(visible, scores, MASK_FILL)
                largest = top[h]
                for t in range(block_k // LANES):
                    largest = jnp.maximum(largest, scores[:, t * LANES : (t + 1) * LANES])
                top[h] = largest

        over_keys(find_top)
        maxima = []
        for h in range(2):
            maximum = jnp.max(top[h], axis=1, keepdims=True)
            maxima.append(maximum)
            columns = three_columns(jnp.broadcast_to(-maximum, (block_q, LANES)), place)
            mine = block_first if h == 0 else jnp.logical_not(block_first)
            query_aug[h, here, LANES:] = jnp.where(mine, columns, 0.0).astype(BF16)
        total[...] = jnp.zeros_like(total)

        def add_up(at, masked):
            at = pl.multiple_of(at, block_k)
            visible = allowed(at) if masked else None
            for h in range(2):
                scores = nt(query_aug[h, here, :], key_aug[h, pl.ds(at, block_k), :])
                if masked:
                    scores = jnp.where(visible, scores, MASK_FILL)
                total[h] += nn(jnp.exp2(scores).astype(BF16), value_aug[h, pl.ds(at, block_k), :])

        over_keys(add_up)
        sum_a, sum_b = total[0], total[1]
        weight = jnp.where(
            block_first, pltpu.roll(sum_a, HEAD_DIM, 1), pltpu.roll(sum_b, HEAD_DIM, 1)
        )
        out_ref[here, :] = (jnp.where(block_first, sum_a, sum_b) / weight).astype(BF16)
        lse_ref[here, :] = jnp.where(block_first, maxima[0], maxima[1]) + jnp.log2(weight)


def attention_forward(scalars, queries, prev, own, block_q=1024, block_k=512):
    rows, width = queries.shape
    pairs = width // LANES

    def spec(offset):
        return pl.BlockSpec((rows, LANES), lambda h, scalars: (0, h + offset))

    return pl.pallas_call(
        partial(forward_kernel, block_q, block_k),
        grid_spec=pltpu.PrefetchScalarGridSpec(
            num_scalar_prefetch=1,
            grid=(pairs,),
            in_specs=[spec(0), spec(0), spec(pairs), spec(0), spec(pairs)],
            out_specs=[spec(0), spec(0)],
            scratch_shapes=[
                pltpu.VMEM((2, 2 * rows, 2 * LANES), BF16),
                pltpu.VMEM((2, 2 * rows, LANES), BF16),
                pltpu.VMEM((2, rows, 2 * LANES), BF16),
                pltpu.VMEM((2, block_q, LANES), F32),
                pltpu.VMEM((2, block_q, LANES), F32),
            ],
        ),
        out_shape=[
            jax.ShapeDtypeStruct((rows, width), BF16),
            jax.ShapeDtypeStruct((rows, width), F32),
        ],
        compiler_params=pltpu.CompilerParams(vmem_limit_bytes=VMEM_LIMIT),
        cost_estimate=pl.CostEstimate(
            flops=40 * rows * rows * width,
            bytes_accessed=16 * rows * width,
            transcendentals=2 * rows * rows * width // HEAD_DIM,
        ),
        name="attention_forward",
    )(scalars, queries, prev, prev, own, own)


def backward_kernel(
    block_q,
    block_k,
    scalars,
    q_ref,
    prev_k_ref,
    prev_v_ref,
    own_k_ref,
    own_v_ref,
    out_ref,
    lse_ref,
    grad_ref,
    dq_ref,
    prev_grad_ref,
    own_grad_ref,
    key_aug,
    key_zero,
    value_aug,
    query_aug,
    query_zero,
    grad_aug,
    grad_zero,
    dq_total,
    dk_total,
    dv_total,
):
    rows = q_ref.shape[0]
    has_prev, own_prefix = scalars[0], scalars[1]
    lane = lane_index(rows)
    first = lane < HEAD_DIM
    place = lane & (HEAD_DIM - 1)
    zero = jnp.zeros((rows, LANES), BF16)
    ones = jnp.where(place < 3, 1.0, 0.0).astype(BF16)
    queries = q_ref[...]
    head_a, head_b = split_queries(queries)
    columns = three_columns(-lse_ref[...], place)
    query_aug[0, :, :LANES] = head_a
    query_aug[1, :, :LANES] = head_b
    query_aug[0, :, LANES:] = jnp.where(first, columns, 0.0).astype(BF16)
    query_aug[1, :, LANES:] = jnp.where(first, 0.0, columns).astype(BF16)
    query_zero[0] = jnp.where(first, queries, zero)
    query_zero[1] = jnp.where(first, zero, queries)
    grads = grad_ref[...]
    grad_zero[0] = jnp.where(first, grads, zero)
    grad_zero[1] = jnp.where(first, zero, grads)
    products = grads.astype(F32) * out_ref[...].astype(F32)
    delta_a = jnp.sum(jnp.where(first, products, 0.0), axis=1, keepdims=True)
    delta_b = jnp.sum(jnp.where(first, 0.0, products), axis=1, keepdims=True)
    columns = three_columns(jnp.where(first, -delta_b, -delta_a), place).astype(BF16)
    grad_aug[0] = jnp.where(first, grads, columns)
    grad_aug[1] = jnp.where(first, columns, grads)

    def prepare(k_ref, v_ref, at):
        keys, values = k_ref[...], v_ref[...]
        keys_a, keys_b = twice(keys)
        where = pl.ds(at, rows)
        key_aug[0, where, :LANES] = keys_a
        key_aug[1, where, :LANES] = keys_b
        key_aug[0, where, LANES:] = ones
        key_aug[1, where, LANES:] = ones
        key_zero[0, where] = jnp.where(first, keys, zero)
        key_zero[1, where] = jnp.where(first, zero, keys)
        value_aug[0, where] = jnp.where(first, values, ones)
        value_aug[1, where] = jnp.where(first, ones, values)

    @pl.when(has_prev > 0)
    def _():
        prepare(prev_k_ref, prev_v_ref, 0)

    prepare(own_k_ref, own_v_ref, rows)
    dq_total[...] = jnp.zeros_like(dq_total)

    def block(at, i, masked):
        keys_at = pl.ds(pl.multiple_of(at, block_k), block_k)
        start = pl.multiple_of(i * block_q, block_q)
        queries_at = pl.ds(start, block_q)
        if masked:
            key_pos = at - rows + lax.broadcasted_iota(jnp.int32, (block_k, block_q), 0)
            query_pos = start + lax.broadcasted_iota(jnp.int32, (block_k, block_q), 1)
            visible = key_pos <= jnp.maximum(query_pos, own_prefix - 1)
        probs, d_scores = [], []
        for h in range(2):
            scores = nt(key_aug[h, keys_at, :], query_aug[h, queries_at, :])
            if masked:
                scores = jnp.where(visible, scores, MASK_FILL)
            part = jnp.exp2(scores)
            centered = nt(value_aug[h, keys_at, :], grad_aug[h, queries_at, :])
            d_scores.append((part * centered).astype(BF16))
            probs.append(part.astype(BF16))
        dv_total[...] += nn(probs[0], grad_zero[0, queries_at, :]) + nn(
            probs[1], grad_zero[1, queries_at, :]
        )
        dk_total[...] += nn(d_scores[0], query_zero[0, queries_at, :]) + nn(
            d_scores[1], query_zero[1, queries_at, :]
        )
        dq_total[queries_at, :] += tn(d_scores[0], key_zero[0, keys_at, :]) + tn(
            d_scores[1], key_zero[1, keys_at, :]
        )

    query_blocks = rows // block_q

    def clear():
        dk_total[...] = jnp.zeros_like(dk_total)
        dv_total[...] = jnp.zeros_like(dv_total)

    def put(ref, j):
        here = slice(j * block_k, (j + 1) * block_k)
        ref[0, here, :] = dk_total[...].astype(BF16)
        ref[1, here, :] = dv_total[...].astype(BF16)

    @pl.when(has_prev > 0)
    def _():
        for j in range(rows // block_k):
            clear()

            def step(i, carried):
                block(j * block_k, i, False)
                return carried

            lax.fori_loop(0, query_blocks, step, 0)
            put(prev_grad_ref, j)

    @pl.when(has_prev == 0)
    def _():
        prev_grad_ref[0] = zero
        prev_grad_ref[1] = zero

    for j in range(rows // block_k):
        clear()
        inside = own_prefix >= (j + 1) * block_k
        reached = own_prefix > j * block_k
        first_whole = jnp.where(inside, 0, min(query_blocks, -(-((j + 1) * block_k - 1) // block_q)))
        first_seen = jnp.where(reached, 0, min(query_blocks, j * block_k // block_q))

        def masked(i, carried):
            block(rows + j * block_k, i, True)
            return carried

        def unmasked(i, carried):
            block(rows + j * block_k, i, False)
            return carried

        lax.fori_loop(first_seen, first_whole, masked, 0)
        lax.fori_loop(first_whole, query_blocks, unmasked, 0)
        put(own_grad_ref, j)
    dq_ref[...] = (dq_total[...] * (HEAD_DIM**-0.5)).astype(BF16)


def attention_backward(scalars, queries, prev, own, out, lse, grads, block_q=512, block_k=512):
    rows, width = queries.shape
    pairs = width // LANES

    def spec(offset):
        return pl.BlockSpec((rows, LANES), lambda h, scalars: (0, h + offset))

    both = pl.BlockSpec((2, rows, LANES), lambda h, scalars: (0, 0, h))
    return pl.pallas_call(
        partial(backward_kernel, block_q, block_k),
        grid_spec=pltpu.PrefetchScalarGridSpec(
            num_scalar_prefetch=1,
            grid=(pairs,),
            in_specs=[spec(0), spec(0), spec(pairs), spec(0), spec(pairs)] + [spec(0)] * 3,
            out_specs=[spec(0), both, both],
            scratch_shapes=[
                pltpu.VMEM((2, 2 * rows, 2 * LANES), BF16),
                pltpu.VMEM((2, 2 * rows, LANES), BF16),
                pltpu.VMEM((2, 2 * rows, LANES), BF16),
                pltpu.VMEM((2, rows, 2 * LANES), BF16),
                pltpu.VMEM((2, rows, LANES), BF16),
                pltpu.VMEM((2, rows, LANES), BF16),
                pltpu.VMEM((2, rows, LANES), BF16),
                pltpu.VMEM((rows, LANES), F32),
                pltpu.VMEM((block_k, LANES), F32),
                pltpu.VMEM((block_k, LANES), F32),
            ],
        ),
        out_shape=[
            jax.ShapeDtypeStruct((rows, width), BF16),
            jax.ShapeDtypeStruct((2, rows, width), BF16),
            jax.ShapeDtypeStruct((2, rows, width), BF16),
        ],
        compiler_params=pltpu.CompilerParams(vmem_limit_bytes=VMEM_LIMIT),
        cost_estimate=pl.CostEstimate(
            flops=60 * rows * rows * width,
            bytes_accessed=26 * rows * width,
            transcendentals=2 * rows * rows * width // HEAD_DIM,
        ),
        name="attention_backward",
    )(scalars, queries, prev, prev, own, own, out, lse, grads)


def expert_kernel(
    experts,
    block_r,
    scalars,
    rows_ref,
    cot_ref,
    w_in_ref,
    w_down_ref,
    router_ref,
    y_ref,
    dm_ref,
    act_ref,
    du_ref,
    dy_ref,
    dz_ref,
    y_total,
    dm_total,
    probs,
):
    step = pl.program_id(0)
    blocks = rows_ref.shape[0] // block_r
    lane = lane_index(block_r)
    is_mine = lane == scalars[0]

    def over_rows(work):
        def one(b, carried):
            work(pl.ds(pl.multiple_of(b * block_r, block_r), block_r))
            return carried

        lax.fori_loop(0, blocks, one, 0)

    @pl.when(step == 0)
    def _():
        def gate(here):
            logits = nt(rows_ref[here, :], router_ref[...])
            logits = jnp.where(lane < experts, logits, MASK_FILL)
            spread = jnp.exp(logits - jnp.max(logits, axis=1, keepdims=True))
            part = spread / jnp.sum(spread, axis=1, keepdims=True)
            probs[here, :] = part
            mine = jnp.sum(jnp.where(is_mine, part, 0.0), axis=1, keepdims=True)
            dy_ref[here, :] = (mine * cot_ref[here, :].astype(F32)).astype(BF16)
            y_total[here, :] = jnp.zeros((block_r, y_total.shape[1]), F32)
            dm_total[here, :] = jnp.zeros((block_r, dm_total.shape[1]), F32)

        over_rows(gate)

    def hidden_block(here):
        u = nn(rows_ref[here, :], w_in_ref[...])
        d_act = nt(dy_ref[here, :], w_down_ref[...])
        square = u * u
        bend = jnp.tanh(u * (GELU_A + (GELU_A * GELU_B) * square))
        half = 0.5 + 0.5 * bend
        act = (u * half).astype(BF16)
        slope = half + (0.5 * u) * (1.0 - bend * bend) * (
            GELU_A + (3.0 * GELU_A * GELU_B) * square
        )
        du = (d_act * slope).astype(BF16)
        act_ref[here, :] = act
        du_ref[here, :] = du
        y_total[here, :] += nn(act, w_down_ref[...])
        dm_total[here, :] += nt(du, w_in_ref[...])

    over_rows(hidden_block)

    @pl.when(step == pl.num_programs(0) - 1)
    def _():
        def finish(here):
            y = y_total[here, :].astype(BF16)
            y_ref[here, :] = y
            d_gate = jnp.sum(cot_ref[here, :].astype(F32) * y.astype(F32), axis=1, keepdims=True)
            part = probs[here, :]
            mine = jnp.sum(jnp.where(is_mine, part, 0.0), axis=1, keepdims=True)
            dz = ((d_gate * mine) * (jnp.where(is_mine, 1.0, 0.0) - part)).astype(BF16)
            dz = jnp.where(lane < experts, dz, jnp.zeros_like(dz))
            dz_ref[here, :] = dz
            dm_ref[here, :] = (dm_total[here, :] + nn(dz, router_ref[...])).astype(BF16)

        over_rows(finish)


def run_expert(scalars, rows_in, cots, w_in, w_down, router, experts, block_h=512, block_r=256):
    rows, width = rows_in.shape
    half = w_in.shape[2]
    per_half = half // block_h
    whole = pl.BlockSpec((rows, width), lambda j, s: (0, 0))
    hidden = pl.BlockSpec((rows, block_h), lambda j, s: (0, j))

    def which(j, s):
        return lax.rem(j // per_half + s[1], 2)

    return pl.pallas_call(
        partial(expert_kernel, experts, block_r),
        grid_spec=pltpu.PrefetchScalarGridSpec(
            num_scalar_prefetch=1,
            grid=(2 * per_half,),
            in_specs=[
                whole,
                whole,
                pl.BlockSpec(
                    (None, width, block_h), lambda j, s: (which(j, s), 0, lax.rem(j, per_half))
                ),
                pl.BlockSpec(
                    (None, block_h, width), lambda j, s: (which(j, s), lax.rem(j, per_half), 0)
                ),
                pl.BlockSpec((LANES, width), lambda j, s: (0, 0)),
            ],
            out_specs=[
                whole,
                whole,
                hidden,
                hidden,
                whole,
                pl.BlockSpec((rows, LANES), lambda j, s: (0, 0)),
            ],
            scratch_shapes=[
                pltpu.VMEM((rows, width), F32),
                pltpu.VMEM((rows, width), F32),
                pltpu.VMEM((rows, LANES), F32),
            ],
        ),
        out_shape=[
            jax.ShapeDtypeStruct((rows, width), BF16),
            jax.ShapeDtypeStruct((rows, width), BF16),
            jax.ShapeDtypeStruct((rows, 2 * half), BF16),
            jax.ShapeDtypeStruct((rows, 2 * half), BF16),
            jax.ShapeDtypeStruct((rows, width), BF16),
            jax.ShapeDtypeStruct((rows, LANES), BF16),
        ],
        compiler_params=pltpu.CompilerParams(vmem_limit_bytes=VMEM_LIMIT),
        cost_estimate=pl.CostEstimate(
            flops=16 * rows * width * half,
            bytes_accessed=8 * width * half + 12 * rows * width + 8 * rows * half,
            transcendentals=2 * rows * half,
        ),
        name="expert_rows",
    )(scalars, rows_in, cots, w_in, w_down, router)


def layer_norm(values, norm_gain, norm_bias):
    center = values - jnp.mean(values, axis=-1, keepdims=True)
    inv_std = lax.rsqrt(jnp.mean(center * center, axis=-1, keepdims=True) + NORM_EPSILON)
    normed = center * inv_std
    return (normed * norm_gain + norm_bias, normed, inv_std)


def norm_backward(grad_out, normed, inv_std, norm_gain):
    scaled = grad_out * norm_gain
    return inv_std * (
        scaled
        - jnp.mean(scaled, axis=-1, keepdims=True)
        - normed * jnp.mean(scaled * normed, axis=-1, keepdims=True)
    )


def swapped(array):
    return lax.ppermute(array, "fsdp", [(0, 1), (1, 0)])


def exchanged(array):
    return lax.all_to_all(array, "expert", split_axis=0, concat_axis=0, tiled=True)


def body(
    tokens,
    out_grad,
    routes,
    prefix,
    ln1_gain,
    ln1_bias,
    w_qkv,
    q_bias,
    v_bias,
    attention_output_weight,
    attention_output_bias,
    ln2_gain,
    ln2_bias,
    w_router,
    moe_bias,
    w_in,
    w_down,
):
    experts = lax.axis_size("expert")
    my_expert = lax.axis_index("expert")
    my_half = lax.axis_index("fsdp")
    is_first = my_half == 0
    rows, width = tokens.shape[1], tokens.shape[2]
    half_width = width // 2
    slots = max(2, 2 * rows // experts) // CHUNKS
    chunk_rows = experts * slots

    def in_order(own, other, axis):
        return jnp.where(
            is_first,
            jnp.concatenate([own, other], axis=axis),
            jnp.concatenate([other, own], axis=axis),
        )

    small = jnp.concatenate(
        [
            jnp.stack(
                [
                    ln1_gain,
                    ln1_bias,
                    q_bias,
                    v_bias,
                    attention_output_bias,
                    ln2_gain,
                    ln2_bias,
                    moe_bias,
                ]
            ),
            w_router.T,
        ],
        axis=0,
    )
    small = in_order(small, swapped(small), 1)
    vectors = small[:8].astype(F32)
    norm1_gain, norm1_bias, query_bias, value_bias = (vectors[i] for i in range(4))
    output_bias, norm2_gain, norm2_bias, expert_bias = (vectors[i] for i in range(4, 8))
    router_t = small[8:]
    qkv_weight = in_order(w_qkv, swapped(w_qkv), 0)
    out_weight = lax.all_gather(attention_output_weight, "fsdp", axis=0, tiled=True)
    w_in_both = lax.all_gather(w_in[0], "fsdp", axis=0, tiled=False)
    w_down_both = lax.all_gather(w_down[0], "fsdp", axis=0, tiled=False)

    token_route = routes[0, :, 0]
    one_hot = token_route[:, None] == jnp.arange(experts, dtype=jnp.int32)[None, :]
    row_ids = jnp.arange(rows, dtype=jnp.int32)
    earlier_same = nn(
        (row_ids[None, :] < row_ids[:, None]).astype(BF16), one_hot.astype(BF16)
    )
    slot_index = jnp.sum(jnp.where(one_hot, earlier_same, 0.0), axis=-1).astype(jnp.int32)
    chunk_of = slot_index // slots
    place_in = token_route * slots + slot_index % slots
    buffer_ids = jnp.arange(chunk_rows, dtype=jnp.int32)

    def dispatch(row_values, chunk):
        place = jnp.where(chunk_of == chunk, place_in, -1)
        picked = nn((buffer_ids[:, None] == place[None, :]).astype(BF16), row_values)
        return exchanged(picked.astype(BF16).reshape(experts, slots, width)).reshape(
            chunk_rows, width
        )

    def give_back(buffers):
        got = [exchanged(b.reshape(experts, slots, width)).reshape(chunk_rows, width) for b in buffers]
        total = None
        for chunk in range(CHUNKS):
            place = jnp.where(chunk_of == chunk, place_in, -1)
            part = nn((place[:, None] == buffer_ids[None, :]).astype(BF16), got[chunk])
            total = part if total is None else total + part
        return total

    cot_rows = [dispatch(out_grad[0], chunk) for chunk in range(CHUNKS)]

    residual = tokens[0].astype(F32)
    norm1_out, normed1, inv_std1 = layer_norm(residual, norm1_gain, norm1_bias)
    attn_in = norm1_out.astype(BF16)
    key_value = (
        nn(attn_in, qkv_weight[:, width:])
        + jnp.concatenate([jnp.zeros_like(value_bias), value_bias])
    ).astype(BF16)
    prev_key_value = lax.ppermute(key_value, "fsdp", [(0, 1)])
    queries = ((nn(attn_in, qkv_weight[:, :width]) + query_bias) * (HEAD_DIM**-0.5)).astype(BF16)
    scalars = jnp.stack([my_half, prefix[0] - my_half * rows]).astype(jnp.int32)
    context, lse = attention_forward(scalars, queries, prev_key_value, key_value)
    hidden = residual + (nn(context, out_weight) + output_bias)
    norm2_out, normed2, inv_std2 = layer_norm(hidden, norm2_gain, norm2_bias)
    mixed = norm2_out.astype(BF16)

    mixed_rows = [dispatch(mixed, chunk) for chunk in range(CHUNKS)]
    router_pad = jnp.pad(router_t, ((0, LANES - experts), (0, 0)))
    expert_scalars = jnp.stack([my_expert, my_half]).astype(jnp.int32)
    done = [
        run_expert(
            expert_scalars, mixed_rows[c], cot_rows[c], w_in_both, w_down_both, router_pad, experts
        )
        for c in range(CHUNKS)
    ]
    d_mixed = give_back([d[1] for d in done])

    hidden_half = w_in.shape[2]

    def both_chunks(pick_left, pick_right):
        total = None
        for c in range(CHUNKS):
            part = tn(pick_left(c), pick_right(c))
            total = part if total is None else total + part
        return total

    own, other = slice(0, hidden_half), slice(hidden_half, 2 * hidden_half)
    d_in_other = both_chunks(lambda c: mixed_rows[c], lambda c: done[c][3][:, other])
    d_down_other = both_chunks(lambda c: done[c][2][:, other], lambda c: done[c][4])
    d_in_got = swapped(d_in_other.astype(BF16))
    d_down_got = swapped(d_down_other.astype(BF16))
    d_w_in = both_chunks(lambda c: mixed_rows[c], lambda c: done[c][3][:, own]) + d_in_got
    d_w_down = both_chunks(lambda c: done[c][2][:, own], lambda c: done[c][4]) + d_down_got
    d_router = both_chunks(lambda c: mixed_rows[c], lambda c: done[c][5])

    out_cot = out_grad[0].astype(F32)
    d_expert_bias = jnp.sum(out_cot, axis=0)
    d_norm2_gain = jnp.sum(d_mixed * normed2, axis=0)
    d_norm2_bias = jnp.sum(d_mixed, axis=0)
    d_hidden = out_cot + norm_backward(d_mixed, normed2, inv_std2, norm2_gain)
    d_attn = d_hidden.astype(BF16)
    d_output_bias = jnp.sum(d_attn.astype(F32), axis=0)
    d_context = nt(d_attn, out_weight).astype(BF16)

    logits = nt(mixed, router_t)
    router_probs = jax.nn.softmax(logits, axis=-1)
    gate_value = jnp.sum(jnp.where(one_hot, router_probs, 0.0), axis=-1)
    expert_value = give_back([d[0] for d in done])
    output = hidden + gate_value[:, None] * expert_value + expert_bias

    def halves(columns):
        left, right = columns[:, :half_width], columns[:, half_width:]
        return jnp.where(is_first, left, right), jnp.where(is_first, right, left)

    def row_halves(matrix):
        top, bottom = matrix[:half_width], matrix[half_width:]
        return jnp.where(is_first, top, bottom), jnp.where(is_first, bottom, top)

    def scattered(own_part, other_part):
        pair = own_part + swapped(other_part.astype(BF16)).astype(F32)
        blocks = pair.astype(BF16).reshape(experts, half_width // experts, pair.shape[1])
        return jnp.sum(exchanged(blocks).astype(F32), axis=0)

    def as_columns(pieces):
        packed = jnp.concatenate(pieces, axis=1)
        return jnp.pad(packed, ((0, 0), (0, -packed.shape[1] % LANES)))

    context_own, context_other = halves(context)
    extra_own, extra_other = row_halves(
        as_columns(
            [
                d_router[:, :experts],
                jnp.stack([d_expert_bias, d_norm2_gain, d_norm2_bias, d_output_bias], axis=1),
            ]
        )
    )
    sum_out = scattered(
        jnp.concatenate([tn(context_own, d_attn), extra_own], axis=1),
        jnp.concatenate([tn(context_other, d_attn), extra_other], axis=1),
    )

    d_query, prev_grad, own_grad = attention_backward(
        scalars, queries, prev_key_value, key_value, context, lse, d_context
    )
    returned = lax.ppermute(prev_grad, "fsdp", [(1, 0)])
    in_own, in_other = halves(attn_in)
    sum_query = scattered(tn(in_own, d_query), tn(in_other, d_query))
    d_key_value = (own_grad.astype(F32) + returned.astype(F32)).astype(BF16)
    d_key, d_value = d_key_value[0], d_key_value[1]
    sum_key = scattered(tn(in_own, d_key), tn(in_other, d_key))
    sum_value = scattered(tn(in_own, d_value), tn(in_other, d_value))
    d_norm1_out = (
        nt(d_query, qkv_weight[:, :width])
        + nt(d_key, qkv_weight[:, width : 2 * width])
        + nt(d_value, qkv_weight[:, 2 * width :])
    )
    d_tokens = (d_hidden + norm_backward(d_norm1_out, normed1, inv_std1, norm1_gain)).astype(BF16)
    last_own, last_other = row_halves(
        as_columns(
            [
                jnp.stack(
                    [
                        jnp.sum(d_query.astype(F32), axis=0),
                        jnp.sum(d_value.astype(F32), axis=0),
                        jnp.sum(d_norm1_out * normed1, axis=0),
                        jnp.sum(d_norm1_out, axis=0),
                    ],
                    axis=1,
                )
            ]
        )
    )
    sum_last = scattered(last_own, last_other)
    return (
        output.astype(BF16)[None],
        d_tokens[None],
        sum_last[:, 2],
        sum_last[:, 3],
        jnp.concatenate([sum_query, sum_key, sum_value], axis=1),
        sum_last[:, 0],
        sum_last[:, 1],
        sum_out[:, :width],
        sum_out[:, width + experts + 3],
        sum_out[:, width + experts + 1],
        sum_out[:, width + experts + 2],
        sum_out[:, width : width + experts],
        sum_out[:, width + experts],
        d_w_in[None],
        d_w_down[None],
    )


def solution(mesh):
    vector = P(("fsdp", "expert"))
    matrix = P(("fsdp", "expert"), None)
    tokens = P("expert", "fsdp", None)
    return jax.shard_map(
        body,
        mesh=mesh,
        in_specs=(
            tokens,
            tokens,
            tokens,
            P("expert"),
            P("fsdp"),
            P("fsdp"),
            P("fsdp", None),
            P("fsdp"),
            P("fsdp"),
            P("fsdp", None),
            P("fsdp"),
            P("fsdp"),
            P("fsdp"),
            P("fsdp", None),
            P("fsdp"),
            P("expert", None, "fsdp"),
            P("expert", "fsdp", None),
        ),
        out_specs=(
            tokens,
            tokens,
            vector,
            vector,
            matrix,
            vector,
            vector,
            matrix,
            vector,
            vector,
            vector,
            matrix,
            vector,
            P("expert", None, "fsdp"),
            P("expert", "fsdp", None),
        ),
        check_vma=False,
    )
```

```python
from functools import partial

import jax
import jax.numpy as jnp
from jax import lax
from jax.experimental import pallas as pl
from jax.experimental.pallas import tpu as pltpu
from jax.sharding import PartitionSpec as P

HEAD_DIM = 64
NORM_EPSILON = 1e-05
MASK_FILL = -1e30
LOG2E = 1.4426950408889634
GELU_A = 0.7978845608028654
GELU_B = 0.044715
CHUNKS = 2
FIRST_PAIRS = 5
LANES = 128
BF16 = jnp.bfloat16
F32 = jnp.float32
VMEM_LIMIT = 56 << 20


def nn(left, right):
    return lax.dot_general(left, right, (((1,), (0,)), ((), ())), preferred_element_type=F32)


def nt(left, right):
    return lax.dot_general(left, right, (((1,), (1,)), ((), ())), preferred_element_type=F32)


def tn(left, right):
    return lax.dot_general(left, right, (((0,), (0,)), ((), ())), preferred_element_type=F32)


def lane_index(rows):
    return lax.broadcasted_iota(jnp.int32, (rows, LANES), 1)


def split_queries(queries):
    scaled = queries.astype(F32) * LOG2E
    high = scaled.astype(BF16).astype(F32)
    low = scaled - high
    first = lane_index(queries.shape[0]) < HEAD_DIM
    head_a = jnp.where(first, high, pltpu.roll(low, HEAD_DIM, 1)).astype(BF16)
    head_b = jnp.where(first, pltpu.roll(high, HEAD_DIM, 1), low).astype(BF16)
    return head_a, head_b


def twice(keys):
    wide = keys.astype(F32)
    rolled = pltpu.roll(wide, HEAD_DIM, 1)
    first = lane_index(keys.shape[0]) < HEAD_DIM
    return jnp.where(first, wide, rolled).astype(BF16), jnp.where(first, rolled, wide).astype(BF16)


def in_three(values):
    high = values.astype(BF16).astype(F32)
    rest = values - high
    middle = rest.astype(BF16).astype(F32)
    return high, middle, rest - middle


def three_columns(values, place):
    high, middle, low = in_three(values)
    return jnp.where(
        place == 0, high, jnp.where(place == 1, middle, jnp.where(place == 2, low, 0.0))
    )


def forward_kernel(
    block_q,
    block_k,
    scalars,
    q_ref,
    prev_k_ref,
    prev_v_ref,
    own_k_ref,
    own_v_ref,
    out_ref,
    lse_ref,
    key_aug,
    value_aug,
    query_aug,
    total,
    top,
):
    rows = q_ref.shape[0]
    has_prev, own_prefix = scalars[0], scalars[1]
    lane = lane_index(rows)
    first = lane < HEAD_DIM
    ones = jnp.where((lane & (HEAD_DIM - 1)) < 3, 1.0, 0.0).astype(BF16)
    head_a, head_b = split_queries(q_ref[...])
    query_aug[0, :, :LANES] = head_a
    query_aug[1, :, :LANES] = head_b

    def prepare(k_ref, v_ref, at):
        keys_a, keys_b = twice(k_ref[...])
        values = v_ref[...]
        one = jnp.ones_like(values)
        where = pl.ds(at, rows)
        key_aug[0, where, :LANES] = keys_a
        key_aug[1, where, :LANES] = keys_b
        key_aug[0, where, LANES:] = ones
        key_aug[1, where, LANES:] = ones
        value_aug[0, where] = jnp.where(first, values, one)
        value_aug[1, where] = jnp.where(first, one, values)

    @pl.when(has_prev > 0)
    def _():
        prepare(prev_k_ref, prev_v_ref, 0)

    prepare(own_k_ref, own_v_ref, rows)
    block_lane = lane_index(block_q)
    block_first = block_lane < HEAD_DIM
    place = block_lane & (HEAD_DIM - 1)
    key_blocks = rows // block_k
    for i in range(rows // block_q):
        here = slice(i * block_q, (i + 1) * block_q)
        seen = jnp.minimum(
            jnp.maximum(-(-(i + 1) * block_q // block_k), (own_prefix + block_k - 1) // block_k),
            key_blocks,
        )
        whole = jnp.minimum(jnp.maximum(i * block_q // block_k, own_prefix // block_k), seen)

        def over_keys(block):
            def unmasked(j, carried):
                block(j * block_k, False)
                return carried

            def masked(j, carried):
                block(j * block_k, True)
                return carried

            lax.fori_loop(
                jnp.where(has_prev > 0, 0, key_blocks), key_blocks + whole, unmasked, 0
            )
            lax.fori_loop(key_blocks + whole, key_blocks + seen, masked, 0)

        def allowed(at):
            key_pos = at - rows + lax.broadcasted_iota(jnp.int32, (block_q, block_k), 1)
            query_pos = i * block_q + lax.broadcasted_iota(jnp.int32, (block_q, block_k), 0)
            return key_pos <= jnp.maximum(query_pos, own_prefix - 1)

        top[...] = jnp.full_like(top, MASK_FILL)

        def find_top(at, masked):
            at = pl.multiple_of(at, block_k)
            visible = allowed(at) if masked else None
            for h in range(2):
                scores = nt(query_aug[h, here, :LANES], key_aug[h, pl.ds(at, block_k), :LANES])
                if masked:
                    scores = jnp.where(visible, scores, MASK_FILL)
                largest = top[h]
                for t in range(block_k // LANES):
                    largest = jnp.maximum(largest, scores[:, t * LANES : (t + 1) * LANES])
                top[h] = largest

        over_keys(find_top)
        maxima = []
        for h in range(2):
            maximum = jnp.max(top[h], axis=1, keepdims=True)
            maxima.append(maximum)
            columns = three_columns(jnp.broadcast_to(-maximum, (block_q, LANES)), place)
            mine = block_first if h == 0 else jnp.logical_not(block_first)
            query_aug[h, here, LANES:] = jnp.where(mine, columns, 0.0).astype(BF16)
        total[...] = jnp.zeros_like(total)

        def add_up(at, masked):
            at = pl.multiple_of(at, block_k)
            visible = allowed(at) if masked else None
            for h in range(2):
                scores = nt(query_aug[h, here, :], key_aug[h, pl.ds(at, block_k), :])
                if masked:
                    scores = jnp.where(visible, scores, MASK_FILL)
                total[h] += nn(jnp.exp2(scores).astype(BF16), value_aug[h, pl.ds(at, block_k), :])

        over_keys(add_up)
        sum_a, sum_b = total[0], total[1]
        weight = jnp.where(
            block_first, pltpu.roll(sum_a, HEAD_DIM, 1), pltpu.roll(sum_b, HEAD_DIM, 1)
        )
        out_ref[here, :] = (jnp.where(block_first, sum_a, sum_b) / weight).astype(BF16)
        lse_ref[here, :] = jnp.where(block_first, maxima[0], maxima[1]) + jnp.log2(weight)


def attention_forward(scalars, queries, prev, own, block_q=1024, block_k=512):
    rows, width = queries.shape
    pairs = width // LANES

    def spec(offset):
        return pl.BlockSpec((rows, LANES), lambda h, scalars: (0, h + offset))

    return pl.pallas_call(
        partial(forward_kernel, block_q, block_k),
        grid_spec=pltpu.PrefetchScalarGridSpec(
            num_scalar_prefetch=1,
            grid=(pairs,),
            in_specs=[spec(0), spec(0), spec(pairs), spec(0), spec(pairs)],
            out_specs=[spec(0), spec(0)],
            scratch_shapes=[
                pltpu.VMEM((2, 2 * rows, 2 * LANES), BF16),
                pltpu.VMEM((2, 2 * rows, LANES), BF16),
                pltpu.VMEM((2, rows, 2 * LANES), BF16),
                pltpu.VMEM((2, block_q, LANES), F32),
                pltpu.VMEM((2, block_q, LANES), F32),
            ],
        ),
        out_shape=[
            jax.ShapeDtypeStruct((rows, width), BF16),
            jax.ShapeDtypeStruct((rows, width), F32),
        ],
        compiler_params=pltpu.CompilerParams(vmem_limit_bytes=VMEM_LIMIT),
        cost_estimate=pl.CostEstimate(
            flops=40 * rows * rows * width,
            bytes_accessed=16 * rows * width,
            transcendentals=2 * rows * rows * width // HEAD_DIM,
        ),
        name="attention_forward",
    )(scalars, queries, prev, prev, own, own)


def backward_kernel(
    block_q,
    block_k,
    scalars,
    q_ref,
    prev_k_ref,
    prev_v_ref,
    own_k_ref,
    own_v_ref,
    out_ref,
    lse_ref,
    grad_ref,
    dq_ref,
    prev_grad_ref,
    own_grad_ref,
    key_aug,
    key_zero,
    value_aug,
    query_aug,
    query_zero,
    grad_aug,
    grad_zero,
    dq_total,
    dk_total,
    dv_total,
):
    rows = q_ref.shape[0]
    has_prev, own_prefix = scalars[0], scalars[1]
    lane = lane_index(rows)
    first = lane < HEAD_DIM
    place = lane & (HEAD_DIM - 1)
    zero = jnp.zeros((rows, LANES), BF16)
    ones = jnp.where(place < 3, 1.0, 0.0).astype(BF16)
    queries = q_ref[...]
    head_a, head_b = split_queries(queries)
    columns = three_columns(-lse_ref[...], place)
    query_aug[0, :, :LANES] = head_a
    query_aug[1, :, :LANES] = head_b
    query_aug[0, :, LANES:] = jnp.where(first, columns, 0.0).astype(BF16)
    query_aug[1, :, LANES:] = jnp.where(first, 0.0, columns).astype(BF16)
    query_zero[0] = jnp.where(first, queries, zero)
    query_zero[1] = jnp.where(first, zero, queries)
    grads = grad_ref[...]
    grad_zero[0] = jnp.where(first, grads, zero)
    grad_zero[1] = jnp.where(first, zero, grads)
    products = grads.astype(F32) * out_ref[...].astype(F32)
    delta_a = jnp.sum(jnp.where(first, products, 0.0), axis=1, keepdims=True)
    delta_b = jnp.sum(jnp.where(first, 0.0, products), axis=1, keepdims=True)
    columns = three_columns(jnp.where(first, -delta_b, -delta_a), place).astype(BF16)
    grad_aug[0] = jnp.where(first, grads, columns)
    grad_aug[1] = jnp.where(first, columns, grads)

    def prepare(k_ref, v_ref, at):
        keys, values = k_ref[...], v_ref[...]
        keys_a, keys_b = twice(keys)
        where = pl.ds(at, rows)
        key_aug[0, where, :LANES] = keys_a
        key_aug[1, where, :LANES] = keys_b
        key_aug[0, where, LANES:] = ones
        key_aug[1, where, LANES:] = ones
        key_zero[0, where] = jnp.where(first, keys, zero)
        key_zero[1, where] = jnp.where(first, zero, keys)
        value_aug[0, where] = jnp.where(first, values, ones)
        value_aug[1, where] = jnp.where(first, ones, values)

    @pl.when(has_prev > 0)
    def _():
        prepare(prev_k_ref, prev_v_ref, 0)

    prepare(own_k_ref, own_v_ref, rows)
    dq_total[...] = jnp.zeros_like(dq_total)

    def block(at, i, masked):
        keys_at = pl.ds(pl.multiple_of(at, block_k), block_k)
        start = pl.multiple_of(i * block_q, block_q)
        queries_at = pl.ds(start, block_q)
        if masked:
            key_pos = at - rows + lax.broadcasted_iota(jnp.int32, (block_k, block_q), 0)
            query_pos = start + lax.broadcasted_iota(jnp.int32, (block_k, block_q), 1)
            visible = key_pos <= jnp.maximum(query_pos, own_prefix - 1)
        probs, d_scores = [], []
        for h in range(2):
            scores = nt(key_aug[h, keys_at, :], query_aug[h, queries_at, :])
            if masked:
                scores = jnp.where(visible, scores, MASK_FILL)
            part = jnp.exp2(scores)
            centered = nt(value_aug[h, keys_at, :], grad_aug[h, queries_at, :])
            d_scores.append((part * centered).astype(BF16))
            probs.append(part.astype(BF16))
        dv_total[...] += nn(probs[0], grad_zero[0, queries_at, :]) + nn(
            probs[1], grad_zero[1, queries_at, :]
        )
        dk_total[...] += nn(d_scores[0], query_zero[0, queries_at, :]) + nn(
            d_scores[1], query_zero[1, queries_at, :]
        )
        dq_total[queries_at, :] += tn(d_scores[0], key_zero[0, keys_at, :]) + tn(
            d_scores[1], key_zero[1, keys_at, :]
        )

    query_blocks = rows // block_q
    key_blocks = rows // block_k

    @pl.when(has_prev == 0)
    def _():
        prev_grad_ref[0] = zero
        prev_grad_ref[1] = zero

    def one_key_block(j, carried):
        at = j * block_k
        own_at = at - rows
        dk_total[...] = jnp.zeros_like(dk_total)
        dv_total[...] = jnp.zeros_like(dv_total)
        first_whole = jnp.where(
            own_prefix >= own_at + block_k,
            0,
            jnp.clip((own_at + block_k - 1 + block_q - 1) // block_q, 0, query_blocks),
        )
        first_seen = jnp.where(own_prefix > own_at, 0, jnp.clip(own_at // block_q, 0, query_blocks))
        first_whole = jnp.where(own_at < 0, 0, first_whole)
        first_seen = jnp.where(own_at < 0, 0, first_seen)

        def masked(i, carried):
            block(at, i, True)
            return carried

        def unmasked(i, carried):
            block(at, i, False)
            return carried

        lax.fori_loop(first_seen, first_whole, masked, 0)
        lax.fori_loop(first_whole, query_blocks, unmasked, 0)

        @pl.when(own_at < 0)
        def _():
            here = pl.ds(pl.multiple_of(at, block_k), block_k)
            prev_grad_ref[0, here, :] = dk_total[...].astype(BF16)
            prev_grad_ref[1, here, :] = dv_total[...].astype(BF16)

        @pl.when(own_at >= 0)
        def _():
            here = pl.ds(pl.multiple_of(own_at, block_k), block_k)
            own_grad_ref[0, here, :] = dk_total[...].astype(BF16)
            own_grad_ref[1, here, :] = dv_total[...].astype(BF16)

        return carried

    lax.fori_loop(jnp.where(has_prev > 0, 0, key_blocks), 2 * key_blocks, one_key_block, 0)
    dq_ref[...] = (dq_total[...] * (HEAD_DIM**-0.5)).astype(BF16)


def attention_backward(
    scalars, queries, prev, own, out, lse, grads, begin, count, block_q=512, block_k=512
):
    rows, width = queries.shape
    pairs = width // LANES

    def spec(offset):
        return pl.BlockSpec((rows, LANES), lambda h, scalars: (0, h + begin + offset))

    both = pl.BlockSpec((2, rows, LANES), lambda h, scalars: (0, 0, h))
    share = count * LANES
    return pl.pallas_call(
        partial(backward_kernel, block_q, block_k),
        grid_spec=pltpu.PrefetchScalarGridSpec(
            num_scalar_prefetch=1,
            grid=(count,),
            in_specs=[spec(0), spec(0), spec(pairs), spec(0), spec(pairs)] + [spec(0)] * 3,
            out_specs=[pl.BlockSpec((rows, LANES), lambda h, scalars: (0, h)), both, both],
            scratch_shapes=[
                pltpu.VMEM((2, 2 * rows, 2 * LANES), BF16),
                pltpu.VMEM((2, 2 * rows, LANES), BF16),
                pltpu.VMEM((2, 2 * rows, LANES), BF16),
                pltpu.VMEM((2, rows, 2 * LANES), BF16),
                pltpu.VMEM((2, rows, LANES), BF16),
                pltpu.VMEM((2, rows, LANES), BF16),
                pltpu.VMEM((2, rows, LANES), BF16),
                pltpu.VMEM((rows, LANES), F32),
                pltpu.VMEM((block_k, LANES), F32),
                pltpu.VMEM((block_k, LANES), F32),
            ],
        ),
        out_shape=[
            jax.ShapeDtypeStruct((rows, share), BF16),
            jax.ShapeDtypeStruct((2, rows, share), BF16),
            jax.ShapeDtypeStruct((2, rows, share), BF16),
        ],
        compiler_params=pltpu.CompilerParams(vmem_limit_bytes=VMEM_LIMIT),
        cost_estimate=pl.CostEstimate(
            flops=60 * rows * rows * share,
            bytes_accessed=26 * rows * share,
            transcendentals=2 * rows * rows * share // HEAD_DIM,
        ),
        name="attention_backward",
    )(scalars, queries, prev, prev, own, own, out, lse, grads)


def expert_kernel(
    experts,
    block_r,
    scalars,
    rows_ref,
    cot_ref,
    w_in_ref,
    w_down_ref,
    router_ref,
    y_before_ref,
    y_ref,
    dm_ref,
    act_ref,
    du_ref,
    dy_ref,
    dz_ref,
    y_total,
    dm_total,
    probs,
):
    step = pl.program_id(0)
    slots, width = cot_ref.shape[1], cot_ref.shape[2]
    sources = block_r // slots
    lane = lane_index(block_r)
    is_mine = lane == scalars[0]

    def over_rows(work):
        for b in range(rows_ref.shape[0] // block_r):
            work(slice(b * block_r, (b + 1) * block_r), slice(b * sources, (b + 1) * sources))

    def cots(source):
        return cot_ref[source].reshape(block_r, width).astype(F32)

    @pl.when(step == 0)
    def _():
        def gate(here, source):
            logits = nt(rows_ref[here, :], router_ref[...])
            logits = jnp.where(lane < experts, logits, MASK_FILL)
            spread = jnp.exp(logits - jnp.max(logits, axis=1, keepdims=True))
            part = spread / jnp.sum(spread, axis=1, keepdims=True)
            probs[here, :] = part
            mine = jnp.sum(jnp.where(is_mine, part, 0.0), axis=1, keepdims=True)
            dy_ref[here, :] = (mine * cots(source)).astype(BF16)
            y_total[here, :] = jnp.zeros((block_r, y_total.shape[1]), F32)
            dm_total[here, :] = jnp.zeros((block_r, dm_total.shape[1]), F32)

        over_rows(gate)

    def hidden_block(here, source):
        u = nn(rows_ref[here, :], w_in_ref[...])
        d_act = nt(dy_ref[here, :], w_down_ref[...])
        square = u * u
        bend = jnp.tanh(u * (GELU_A + (GELU_A * GELU_B) * square))
        half = 0.5 + 0.5 * bend
        act = (u * half).astype(BF16)
        slope = half + (0.5 * u) * (1.0 - bend * bend) * (
            GELU_A + (3.0 * GELU_A * GELU_B) * square
        )
        du = (d_act * slope).astype(BF16)
        act_ref[here, :] = act
        du_ref[here, :] = du
        y_total[here, :] += nn(act, w_down_ref[...])
        dm_total[here, :] += nt(du, w_in_ref[...])

    over_rows(hidden_block)

    @pl.when(step == pl.num_programs(0) - 1)
    def _():
        def finish(here, source):
            y = y_total[here, :].astype(BF16)
            y_ref[source] = y.reshape(sources, slots, width)
            d_gate = jnp.sum(cots(source) * y.astype(F32), axis=1, keepdims=True)
            part = probs[here, :]
            mine = jnp.sum(jnp.where(is_mine, part, 0.0), axis=1, keepdims=True)
            dz = ((d_gate * mine) * (jnp.where(is_mine, 1.0, 0.0) - part)).astype(BF16)
            dz = jnp.where(lane < experts, dz, jnp.zeros_like(dz))
            dz_ref[here, :] = dz
            dm_ref[here, :] = (dm_total[here, :] + nn(dz, router_ref[...])).astype(BF16)

        over_rows(finish)


def run_expert(
    scalars, rows_in, cots, w_in, w_down, router, y_before, chunk, experts, block_h=512, block_r=1024
):
    rows, width = rows_in.shape
    half = w_in.shape[2]
    per_half = half // block_h
    whole = pl.BlockSpec((rows, width), lambda j, s: (0, 0))
    hidden = pl.BlockSpec((rows, block_h), lambda j, s: (0, j))
    mine = pl.BlockSpec(
        (cots.shape[0], None, cots.shape[2], width), lambda j, s: (0, chunk, 0, 0)
    )

    def which(j, s):
        return lax.rem(j // per_half + s[1], 2)

    first = y_before is None
    return pl.pallas_call(
        partial(expert_kernel, experts, block_r),
        grid_spec=pltpu.PrefetchScalarGridSpec(
            num_scalar_prefetch=1,
            grid=(2 * per_half,),
            in_specs=[
                whole,
                mine,
                pl.BlockSpec(
                    (None, width, block_h), lambda j, s: (which(j, s), 0, lax.rem(j, per_half))
                ),
                pl.BlockSpec(
                    (None, block_h, width), lambda j, s: (which(j, s), lax.rem(j, per_half), 0)
                ),
                pl.BlockSpec((LANES, width), lambda j, s: (0, 0)),
                pl.BlockSpec(memory_space=pl.ANY),
            ],
            out_specs=[
                mine,
                whole,
                hidden,
                hidden,
                whole,
                pl.BlockSpec((rows, LANES), lambda j, s: (0, 0)),
            ],
            scratch_shapes=[
                pltpu.VMEM((rows, width), F32),
                pltpu.VMEM((rows, width), F32),
                pltpu.VMEM((rows, LANES), F32),
            ],
        ),
        out_shape=[
            jax.ShapeDtypeStruct(cots.shape, BF16),
            jax.ShapeDtypeStruct((rows, width), BF16),
            jax.ShapeDtypeStruct((rows, 2 * half), BF16),
            jax.ShapeDtypeStruct((rows, 2 * half), BF16),
            jax.ShapeDtypeStruct((rows, width), BF16),
            jax.ShapeDtypeStruct((rows, LANES), BF16),
        ],
        input_output_aliases={} if first else {6: 0},
        compiler_params=pltpu.CompilerParams(vmem_limit_bytes=VMEM_LIMIT),
        cost_estimate=pl.CostEstimate(
            flops=16 * rows * width * half,
            bytes_accessed=8 * width * half + 12 * rows * width + 8 * rows * half,
            transcendentals=2 * rows * half,
        ),
        name="expert_rows",
    )(scalars, rows_in, cots, w_in, w_down, router, scalars if first else y_before)


def expert_weights_kernel(chunks, add, *refs):
    rows_refs, dy_refs, act_refs, du_refs = (
        refs[i * chunks : (i + 1) * chunks] for i in range(4)
    )
    rest = refs[4 * chunks :]
    d_in_ref, d_down_ref, turned = rest[-3:]
    rows = rows_refs[0].shape[0]

    @pl.when(pl.program_id(0) == 0)
    def _():
        for c in range(chunks):
            turned[:, c * rows : (c + 1) * rows] = rows_refs[c][...].T

    d_in, d_down = None, None
    for c in range(chunks):
        part = nn(turned[:, c * rows : (c + 1) * rows], du_refs[c][...])
        d_in = part if d_in is None else d_in + part
        part = tn(act_refs[c][...], dy_refs[c][...])
        d_down = part if d_down is None else d_down + part
    if add:
        d_in = d_in + rest[0][...].astype(F32)
        d_down = d_down + rest[1][...].astype(F32)
    d_in_ref[...] = d_in.astype(d_in_ref.dtype)
    d_down_ref[...] = d_down.astype(d_down_ref.dtype)


def expert_weights(rows_in, dy, act, du, half_index, got, block_h=512):
    chunks = len(rows_in)
    rows, width = rows_in[0].shape
    half = du[0].shape[1] // 2
    steps = half // block_h
    whole = pl.BlockSpec((rows, width), lambda j: (0, 0))
    hidden = pl.BlockSpec((rows, block_h), lambda j: (0, j + half_index * steps))
    columns = pl.BlockSpec((width, block_h), lambda j: (0, j))
    lines = pl.BlockSpec((block_h, width), lambda j: (j, 0))
    dtype = BF16 if got is None else F32
    extra = () if got is None else tuple(got)
    return pl.pallas_call(
        partial(expert_weights_kernel, chunks, got is not None),
        grid=(steps,),
        in_specs=[whole] * (2 * chunks) + [hidden] * (2 * chunks) + [columns, lines][: len(extra)],
        out_specs=[columns, lines],
        out_shape=[
            jax.ShapeDtypeStruct((width, half), dtype),
            jax.ShapeDtypeStruct((half, width), dtype),
        ],
        scratch_shapes=[pltpu.VMEM((width, chunks * rows), BF16)],
        compiler_params=pltpu.CompilerParams(vmem_limit_bytes=VMEM_LIMIT),
        cost_estimate=pl.CostEstimate(
            flops=4 * chunks * rows * width * half,
            bytes_accessed=4 * chunks * rows * (width + half) + 8 * width * half,
            transcendentals=0,
        ),
        name="expert_weights",
    )(*rows_in, *dy, *act, *du, *extra)


def pair_weights_kernel(groups, add, scalars, *refs):
    out_ref = refs[-1]
    at, column = 0, 0
    got = refs[-4:-1] if add else None
    for rights in groups:
        turned = refs[at][...].T
        at += 1
        for stacked in rights:
            for i in range(max(1, stacked)):
                grads = refs[at][i] if stacked else refs[at][...]
                part = nn(turned, grads)
                here = slice(column, column + part.shape[1])
                column += part.shape[1]
                if add:
                    part = part + got[0][:, here].astype(F32)
                out_ref[:, here] = part.astype(BF16)
            at += 1
    if add:
        out_ref[:, column:] = (got[1][...] + got[2][...].astype(F32)).astype(BF16)


def pair_weights(half_index, products, got=None):
    more = () if got is None else tuple(got)
    arrays, specs, groups, columns, flops = [], [], [], 0, 0

    def full(shape):
        return pl.BlockSpec(shape, lambda i, s: (0,) * len(shape))

    for left, rights in products:
        rows, half = left.shape[0], left.shape[1] // 2
        arrays.append(left)
        specs.append(pl.BlockSpec((rows, half), lambda i, s: (0, s[0])))
        groups.append(tuple(r.shape[0] if r.ndim == 3 else 0 for r in rights))
        for right in rights:
            arrays.append(right)
            specs.append(full(right.shape))
            columns += right.size // rows
    flops = 2 * rows * half * columns
    if got is not None:
        columns += got[1].shape[1]
    return pl.pallas_call(
        partial(pair_weights_kernel, tuple(groups), got is not None),
        grid_spec=pltpu.PrefetchScalarGridSpec(
            num_scalar_prefetch=1,
            grid=(1,),
            in_specs=specs + [full(m.shape) for m in more],
            out_specs=full((half, columns)),
        ),
        out_shape=jax.ShapeDtypeStruct((half, columns), BF16),
        compiler_params=pltpu.CompilerParams(vmem_limit_bytes=VMEM_LIMIT),
        cost_estimate=pl.CostEstimate(
            flops=flops, bytes_accessed=4 * (rows + half) * columns, transcendentals=0
        ),
        name="pair_weights",
    )(half_index, *arrays, *more)


def first_norm_kernel(shares, tokens_ref, dh_ref, gain_ref, w_ref, *refs):
    parts = len(shares)
    out_ref, sums_ref = refs[2 * parts], refs[2 * parts + 1]
    width = tokens_ref.shape[1]
    d_norm = None
    query_sums, value_sums = [], []
    begin = 0
    for p, share in enumerate(shares):
        dq, dkv = refs[2 * p], refs[2 * p + 1]
        for i in range(3):
            grads = dq[...] if i == 0 else dkv[i - 1]
            at = i * width + begin
            part = nt(grads, w_ref[:, at : at + share])
            d_norm = part if d_norm is None else d_norm + part
        query_sums.append(jnp.sum(dq[...].astype(F32), axis=0, keepdims=True))
        value_sums.append(jnp.sum(dkv[1].astype(F32), axis=0, keepdims=True))
        begin += share
    values = tokens_ref[...].astype(F32)
    center = values - jnp.mean(values, axis=1, keepdims=True)
    inv_std = lax.rsqrt(jnp.mean(center * center, axis=1, keepdims=True) + NORM_EPSILON)
    normed = center * inv_std
    scaled = d_norm * gain_ref[...]
    back = inv_std * (
        scaled
        - jnp.mean(scaled, axis=1, keepdims=True)
        - normed * jnp.mean(scaled * normed, axis=1, keepdims=True)
    )
    out_ref[...] = (dh_ref[...] + back).astype(BF16)
    sums = jnp.concatenate(
        [
            jnp.sum(d_norm * normed, axis=0, keepdims=True),
            jnp.sum(d_norm, axis=0, keepdims=True),
            jnp.concatenate(query_sums, axis=1),
            jnp.concatenate(value_sums, axis=1),
            jnp.zeros((4, width), F32),
        ],
        axis=0,
    )
    started = pl.program_id(0) > 0
    sums_ref[...] = jnp.where(started, sums_ref[...], 0.0) + sums


def first_norm(tokens, d_hidden, gain, weight, grads, block_r=256):
    rows, width = tokens.shape
    shares = tuple(g[0].shape[1] for g in grads)
    lines = pl.BlockSpec((block_r, width), lambda i: (i, 0))
    specs, arrays = [], []
    for (d_query, d_key_value), share in zip(grads, shares):
        specs += [
            pl.BlockSpec((block_r, share), lambda i: (i, 0)),
            pl.BlockSpec((2, block_r, share), lambda i: (0, i, 0)),
        ]
        arrays += [d_query, d_key_value]
    return pl.pallas_call(
        partial(first_norm_kernel, shares),
        grid=(rows // block_r,),
        in_specs=[
            lines,
            lines,
            pl.BlockSpec((1, width), lambda i: (0, 0)),
            pl.BlockSpec((width, 3 * width), lambda i: (0, 0)),
        ]
        + specs,
        out_specs=[lines, pl.BlockSpec((8, width), lambda i: (0, 0))],
        out_shape=[
            jax.ShapeDtypeStruct((rows, width), BF16),
            jax.ShapeDtypeStruct((8, width), F32),
        ],
        compiler_params=pltpu.CompilerParams(vmem_limit_bytes=VMEM_LIMIT),
        cost_estimate=pl.CostEstimate(
            flops=6 * rows * width * width,
            bytes_accessed=14 * rows * width + 6 * width * width,
            transcendentals=rows,
        ),
        name="first_norm",
    )(tokens, d_hidden, gain[None, :], weight, *arrays)


def layer_norm(values, norm_gain, norm_bias):
    center = values - jnp.mean(values, axis=-1, keepdims=True)
    inv_std = lax.rsqrt(jnp.mean(center * center, axis=-1, keepdims=True) + NORM_EPSILON)
    normed = center * inv_std
    return (normed * norm_gain + norm_bias, normed, inv_std)


def norm_backward(grad_out, normed, inv_std, norm_gain):
    scaled = grad_out * norm_gain
    return inv_std * (
        scaled
        - jnp.mean(scaled, axis=-1, keepdims=True)
        - normed * jnp.mean(scaled * normed, axis=-1, keepdims=True)
    )


def swapped(array):
    return lax.ppermute(array, "fsdp", [(0, 1), (1, 0)])


def exchanged(array):
    return lax.all_to_all(array, "expert", split_axis=0, concat_axis=0, tiled=True)


def body(
    tokens,
    out_grad,
    routes,
    prefix,
    ln1_gain,
    ln1_bias,
    w_qkv,
    q_bias,
    v_bias,
    attention_output_weight,
    attention_output_bias,
    ln2_gain,
    ln2_bias,
    w_router,
    moe_bias,
    w_in,
    w_down,
):
    experts = lax.axis_size("expert")
    my_expert = lax.axis_index("expert")
    my_half = lax.axis_index("fsdp")
    is_first = my_half == 0
    rows, width = tokens.shape[1], tokens.shape[2]
    half_width = width // 2
    slots = max(2, 2 * rows // experts) // CHUNKS
    chunk_rows = experts * slots

    def in_order(own, other, axis):
        return jnp.where(
            is_first,
            jnp.concatenate([own, other], axis=axis),
            jnp.concatenate([other, own], axis=axis),
        )

    small = jnp.concatenate(
        [
            jnp.stack(
                [
                    ln1_gain,
                    ln1_bias,
                    q_bias,
                    v_bias,
                    attention_output_bias,
                    ln2_gain,
                    ln2_bias,
                    moe_bias,
                ]
            ),
            w_router.T,
        ],
        axis=0,
    )
    small = in_order(small, swapped(small), 1)
    vectors = small[:8].astype(F32)
    norm1_gain, norm1_bias, query_bias, value_bias = (vectors[i] for i in range(4))
    output_bias, norm2_gain, norm2_bias, expert_bias = (vectors[i] for i in range(4, 8))
    router_t = small[8:]
    qkv_weight = in_order(w_qkv, swapped(w_qkv), 0)
    out_weight = lax.all_gather(attention_output_weight, "fsdp", axis=0, tiled=True)
    w_in_both = lax.all_gather(w_in[0], "fsdp", axis=0, tiled=False)
    w_down_both = lax.all_gather(w_down[0], "fsdp", axis=0, tiled=False)

    token_route = routes[0, :, 0]
    one_hot = token_route[:, None] == jnp.arange(experts, dtype=jnp.int32)[None, :]
    row_ids = jnp.arange(rows, dtype=jnp.int32)
    earlier_same = nn(
        (row_ids[None, :] < row_ids[:, None]).astype(BF16), one_hot.astype(BF16)
    )
    slot_index = jnp.sum(jnp.where(one_hot, earlier_same, 0.0), axis=-1).astype(jnp.int32)
    chunk_of = slot_index // slots
    place_in = token_route * slots + slot_index % slots
    buffer_ids = jnp.arange(chunk_rows, dtype=jnp.int32)

    def place_of(chunk):
        return jnp.where(chunk_of == chunk, place_in, -1)

    def dispatch(row_values, chunk):
        picked = nn((buffer_ids[:, None] == place_of(chunk)[None, :]).astype(BF16), row_values)
        return exchanged(picked.astype(BF16).reshape(experts, slots, width)).reshape(
            chunk_rows, width
        )

    def sent_back(buffer):
        return exchanged(buffer.reshape(experts, slots, width)).reshape(chunk_rows, width)

    def picked_up(got):
        total = None
        for chunk in range(CHUNKS):
            part = nn((place_of(chunk)[:, None] == buffer_ids[None, :]).astype(BF16), got[chunk])
            total = part if total is None else total + part
        return total

    full_place = token_route * (CHUNKS * slots) + slot_index
    full_ids = jnp.arange(CHUNKS * chunk_rows, dtype=jnp.int32)
    cot_rows = nn((full_ids[:, None] == full_place[None, :]).astype(BF16), out_grad[0])
    cot_rows = exchanged(cot_rows.astype(BF16).reshape(experts, CHUNKS * slots, width)).reshape(
        experts, CHUNKS, slots, width
    )

    residual = tokens[0].astype(F32)
    norm1_out, normed1, inv_std1 = layer_norm(residual, norm1_gain, norm1_bias)
    attn_in = norm1_out.astype(BF16)
    key_value = (
        nn(attn_in, qkv_weight[:, width:])
        + jnp.concatenate([jnp.zeros_like(value_bias), value_bias])
    ).astype(BF16)
    prev_key_value = lax.ppermute(key_value, "fsdp", [(0, 1)])
    queries = ((nn(attn_in, qkv_weight[:, :width]) + query_bias) * (HEAD_DIM**-0.5)).astype(BF16)
    scalars = jnp.stack([my_half, prefix[0] - my_half * rows]).astype(jnp.int32)
    context, lse = attention_forward(scalars, queries, prev_key_value, key_value)
    hidden = residual + (nn(context, out_weight) + output_bias)
    norm2_out, normed2, inv_std2 = layer_norm(hidden, norm2_gain, norm2_bias)
    mixed = norm2_out.astype(BF16)

    mixed_rows = [dispatch(mixed, chunk) for chunk in range(CHUNKS)]
    router_pad = jnp.pad(router_t, ((0, LANES - experts), (0, 0)))
    expert_scalars = jnp.stack([my_expert, my_half]).astype(jnp.int32)
    done, y_rows = [], None
    for c in range(CHUNKS):
        y_rows, *rest = run_expert(
            expert_scalars,
            mixed_rows[c],
            cot_rows,
            w_in_both,
            w_down_both,
            router_pad,
            y_rows,
            c,
            experts,
        )
        done.append(rest)
    d_mixed_chunks, act, du, dy, dz = ([d[i] for d in done] for i in range(5))
    back = [sent_back(d) for d in d_mixed_chunks]
    others = expert_weights(mixed_rows, dy, act, du, 1, None)
    back[-1], others = lax.optimization_barrier((back[-1], others))
    d_mixed = picked_up(back)
    got = [swapped(o) for o in others]
    d_router = None
    for c in range(CHUNKS):
        part = tn(mixed_rows[c], dz[c])
        d_router = part if d_router is None else d_router + part

    out_cot = out_grad[0].astype(F32)
    d_expert_bias = jnp.sum(out_cot, axis=0)
    d_norm2_gain = jnp.sum(d_mixed * normed2, axis=0)
    d_norm2_bias = jnp.sum(d_mixed, axis=0)
    d_hidden = out_cot + norm_backward(d_mixed, normed2, inv_std2, norm2_gain)
    d_attn = d_hidden.astype(BF16)
    d_output_bias = jnp.sum(d_attn.astype(F32), axis=0)
    d_context = nt(d_attn, out_weight).astype(BF16)

    logits = nt(mixed, router_t)
    router_probs = jax.nn.softmax(logits, axis=-1)
    gate_value = jnp.sum(jnp.where(one_hot, router_probs, 0.0), axis=-1)
    y_back = exchanged(y_rows.reshape(experts, CHUNKS * slots, width)).reshape(-1, width)
    def as_columns(pieces):
        packed = jnp.concatenate(pieces, axis=1)
        return jnp.pad(packed, ((0, 0), (0, -packed.shape[1] % LANES)))

    def split_columns(columns):
        top, bottom = columns[:half_width], columns[half_width:]
        return (
            jnp.where(is_first, top, bottom),
            swapped(jnp.where(is_first, bottom, top).astype(BF16)),
        )

    early = split_columns(
        as_columns(
            [
                d_router[:, :experts],
                jnp.stack([d_expert_bias, d_norm2_gain, d_norm2_bias, d_output_bias], axis=1),
            ]
        )
    )

    own_index = my_half[None].astype(jnp.int32)
    other_index = 1 - own_index
    pairs = width // LANES
    groups = ((0, FIRST_PAIRS), (FIRST_PAIRS, pairs - FIRST_PAIRS))
    grads, sums = [], []
    for number, (begin, count) in enumerate(groups):
        d_query, prev_grad, own_grad = attention_backward(
            scalars, queries, prev_key_value, key_value, context, lse, d_context, begin, count
        )
        returned = lax.ppermute(prev_grad, "fsdp", [(1, 0)])
        d_key_value = (own_grad.astype(F32) + returned.astype(F32)).astype(BF16)
        grads.append((d_query, d_key_value))
        if number == 0:
            d_key_value, y_back = lax.optimization_barrier((d_key_value, y_back))
        products = [(attn_in, [d_query, d_key_value])]
        if number == 0:
            products.append((context, [d_attn]))
        other_part = swapped(pair_weights(other_index, products))
        if number == 0:
            extra = early
        else:
            d_tokens, norm_sums = first_norm(tokens[0], d_hidden, norm1_gain, qkv_weight, grads)
            norm_sums, sums[0] = lax.optimization_barrier((norm_sums, sums[0]))
            extra = split_columns(as_columns([norm_sums.T]))
        own_part = pair_weights(own_index, products, (other_part,) + extra)
        blocks = own_part.reshape(experts, half_width // experts, own_part.shape[1])
        if number < len(groups) - 1:
            d_context, blocks = lax.optimization_barrier((d_context, blocks))
        sums.append(jnp.sum(exchanged(blocks).astype(F32), axis=0))
    d_w_in, d_w_down = expert_weights(mixed_rows, dy, act, du, 0, got)
    expert_value = nn((full_place[:, None] == full_ids[None, :]).astype(BF16), y_back)
    output = hidden + gate_value[:, None] * expert_value + expert_bias

    sum_qkv = jnp.concatenate(
        [
            sums[g][:, i * count * LANES : (i + 1) * count * LANES]
            for i in range(3)
            for g, (begin, count) in enumerate(groups)
        ],
        axis=1,
    )
    sum_out = sums[0][:, 3 * groups[0][1] * LANES :]
    sum_last = sums[-1][:, 3 * groups[-1][1] * LANES :]
    return (
        output.astype(BF16)[None],
        d_tokens[None],
        sum_last[:, 0],
        sum_last[:, 1],
        sum_qkv,
        sum_last[:, 2],
        sum_last[:, 3],
        sum_out[:, :width],
        sum_out[:, width + experts + 3],
        sum_out[:, width + experts + 1],
        sum_out[:, width + experts + 2],
        sum_out[:, width : width + experts],
        sum_out[:, width + experts],
        d_w_in[None],
        d_w_down[None],
    )


def solution(mesh):
    vector = P(("fsdp", "expert"))
    matrix = P(("fsdp", "expert"), None)
    tokens = P("expert", "fsdp", None)
    return jax.shard_map(
        body,
        mesh=mesh,
        in_specs=(
            tokens,
            tokens,
            tokens,
            P("expert"),
            P("fsdp"),
            P("fsdp"),
            P("fsdp", None),
            P("fsdp"),
            P("fsdp"),
            P("fsdp", None),
            P("fsdp"),
            P("fsdp"),
            P("fsdp"),
            P("fsdp", None),
            P("fsdp"),
            P("expert", None, "fsdp"),
            P("expert", "fsdp", None),
        ),
        out_specs=(
            tokens,
            tokens,
            vector,
            vector,
            matrix,
            vector,
            vector,
            matrix,
            vector,
            vector,
            vector,
            matrix,
            vector,
            P("expert", None, "fsdp"),
            P("expert", "fsdp", None),
        ),
        check_vma=False,
    )
```

```python
from functools import partial

import jax
import jax.numpy as jnp
from jax import lax
from jax.experimental import pallas as pl
from jax.experimental.pallas import tpu as pltpu
from jax.sharding import PartitionSpec as P

HEAD_DIM = 64
NORM_EPSILON = 1e-05
MASK_FILL = -1e30
LOG2E = 1.4426950408889634
SAFE_LOG2 = 90.0
GELU_A = 0.7978845608028654
GELU_B = 0.044715
CHUNKS = 2
BWD_Q = 512
BWD_K = 512
FIRST_PAIRS = 4
LANES = 128
BF16 = jnp.bfloat16
F32 = jnp.float32
VMEM_LIMIT = 56 << 20


def nn(left, right):
    return lax.dot_general(left, right, (((1,), (0,)), ((), ())), preferred_element_type=F32)


def nt(left, right):
    return lax.dot_general(left, right, (((1,), (1,)), ((), ())), preferred_element_type=F32)


def tn(left, right):
    return lax.dot_general(left, right, (((0,), (0,)), ((), ())), preferred_element_type=F32)


def lane_index(rows):
    return lax.broadcasted_iota(jnp.int32, (rows, LANES), 1)


def in_three(values):
    high = values.astype(BF16).astype(F32)
    rest = values - high
    middle = rest.astype(BF16).astype(F32)
    return high, middle, rest - middle


def three_columns(values, place):
    high, middle, low = in_three(values)
    return jnp.where(
        place == 0, high, jnp.where(place == 1, middle, jnp.where(place == 2, low, 0.0))
    )


def forward_kernel(
    block,
    scalars,
    q_ref,
    prev_k_ref,
    prev_v_ref,
    own_k_ref,
    own_v_ref,
    out_ref,
    lse_ref,
    values_one,
    query_parts,
    keys_both,
    total,
    top,
):
    rows = q_ref.shape[0]
    has_prev, own_prefix = scalars[0], scalars[1]
    lane = lane_index(rows)
    first = lane < HEAD_DIM
    zero = jnp.zeros((rows, LANES), BF16)
    one = jnp.ones((rows, LANES), BF16)
    own_values, prev_values = own_v_ref[...], prev_v_ref[...]
    values_one[0, 0] = jnp.where(first, prev_values, one)
    values_one[1, 0] = jnp.where(first, one, prev_values)
    values_one[0, 1] = jnp.where(first, own_values, one)
    values_one[1, 1] = jnp.where(first, one, own_values)
    scaled = q_ref[...].astype(F32) * LOG2E
    high = scaled.astype(BF16)
    low = (scaled - high.astype(F32)).astype(BF16)
    query_parts[0, :, :LANES] = jnp.where(first, high, zero)
    query_parts[0, :, LANES:] = jnp.where(first, low, zero)
    query_parts[1, :, :LANES] = jnp.where(first, zero, high)
    query_parts[1, :, LANES:] = jnp.where(first, zero, low)

    same_head = (
        lax.broadcasted_iota(jnp.int32, (LANES, LANES), 0) < HEAD_DIM
    ) == (lax.broadcasted_iota(jnp.int32, (LANES, LANES), 1) < HEAD_DIM)
    same_head = jnp.where(same_head, 1.0, 0.0).astype(BF16)

    def longest(ref):
        values = ref[...].astype(F32)
        return jnp.max(nn((values * values).astype(BF16), same_head), axis=0, keepdims=True)

    keys_longest = jnp.maximum(longest(own_k_ref), longest(prev_k_ref))
    small = jnp.max(longest(q_ref) * keys_longest) < (SAFE_LOG2 / LOG2E) ** 2
    keys_both[0] = prev_k_ref[...]
    keys_both[1] = own_k_ref[...]
    first_part = jnp.where(has_prev > 0, 0, 1)
    total[...] = jnp.zeros_like(total)

    def scores_of(h, keys, queries_at, size_q, part, at, size_k):
        scores = nt(query_parts[h, queries_at, :], keys)
        key_pos = at + (part - 1) * rows + lax.broadcasted_iota(jnp.int32, (1, size_k), 1)
        query_pos = queries_at.start + lax.broadcasted_iota(jnp.int32, (size_q, 1), 0)
        visible = key_pos <= jnp.maximum(query_pos, own_prefix - 1)
        return jnp.where(visible, scores, MASK_FILL)

    def keys_twice(part, at, size):
        keys = keys_both[part, pl.ds(at, size), :]
        return jnp.concatenate([keys, keys], axis=1)

    @pl.when(small)
    def _():
        top[...] = jnp.zeros_like(top)

        def add_up(part, carried):
            keys = keys_twice(part, 0, rows)
            for h in range(2):
                scores = scores_of(h, keys, pl.ds(0, rows), rows, part, 0, rows)
                total[h] += nn(jnp.exp2(scores).astype(BF16), values_one[h, part])
            return carried

        lax.fori_loop(first_part, 2, add_up, 0)

    @pl.when(jnp.logical_not(small))
    def _():
        size = block
        blocks = rows // size
        lane = lane_index(size)
        place = lane & (HEAD_DIM - 1)
        three = jnp.where(place < 3, 1.0, 0.0).astype(BF16)

        def queries_block(i, carried):
            here = pl.ds(pl.multiple_of(i * size, size), size)

            def over_keys(visit):
                def one(n, carried):
                    part = n // blocks
                    visit(part, pl.multiple_of(lax.rem(n, blocks) * size, size))
                    return carried

                lax.fori_loop(first_part * blocks, 2 * blocks, one, 0)

            for h in range(2):
                top[h, here, :] = jnp.full((size, LANES), MASK_FILL, F32)

                def find_top(part, at):
                    keys = keys_twice(part, at, size)
                    scores = scores_of(h, keys, here, size, part, at, size)
                    largest = top[h, here, :]
                    for t in range(size // LANES):
                        largest = jnp.maximum(largest, scores[:, t * LANES : (t + 1) * LANES])
                    top[h, here, :] = largest

                over_keys(find_top)
                maximum = jnp.max(top[h, here, :], axis=1, keepdims=True)
                maximum = jnp.broadcast_to(maximum, (size, LANES))
                top[h, here, :] = maximum
                mine = (lane < HEAD_DIM) == (h == 0)
                less = jnp.where(mine, three_columns(-maximum, place), 0.0).astype(BF16)

                def add_up(part, at):
                    keys = keys_twice(part, at, size)
                    scores = scores_of(h, keys, here, size, part, at, size) + nt(less, three)
                    weights = jnp.exp2(scores).astype(BF16)
                    total[h, here, :] += nn(weights, values_one[h, part, pl.ds(at, size), :])

                over_keys(add_up)
            return carried

        lax.fori_loop(0, blocks, queries_block, 0)

    sum_a, sum_b = total[0], total[1]
    weight = jnp.where(first, pltpu.roll(sum_a, HEAD_DIM, 1), pltpu.roll(sum_b, HEAD_DIM, 1))
    out_ref[...] = (jnp.where(first, sum_a, sum_b) / weight).astype(BF16)
    lse_ref[...] = jnp.where(first, top[0], top[1]) * (1.0 / LOG2E) + jnp.log(weight)


def attention_forward(scalars, queries, prev, own, block=512):
    rows, width = queries.shape
    pairs = width // LANES

    def spec(offset):
        return pl.BlockSpec((rows, LANES), lambda h, scalars: (0, h + offset))

    return pl.pallas_call(
        partial(forward_kernel, block),
        grid_spec=pltpu.PrefetchScalarGridSpec(
            num_scalar_prefetch=1,
            grid=(pairs,),
            in_specs=[spec(0), spec(0), spec(pairs), spec(0), spec(pairs)],
            out_specs=[spec(0), spec(0)],
            scratch_shapes=[
                pltpu.VMEM((2, 2, rows, LANES), BF16),
                pltpu.VMEM((2, rows, 2 * LANES), BF16),
                pltpu.VMEM((2, rows, LANES), BF16),
                pltpu.VMEM((2, rows, LANES), F32),
                pltpu.VMEM((2, rows, LANES), F32),
            ],
        ),
        out_shape=[
            jax.ShapeDtypeStruct((rows, width), BF16),
            jax.ShapeDtypeStruct((rows, width), F32),
        ],
        compiler_params=pltpu.CompilerParams(vmem_limit_bytes=VMEM_LIMIT),
        cost_estimate=pl.CostEstimate(
            flops=4 * rows * rows * width,
            bytes_accessed=16 * rows * width,
            transcendentals=rows * rows,
        ),
        name="attention_forward",
    )(scalars, queries, prev, prev, own, own)


def over_visible(has_prev, own_prefix, rows, block_q, block_k, begin, visit, end):
    query_blocks, key_blocks = rows // block_q, rows // block_k

    def one_block(j, carried):
        line = pl.multiple_of(j * block_k, block_k)
        at = line - rows
        begin()
        seen_by_all = (at < 0) | (own_prefix > at)
        first_seen = jnp.where(seen_by_all, 0, jnp.maximum(at, 0) // block_q)

        def step(i, carried):
            visit(line, pl.multiple_of(i * block_q, block_q))
            return carried

        lax.fori_loop(first_seen, query_blocks, step, 0)
        end(line)
        return carried

    lax.fori_loop(jnp.where(has_prev > 0, 0, key_blocks), 2 * key_blocks, one_block, 0)


def weights_kernel(
    block_q, block_k, scalars, q_ref, prev_k_ref, own_k_ref, lse_ref, weights_ref, query_aug, keys_both
):
    rows = q_ref.shape[0]
    has_prev, own_prefix = scalars[0], scalars[1]
    lane = lane_index(rows)
    first = lane < HEAD_DIM
    zero = jnp.zeros((rows, LANES), BF16)
    queries = q_ref[...]
    less = three_columns(-lse_ref[...], lane & (HEAD_DIM - 1)).astype(BF16)
    query_aug[0, :, :LANES] = jnp.where(first, queries, zero)
    query_aug[0, :, LANES:] = jnp.where(first, less, zero)
    query_aug[1, :, :LANES] = jnp.where(first, zero, queries)
    query_aug[1, :, LANES:] = jnp.where(first, zero, less)
    ones = jnp.where((lane_index(block_k) & (HEAD_DIM - 1)) < 3, 1.0, 0.0).astype(BF16)

    keys_both[:rows] = prev_k_ref[...]
    keys_both[rows:] = own_k_ref[...]

    def visit(line, start):
        keys_aug = jnp.concatenate([keys_both[pl.ds(line, block_k), :], ones], axis=1)
        key_pos = line - rows + lax.broadcasted_iota(jnp.int32, (block_k, 1), 0)
        query_pos = start + lax.broadcasted_iota(jnp.int32, (1, block_q), 1)
        visible = key_pos <= jnp.maximum(query_pos, own_prefix - 1)
        for h in range(2):
            scores = nt(keys_aug, query_aug[h, pl.ds(start, block_q), :]) * LOG2E
            scores = jnp.where(visible, scores, MASK_FILL)
            weights_ref[h, pl.ds(line, block_k), pl.ds(start, block_q)] = jnp.exp2(
                scores
            ).astype(BF16)

    def nothing(*unused):
        return None

    over_visible(has_prev, own_prefix, rows, block_q, block_k, nothing, visit, nothing)


def attention_weights(scalars, queries, prev, own, lse, block_q=1024, block_k=512):
    rows, width = queries.shape
    pairs = width // LANES
    spec = pl.BlockSpec((rows, LANES), lambda h, scalars: (0, h))
    return pl.pallas_call(
        partial(weights_kernel, block_q, block_k),
        grid_spec=pltpu.PrefetchScalarGridSpec(
            num_scalar_prefetch=1,
            grid=(pairs,),
            in_specs=[spec] * 4,
            out_specs=pl.BlockSpec((None, 2, 2 * rows, rows), lambda h, scalars: (h, 0, 0, 0)),
            scratch_shapes=[
                pltpu.VMEM((2, rows, 2 * LANES), BF16),
                pltpu.VMEM((2 * rows, LANES), BF16),
            ],
        ),
        out_shape=jax.ShapeDtypeStruct((pairs, 2, 2 * rows, rows), BF16),
        compiler_params=pltpu.CompilerParams(vmem_limit_bytes=VMEM_LIMIT),
        cost_estimate=pl.CostEstimate(
            flops=8 * rows * rows * width,
            bytes_accessed=4 * pairs * rows * rows * 2 + 10 * rows * width,
            transcendentals=2 * rows * rows * width // HEAD_DIM,
        ),
        name="attention_weights",
    )(scalars, queries, prev, own, lse)


def backward_kernel(
    block_q,
    block_k,
    scalars,
    q_ref,
    prev_k_ref,
    prev_v_ref,
    own_k_ref,
    own_v_ref,
    out_ref,
    grad_ref,
    weights_ref,
    dq_ref,
    prev_grad_ref,
    own_grad_ref,
    grad_aug,
    keys_both,
    values_both,
    dq_total,
    dk_total,
    dv_total,
):
    rows = q_ref.shape[0]
    has_prev, own_prefix = scalars[0], scalars[1]
    lane = lane_index(rows)
    first = lane < HEAD_DIM
    zero = jnp.zeros((rows, LANES), BF16)
    grads = grad_ref[...]
    products = grads.astype(F32) * out_ref[...].astype(F32)
    delta_a = jnp.sum(jnp.where(first, products, 0.0), axis=1, keepdims=True)
    delta_b = jnp.sum(jnp.where(first, 0.0, products), axis=1, keepdims=True)
    less = three_columns(-jnp.where(first, delta_a, delta_b), lane & (HEAD_DIM - 1)).astype(BF16)
    grad_aug[0, :, :LANES] = jnp.where(first, grads, zero)
    grad_aug[0, :, LANES:] = jnp.where(first, less, zero)
    grad_aug[1, :, :LANES] = jnp.where(first, zero, grads)
    grad_aug[1, :, LANES:] = jnp.where(first, zero, less)
    ones = jnp.where((lane_index(block_k) & (HEAD_DIM - 1)) < 3, 1.0, 0.0).astype(BF16)
    keys_first = lane_index(block_k) < HEAD_DIM
    queries_first = lane_index(block_q) < HEAD_DIM
    dq_total[...] = jnp.zeros_like(dq_total)

    keys_both[:rows] = prev_k_ref[...]
    keys_both[rows:] = own_k_ref[...]
    values_both[:rows] = prev_v_ref[...]
    values_both[rows:] = own_v_ref[...]

    def visit(line, start):
        lines, queries_at = pl.ds(line, block_k), pl.ds(start, block_q)
        keys = keys_both[lines, :]
        values_aug = jnp.concatenate([values_both[lines, :], ones], axis=1)
        probs, d_scores = [], []
        for h in range(2):
            part = weights_ref[h, lines, queries_at]
            centered = nt(values_aug, grad_aug[h, queries_at, :])
            d_scores.append((part.astype(F32) * centered).astype(BF16))
            probs.append(part)
        here_grads, here_queries = grad_ref[queries_at, :], q_ref[queries_at, :]
        dv_total[...] += jnp.where(keys_first, nn(probs[0], here_grads), nn(probs[1], here_grads))
        dk_total[...] += jnp.where(
            keys_first, nn(d_scores[0], here_queries), nn(d_scores[1], here_queries)
        )
        dq_total[queries_at, :] += jnp.where(
            queries_first, tn(d_scores[0], keys), tn(d_scores[1], keys)
        )

    @pl.when(has_prev == 0)
    def _():
        prev_grad_ref[0] = zero
        prev_grad_ref[1] = zero

    def clear():
        dk_total[...] = jnp.zeros_like(dk_total)
        dv_total[...] = jnp.zeros_like(dv_total)

    def put(line):
        @pl.when(line < rows)
        def _():
            prev_grad_ref[0, pl.ds(line, block_k), :] = dk_total[...].astype(BF16)
            prev_grad_ref[1, pl.ds(line, block_k), :] = dv_total[...].astype(BF16)

        @pl.when(line >= rows)
        def _():
            at = pl.multiple_of(line - rows, block_k)
            own_grad_ref[0, pl.ds(at, block_k), :] = dk_total[...].astype(BF16)
            own_grad_ref[1, pl.ds(at, block_k), :] = dv_total[...].astype(BF16)

    over_visible(has_prev, own_prefix, rows, block_q, block_k, clear, visit, put)
    dq_ref[...] = (dq_total[...] * (HEAD_DIM**-0.5)).astype(BF16)


def attention_backward(
    scalars, queries, prev, own, out, grads, weights, begin, count, block_q=BWD_Q, block_k=BWD_K
):
    rows, width = queries.shape
    pairs = width // LANES

    def spec(offset):
        return pl.BlockSpec((rows, LANES), lambda h, scalars: (0, h + begin + offset))

    both = pl.BlockSpec((2, rows, LANES), lambda h, scalars: (0, 0, h))
    share = count * LANES
    return pl.pallas_call(
        partial(backward_kernel, block_q, block_k),
        grid_spec=pltpu.PrefetchScalarGridSpec(
            num_scalar_prefetch=1,
            grid=(count,),
            in_specs=[spec(0), spec(0), spec(pairs), spec(0), spec(pairs), spec(0), spec(0)]
            + [pl.BlockSpec((None, 2, 2 * rows, rows), lambda h, scalars: (h + begin, 0, 0, 0))],
            out_specs=[pl.BlockSpec((rows, LANES), lambda h, scalars: (0, h)), both, both],
            scratch_shapes=[
                pltpu.VMEM((2, rows, 2 * LANES), BF16),
                pltpu.VMEM((2 * rows, LANES), BF16),
                pltpu.VMEM((2 * rows, LANES), BF16),
                pltpu.VMEM((rows, LANES), F32),
                pltpu.VMEM((block_k, LANES), F32),
                pltpu.VMEM((block_k, LANES), F32),
            ],
        ),
        out_shape=[
            jax.ShapeDtypeStruct((rows, share), BF16),
            jax.ShapeDtypeStruct((2, rows, share), BF16),
            jax.ShapeDtypeStruct((2, rows, share), BF16),
        ],
        compiler_params=pltpu.CompilerParams(vmem_limit_bytes=VMEM_LIMIT),
        cost_estimate=pl.CostEstimate(
            flops=60 * rows * rows * share,
            bytes_accessed=26 * rows * share,
            transcendentals=2 * rows * rows * share // HEAD_DIM,
        ),
        name="attention_backward",
    )(scalars, queries, prev, prev, own, own, out, grads, weights)


def expert_kernel(
    experts,
    block_r,
    scalars,
    rows_ref,
    cot_ref,
    w_in_ref,
    w_down_ref,
    router_ref,
    y_before_ref,
    y_ref,
    dm_ref,
    act_ref,
    du_ref,
    dy_ref,
    dz_ref,
    y_total,
    dm_total,
    probs,
):
    step = pl.program_id(0)
    slots, width = cot_ref.shape[1], cot_ref.shape[2]
    sources = block_r // slots
    lane = lane_index(block_r)
    is_mine = lane == scalars[0]

    def over_rows(work):
        for b in range(rows_ref.shape[0] // block_r):
            work(slice(b * block_r, (b + 1) * block_r), slice(b * sources, (b + 1) * sources))

    def cots(source):
        return cot_ref[source].reshape(block_r, width).astype(F32)

    @pl.when(step == 0)
    def _():
        def gate(here, source):
            logits = nt(rows_ref[here, :], router_ref[...])
            logits = jnp.where(lane < experts, logits, MASK_FILL)
            spread = jnp.exp(logits - jnp.max(logits, axis=1, keepdims=True))
            part = spread / jnp.sum(spread, axis=1, keepdims=True)
            probs[here, :] = part
            mine = jnp.sum(jnp.where(is_mine, part, 0.0), axis=1, keepdims=True)
            dy_ref[here, :] = (mine * cots(source)).astype(BF16)
            y_total[here, :] = jnp.zeros((block_r, y_total.shape[1]), F32)
            dm_total[here, :] = jnp.zeros((block_r, dm_total.shape[1]), F32)

        over_rows(gate)

    def hidden_block(here, source):
        u = nn(rows_ref[here, :], w_in_ref[...])
        d_act = nt(dy_ref[here, :], w_down_ref[...])
        square = u * u
        bend = jnp.tanh(u * (GELU_A + (GELU_A * GELU_B) * square))
        half = 0.5 + 0.5 * bend
        act = (u * half).astype(BF16)
        slope = half + (0.5 * u) * (1.0 - bend * bend) * (
            GELU_A + (3.0 * GELU_A * GELU_B) * square
        )
        du = (d_act * slope).astype(BF16)
        act_ref[here, :] = act
        du_ref[here, :] = du
        y_total[here, :] += nn(act, w_down_ref[...])
        dm_total[here, :] += nt(du, w_in_ref[...])

    over_rows(hidden_block)

    @pl.when(step == pl.num_programs(0) - 1)
    def _():
        def finish(here, source):
            y = y_total[here, :].astype(BF16)
            y_ref[source] = y.reshape(sources, slots, width)
            d_gate = jnp.sum(cots(source) * y.astype(F32), axis=1, keepdims=True)
            part = probs[here, :]
            mine = jnp.sum(jnp.where(is_mine, part, 0.0), axis=1, keepdims=True)
            dz = ((d_gate * mine) * (jnp.where(is_mine, 1.0, 0.0) - part)).astype(BF16)
            dz = jnp.where(lane < experts, dz, jnp.zeros_like(dz))
            dz_ref[here, :] = dz
            dm_ref[here, :] = (dm_total[here, :] + nn(dz, router_ref[...])).astype(BF16)

        over_rows(finish)


def run_expert(
    scalars, rows_in, cots, w_in, w_down, router, y_before, chunk, experts, block_h=512, block_r=1024
):
    rows, width = rows_in.shape
    half = w_in.shape[2]
    per_half = half // block_h
    whole = pl.BlockSpec((rows, width), lambda j, s: (0, 0))
    hidden = pl.BlockSpec((rows, block_h), lambda j, s: (0, j))
    mine = pl.BlockSpec(
        (cots.shape[0], None, cots.shape[2], width), lambda j, s: (0, chunk, 0, 0)
    )

    def which(j, s):
        return lax.rem(j // per_half + s[1], 2)

    first = y_before is None
    return pl.pallas_call(
        partial(expert_kernel, experts, block_r),
        grid_spec=pltpu.PrefetchScalarGridSpec(
            num_scalar_prefetch=1,
            grid=(2 * per_half,),
            in_specs=[
                whole,
                mine,
                pl.BlockSpec(
                    (None, width, block_h), lambda j, s: (which(j, s), 0, lax.rem(j, per_half))
                ),
                pl.BlockSpec(
                    (None, block_h, width), lambda j, s: (which(j, s), lax.rem(j, per_half), 0)
                ),
                pl.BlockSpec((LANES, width), lambda j, s: (0, 0)),
                pl.BlockSpec(memory_space=pl.ANY),
            ],
            out_specs=[
                mine,
                whole,
                hidden,
                hidden,
                whole,
                pl.BlockSpec((rows, LANES), lambda j, s: (0, 0)),
            ],
            scratch_shapes=[
                pltpu.VMEM((rows, width), F32),
                pltpu.VMEM((rows, width), F32),
                pltpu.VMEM((rows, LANES), F32),
            ],
        ),
        out_shape=[
            jax.ShapeDtypeStruct(cots.shape, BF16),
            jax.ShapeDtypeStruct((rows, width), BF16),
            jax.ShapeDtypeStruct((rows, 2 * half), BF16),
            jax.ShapeDtypeStruct((rows, 2 * half), BF16),
            jax.ShapeDtypeStruct((rows, width), BF16),
            jax.ShapeDtypeStruct((rows, LANES), BF16),
        ],
        input_output_aliases={} if first else {6: 0},
        compiler_params=pltpu.CompilerParams(vmem_limit_bytes=VMEM_LIMIT),
        cost_estimate=pl.CostEstimate(
            flops=16 * rows * width * half,
            bytes_accessed=8 * width * half + 12 * rows * width + 8 * rows * half,
            transcendentals=2 * rows * half,
        ),
        name="expert_rows",
    )(scalars, rows_in, cots, w_in, w_down, router, scalars if first else y_before)


def expert_weights_kernel(chunks, add, *refs):
    rows_refs, dy_refs, act_refs, du_refs = (
        refs[i * chunks : (i + 1) * chunks] for i in range(4)
    )
    rest = refs[4 * chunks :]
    d_in_ref, d_down_ref, turned = rest[-3:]
    rows = rows_refs[0].shape[0]

    @pl.when(pl.program_id(0) == 0)
    def _():
        for c in range(chunks):
            turned[:, c * rows : (c + 1) * rows] = rows_refs[c][...].T

    d_in, d_down = None, None
    for c in range(chunks):
        part = nn(turned[:, c * rows : (c + 1) * rows], du_refs[c][...])
        d_in = part if d_in is None else d_in + part
        part = tn(act_refs[c][...], dy_refs[c][...])
        d_down = part if d_down is None else d_down + part
    if add:
        d_in = d_in + rest[0][...].astype(F32)
        d_down = d_down + rest[1][...].astype(F32)
    d_in_ref[...] = d_in.astype(d_in_ref.dtype)
    d_down_ref[...] = d_down.astype(d_down_ref.dtype)


def expert_weights(rows_in, dy, act, du, half_index, got, block_h=512):
    chunks = len(rows_in)
    rows, width = rows_in[0].shape
    half = du[0].shape[1] // 2
    steps = half // block_h
    whole = pl.BlockSpec((rows, width), lambda j: (0, 0))
    hidden = pl.BlockSpec((rows, block_h), lambda j: (0, j + half_index * steps))
    columns = pl.BlockSpec((width, block_h), lambda j: (0, j))
    lines = pl.BlockSpec((block_h, width), lambda j: (j, 0))
    dtype = BF16 if got is None else F32
    extra = () if got is None else tuple(got)
    return pl.pallas_call(
        partial(expert_weights_kernel, chunks, got is not None),
        grid=(steps,),
        in_specs=[whole] * (2 * chunks) + [hidden] * (2 * chunks) + [columns, lines][: len(extra)],
        out_specs=[columns, lines],
        out_shape=[
            jax.ShapeDtypeStruct((width, half), dtype),
            jax.ShapeDtypeStruct((half, width), dtype),
        ],
        scratch_shapes=[pltpu.VMEM((width, chunks * rows), BF16)],
        compiler_params=pltpu.CompilerParams(vmem_limit_bytes=VMEM_LIMIT),
        cost_estimate=pl.CostEstimate(
            flops=4 * chunks * rows * width * half,
            bytes_accessed=4 * chunks * rows * (width + half) + 8 * width * half,
            transcendentals=0,
        ),
        name="expert_weights",
    )(*rows_in, *dy, *act, *du, *extra)


def both_sums(own_ref, back_ref, i):
    return (own_ref[i].astype(F32) + back_ref[i].astype(F32)).astype(BF16)


def pair_weights_kernel(with_context, scalars, *refs):
    in_ref, dq_ref, own_ref, back_ref, vectors_ref = refs[:5]
    outs = refs[-2:]
    is_first = scalars[0] == 0
    half = outs[0].shape[0]
    column = 0

    def put(top, bottom):
        nonlocal column
        here = slice(column, column + top.shape[1])
        column += top.shape[1]
        top, bottom = top.astype(BF16), bottom.astype(BF16)
        outs[0][:, here] = jnp.where(is_first, top, bottom)
        outs[1][:, here] = jnp.where(is_first, bottom, top)

    def products(left, rights):
        turned = left[...].T
        for right in rights:
            put(nn(turned[:half], right), nn(turned[half:], right))

    products(in_ref, [dq_ref[...]] + [both_sums(own_ref, back_ref, i) for i in range(2)])
    if with_context:
        products(refs[5], [refs[6][...]])
    turned = vectors_ref[...].T
    put(turned[:half], turned[half:])


def pair_weights(half_index, attn_in, grads, vectors, context_side=()):
    d_query, own_grad, back_grad = grads
    rows, width = attn_in.shape
    columns = 3 * d_query.shape[1] + vectors.shape[0]
    if context_side:
        columns += context_side[1].shape[1]

    def full(shape):
        return pl.BlockSpec(shape, lambda i, s: (0,) * len(shape))

    arrays = [attn_in, d_query, own_grad, back_grad, vectors] + list(context_side)
    out = full((width // 2, columns))
    return pl.pallas_call(
        partial(pair_weights_kernel, bool(context_side)),
        grid_spec=pltpu.PrefetchScalarGridSpec(
            num_scalar_prefetch=1,
            grid=(1,),
            in_specs=[full(x.shape) for x in arrays],
            out_specs=[out, out],
        ),
        out_shape=[jax.ShapeDtypeStruct((width // 2, columns), BF16)] * 2,
        compiler_params=pltpu.CompilerParams(vmem_limit_bytes=VMEM_LIMIT),
        cost_estimate=pl.CostEstimate(
            flops=2 * rows * width * columns,
            bytes_accessed=4 * (rows + width) * columns,
            transcendentals=0,
        ),
        name="pair_weights",
    )(half_index, *arrays)


def normalized(values):
    center = values - jnp.mean(values, axis=1, keepdims=True)
    inv_std = lax.rsqrt(jnp.mean(center * center, axis=1, keepdims=True) + NORM_EPSILON)
    return center * inv_std, inv_std


def rows_in_order(is_first, own_ref, other_ref):
    own, other = own_ref[...], other_ref[...]
    return jnp.concatenate(
        [jnp.where(is_first, own, other), jnp.where(is_first, other, own)], axis=0
    )


def key_value_kernel(scalars, tokens_ref, norm_ref, own_ref, other_ref, add_ref, out_ref, in_ref):
    @pl.when(pl.program_id(0) == 0)
    def _():
        normed, inv_std = normalized(tokens_ref[...].astype(F32))
        in_ref[...] = (normed * norm_ref[0:1, :] + norm_ref[1:2, :]).astype(BF16)

    weight = rows_in_order(scalars[0] == 0, own_ref, other_ref)
    out_ref[...] = (nn(in_ref[...], weight) + add_ref[...]).astype(BF16)


def query_kernel(scalars, in_ref, own_ref, other_ref, add_ref, out_ref):
    weight = rows_in_order(scalars[0] == 0, own_ref, other_ref)
    out_ref[...] = ((nn(in_ref[...], weight) + add_ref[...]) * (HEAD_DIM**-0.5)).astype(BF16)


def project(half_index, rows_in, w_own, w_other, bias, norm=None, block_n=512):
    rows, width = rows_in.shape
    columns = bias.shape[0]
    begin = 0 if norm is None else width // block_n
    half = pl.BlockSpec((width // 2, block_n), lambda j, s: (0, begin + j))
    whole = pl.BlockSpec((rows, width), lambda j, s: (0, 0))
    line = pl.BlockSpec((1, block_n), lambda j, s: (0, j))
    block = pl.BlockSpec((rows, block_n), lambda j, s: (0, j))
    shape = jax.ShapeDtypeStruct((rows, columns), BF16)
    if norm is None:
        in_specs, out_specs, out_shape = [whole, half, half, line], block, shape
        arrays = (rows_in, w_own, w_other, bias[None, :])
    else:
        in_specs = [whole, pl.BlockSpec((2, width), lambda j, s: (0, 0)), half, half, line]
        out_specs = [block, whole]
        out_shape = [shape, jax.ShapeDtypeStruct((rows, width), BF16)]
        arrays = (rows_in, norm, w_own, w_other, bias[None, :])
    return pl.pallas_call(
        query_kernel if norm is None else key_value_kernel,
        grid_spec=pltpu.PrefetchScalarGridSpec(
            num_scalar_prefetch=1,
            grid=(columns // block_n,),
            in_specs=in_specs,
            out_specs=out_specs,
        ),
        out_shape=out_shape,
        compiler_params=pltpu.CompilerParams(vmem_limit_bytes=VMEM_LIMIT),
        cost_estimate=pl.CostEstimate(
            flops=2 * rows * width * columns,
            bytes_accessed=2 * (rows * width + width * columns + rows * columns),
            transcendentals=0,
        ),
        name="project",
    )(half_index, *arrays)


def first_norm_kernel(
    shares, scalars, tokens_ref, dh_ref, gain_ref, w_own_ref, w_other_ref, *refs
):
    parts = len(shares)
    out_ref, sums_ref = refs[3 * parts], refs[3 * parts + 1]
    width = tokens_ref.shape[1]
    d_own, d_other = None, None
    query_sums, value_sums = [], []
    begin = 0
    for p, share in enumerate(shares):
        dq, own_grad, back_grad = refs[3 * p : 3 * p + 3]
        for i in range(3):
            grads = dq[...] if i == 0 else both_sums(own_grad, back_grad, i - 1)
            at = i * width + begin
            part = nt(grads, w_own_ref[:, at : at + share])
            d_own = part if d_own is None else d_own + part
            part = nt(grads, w_other_ref[:, at : at + share])
            d_other = part if d_other is None else d_other + part
            if i != 1:
                sums = jnp.sum(grads.astype(F32), axis=0, keepdims=True)
                (query_sums if i == 0 else value_sums).append(sums)
        begin += share
    is_first = scalars[0] == 0
    d_norm = jnp.concatenate(
        [jnp.where(is_first, d_own, d_other), jnp.where(is_first, d_other, d_own)], axis=1
    )
    normed, inv_std = normalized(tokens_ref[...].astype(F32))
    scaled = d_norm * gain_ref[...]
    back = inv_std * (
        scaled
        - jnp.mean(scaled, axis=1, keepdims=True)
        - normed * jnp.mean(scaled * normed, axis=1, keepdims=True)
    )
    out_ref[...] = (dh_ref[...] + back).astype(BF16)
    sums = jnp.concatenate(
        [
            jnp.sum(d_norm * normed, axis=0, keepdims=True),
            jnp.sum(d_norm, axis=0, keepdims=True),
            jnp.concatenate(query_sums, axis=1),
            jnp.concatenate(value_sums, axis=1),
        ],
        axis=0,
    )

    @pl.when(pl.program_id(0) == 0)
    def _():
        sums_ref[...] = jnp.zeros_like(sums_ref)

    sums_ref[0:4, :] += sums


def first_norm(half_index, tokens, d_hidden, gain, w_own, w_other, grads, block_r=256):
    rows, width = tokens.shape
    shares = tuple(g[0].shape[1] for g in grads)
    lines = pl.BlockSpec((block_r, width), lambda i, s: (i, 0))
    weight = pl.BlockSpec((width // 2, 3 * width), lambda i, s: (0, 0))
    specs, arrays = [], []
    for three, share in zip(grads, shares):
        both = pl.BlockSpec((2, block_r, share), lambda i, s: (0, i, 0))
        specs += [pl.BlockSpec((block_r, share), lambda i, s: (i, 0)), both, both]
        arrays += list(three)
    return pl.pallas_call(
        partial(first_norm_kernel, shares),
        grid_spec=pltpu.PrefetchScalarGridSpec(
            num_scalar_prefetch=1,
            grid=(rows // block_r,),
            in_specs=[lines, lines, pl.BlockSpec((1, width), lambda i, s: (0, 0)), weight, weight]
            + specs,
            out_specs=[lines, pl.BlockSpec((LANES, width), lambda i, s: (0, 0))],
        ),
        out_shape=[
            jax.ShapeDtypeStruct((rows, width), BF16),
            jax.ShapeDtypeStruct((LANES, width), F32),
        ],
        compiler_params=pltpu.CompilerParams(vmem_limit_bytes=VMEM_LIMIT),
        cost_estimate=pl.CostEstimate(
            flops=6 * rows * width * width,
            bytes_accessed=14 * rows * width + 6 * width * width,
            transcendentals=rows,
        ),
        name="first_norm",
    )(half_index, tokens, d_hidden, gain[None, :], w_own, w_other, *arrays)


def layer_norm(values, norm_gain, norm_bias):
    center = values - jnp.mean(values, axis=-1, keepdims=True)
    inv_std = lax.rsqrt(jnp.mean(center * center, axis=-1, keepdims=True) + NORM_EPSILON)
    normed = center * inv_std
    return (normed * norm_gain + norm_bias, normed, inv_std)


def norm_backward(grad_out, normed, inv_std, norm_gain):
    scaled = grad_out * norm_gain
    return inv_std * (
        scaled
        - jnp.mean(scaled, axis=-1, keepdims=True)
        - normed * jnp.mean(scaled * normed, axis=-1, keepdims=True)
    )


def swapped(array):
    return lax.ppermute(array, "fsdp", [(0, 1), (1, 0)])


def exchanged(array):
    return lax.all_to_all(array, "expert", split_axis=0, concat_axis=0, tiled=True)


def body(
    tokens,
    out_grad,
    routes,
    prefix,
    ln1_gain,
    ln1_bias,
    w_qkv,
    q_bias,
    v_bias,
    attention_output_weight,
    attention_output_bias,
    ln2_gain,
    ln2_bias,
    w_router,
    moe_bias,
    w_in,
    w_down,
):
    experts = lax.axis_size("expert")
    my_expert = lax.axis_index("expert")
    my_half = lax.axis_index("fsdp")
    is_first = my_half == 0
    rows, width = tokens.shape[1], tokens.shape[2]
    half_width = width // 2
    slots = max(2, 2 * rows // experts) // CHUNKS
    chunk_rows = experts * slots

    def in_order(own, other, axis):
        return jnp.where(
            is_first,
            jnp.concatenate([own, other], axis=axis),
            jnp.concatenate([other, own], axis=axis),
        )

    small = jnp.concatenate(
        [
            jnp.stack(
                [
                    ln1_gain,
                    ln1_bias,
                    q_bias,
                    v_bias,
                    attention_output_bias,
                    ln2_gain,
                    ln2_bias,
                    moe_bias,
                ]
            ),
            w_router.T,
        ],
        axis=0,
    )
    small = in_order(small, swapped(small), 1)
    vectors = small[:8].astype(F32)
    norm1_gain, norm1_bias, query_bias, value_bias = (vectors[i] for i in range(4))
    output_bias, norm2_gain, norm2_bias, expert_bias = (vectors[i] for i in range(4, 8))
    router_t = small[8:]
    w_qkv_other = swapped(w_qkv)
    own_index = my_half[None].astype(jnp.int32)
    out_weight = lax.all_gather(attention_output_weight, "fsdp", axis=0, tiled=True)
    w_in_both = lax.all_gather(w_in[0], "fsdp", axis=0, tiled=False)
    w_down_both = lax.all_gather(w_down[0], "fsdp", axis=0, tiled=False)

    token_route = routes[0, :, 0]
    one_hot = token_route[:, None] == jnp.arange(experts, dtype=jnp.int32)[None, :]
    row_ids = jnp.arange(rows, dtype=jnp.int32)
    earlier_same = nn(
        (row_ids[None, :] < row_ids[:, None]).astype(BF16), one_hot.astype(BF16)
    )
    slot_index = jnp.sum(jnp.where(one_hot, earlier_same, 0.0), axis=-1).astype(jnp.int32)
    chunk_of = slot_index // slots
    place_in = token_route * slots + slot_index % slots
    buffer_ids = jnp.arange(chunk_rows, dtype=jnp.int32)

    def place_of(chunk):
        return jnp.where(chunk_of == chunk, place_in, -1)

    def picked(row_values, chunk):
        return nn(
            (buffer_ids[:, None] == place_of(chunk)[None, :]).astype(BF16), row_values
        ).astype(BF16)

    def sent(buffer):
        return exchanged(buffer.reshape(experts, slots, width)).reshape(chunk_rows, width)

    def picked_up(got):
        total = None
        for chunk in range(CHUNKS):
            part = nn((place_of(chunk)[:, None] == buffer_ids[None, :]).astype(BF16), got[chunk])
            total = part if total is None else total + part
        return total

    full_place = token_route * (CHUNKS * slots) + slot_index
    full_ids = jnp.arange(CHUNKS * chunk_rows, dtype=jnp.int32)
    cot_rows = nn((full_ids[:, None] == full_place[None, :]).astype(BF16), out_grad[0])
    cot_rows, tokens_in = lax.optimization_barrier((cot_rows.astype(BF16), tokens[0]))
    cot_rows = exchanged(cot_rows.reshape(experts, CHUNKS * slots, width)).reshape(
        experts, CHUNKS, slots, width
    )

    key_value, attn_in = project(
        own_index,
        tokens_in,
        w_qkv,
        w_qkv_other,
        jnp.concatenate([jnp.zeros_like(value_bias), value_bias]),
        vectors[0:2],
    )
    prev_key_value = lax.ppermute(key_value, "fsdp", [(0, 1)])
    queries = project(own_index, attn_in, w_qkv, w_qkv_other, query_bias)
    residual = tokens[0].astype(F32)
    scalars = jnp.stack([my_half, prefix[0] - my_half * rows]).astype(jnp.int32)
    context, lse = attention_forward(scalars, queries, prev_key_value, key_value)
    hidden = residual + (nn(context, out_weight) + output_bias)
    norm2_out, normed2, inv_std2 = layer_norm(hidden, norm2_gain, norm2_bias)
    mixed = norm2_out.astype(BF16)

    leaving = [picked(mixed, chunk) for chunk in range(CHUNKS)]
    weights = attention_weights(scalars, queries, prev_key_value, key_value, lse)
    leaving[-1], weights = lax.optimization_barrier((leaving[-1], weights))
    mixed_rows = [sent(rows_out) for rows_out in leaving]
    router_pad = jnp.pad(router_t, ((0, LANES - experts), (0, 0)))
    expert_scalars = jnp.stack([my_expert, my_half]).astype(jnp.int32)
    done, y_rows = [], None
    for c in range(CHUNKS):
        y_rows, *rest = run_expert(
            expert_scalars,
            mixed_rows[c],
            cot_rows,
            w_in_both,
            w_down_both,
            router_pad,
            y_rows,
            c,
            experts,
        )
        done.append(rest)
    d_mixed_chunks, act, du, dy, dz = ([d[i] for d in done] for i in range(5))
    back = [sent(d) for d in d_mixed_chunks]
    others = expert_weights(mixed_rows, dy, act, du, 1, None)
    back[-1], others = lax.optimization_barrier((back[-1], others))
    d_mixed = picked_up(back)
    got = [swapped(o) for o in others]
    d_router_t = None
    for c in range(CHUNKS):
        part = tn(dz[c], mixed_rows[c])
        d_router_t = part if d_router_t is None else d_router_t + part

    out_cot = out_grad[0].astype(F32)
    d_expert_bias = jnp.sum(out_cot, axis=0)
    d_norm2_gain = jnp.sum(d_mixed * normed2, axis=0)
    d_norm2_bias = jnp.sum(d_mixed, axis=0)
    d_hidden = out_cot + norm_backward(d_mixed, normed2, inv_std2, norm2_gain)
    d_attn = d_hidden.astype(BF16)
    d_output_bias = jnp.sum(d_attn.astype(F32), axis=0)
    d_context = nt(d_attn, out_weight).astype(BF16)

    logits = nt(mixed, router_t)
    router_probs = jax.nn.softmax(logits, axis=-1)
    gate_value = jnp.sum(jnp.where(one_hot, router_probs, 0.0), axis=-1)
    y_back = exchanged(y_rows.reshape(experts, CHUNKS * slots, width)).reshape(-1, width)
    early, line = d_router_t, jnp.arange(LANES, dtype=jnp.int32)[:, None]
    for i, vector in enumerate([d_expert_bias, d_norm2_gain, d_norm2_bias, d_output_bias]):
        early = early + jnp.where(line == experts + i, vector[None, :], 0.0)

    pairs = width // LANES
    groups = ((0, FIRST_PAIRS), (FIRST_PAIRS, pairs - FIRST_PAIRS))
    grads, sums = [], []
    for number, (begin, count) in enumerate(groups):
        d_query, prev_grad, own_grad = attention_backward(
            scalars,
            queries,
            prev_key_value,
            key_value,
            context,
            d_context,
            weights,
            begin,
            count,
        )
        returned = lax.ppermute(prev_grad, "fsdp", [(1, 0)])
        group = (d_query, own_grad, returned)
        grads.append(group)
        if number == 0:
            vectors_in, context_side = early, (context, d_attn)
        else:
            d_tokens, norm_sums = first_norm(
                own_index, tokens[0], d_hidden, norm1_gain, w_qkv, w_qkv_other, grads
            )
            norm_sums, sums[0] = lax.optimization_barrier((norm_sums, sums[0]))
            vectors_in, context_side = norm_sums, ()
        own_part, other_part = pair_weights(own_index, attn_in, group, vectors_in, context_side)
        own_part = (own_part.astype(F32) + swapped(other_part).astype(F32)).astype(BF16)
        blocks = own_part.reshape(experts, half_width // experts, own_part.shape[1])
        if number < len(groups) - 1:
            d_context, blocks, y_back = lax.optimization_barrier((d_context, blocks, y_back))
        sums.append(jnp.sum(exchanged(blocks).astype(F32), axis=0))
    d_w_in, d_w_down = expert_weights(mixed_rows, dy, act, du, 0, got)
    expert_value = nn((full_place[:, None] == full_ids[None, :]).astype(BF16), y_back)
    output = hidden + gate_value[:, None] * expert_value + expert_bias

    sum_qkv = jnp.concatenate(
        [
            sums[g][:, i * count * LANES : (i + 1) * count * LANES]
            for i in range(3)
            for g, (begin, count) in enumerate(groups)
        ],
        axis=1,
    )
    sum_out = sums[0][:, 3 * groups[0][1] * LANES :]
    sum_last = sums[-1][:, 3 * groups[-1][1] * LANES :]
    return (
        output.astype(BF16)[None],
        d_tokens[None],
        sum_last[:, 0],
        sum_last[:, 1],
        sum_qkv,
        sum_last[:, 2],
        sum_last[:, 3],
        sum_out[:, :width],
        sum_out[:, width + experts + 3],
        sum_out[:, width + experts + 1],
        sum_out[:, width + experts + 2],
        sum_out[:, width : width + experts],
        sum_out[:, width + experts],
        d_w_in[None],
        d_w_down[None],
    )


def solution(mesh):
    vector = P(("fsdp", "expert"))
    matrix = P(("fsdp", "expert"), None)
    tokens = P("expert", "fsdp", None)
    return jax.shard_map(
        body,
        mesh=mesh,
        in_specs=(
            tokens,
            tokens,
            tokens,
            P("expert"),
            P("fsdp"),
            P("fsdp"),
            P("fsdp", None),
            P("fsdp"),
            P("fsdp"),
            P("fsdp", None),
            P("fsdp"),
            P("fsdp"),
            P("fsdp"),
            P("fsdp", None),
            P("fsdp"),
            P("expert", None, "fsdp"),
            P("expert", "fsdp", None),
        ),
        out_specs=(
            tokens,
            tokens,
            vector,
            vector,
            matrix,
            vector,
            vector,
            matrix,
            vector,
            vector,
            vector,
            matrix,
            vector,
            P("expert", None, "fsdp"),
            P("expert", "fsdp", None),
        ),
        check_vma=False,
    )
```

```python
from functools import partial

import jax
import jax.numpy as jnp
from jax import lax
from jax.experimental import pallas as pl
from jax.experimental.pallas import tpu as pltpu
from jax.sharding import PartitionSpec as P

HEAD_DIM = 64
NORM_EPSILON = 1e-05
MASK_FILL = -1e30
LOG2E = 1.4426950408889634
SAFE_LOG2 = 90.0
GELU_A = 0.7978845608028654
GELU_B = 0.044715
CHUNKS = 2
BWD_Q = 512
BWD_K = 512
FIRST_PAIRS = 4
LANES = 128
BF16 = jnp.bfloat16
F32 = jnp.float32
VMEM_LIMIT = 56 << 20


def nn(left, right):
    return lax.dot_general(left, right, (((1,), (0,)), ((), ())), preferred_element_type=F32)


def nt(left, right):
    return lax.dot_general(left, right, (((1,), (1,)), ((), ())), preferred_element_type=F32)


def tn(left, right):
    return lax.dot_general(left, right, (((0,), (0,)), ((), ())), preferred_element_type=F32)


def lane_index(rows):
    return lax.broadcasted_iota(jnp.int32, (rows, LANES), 1)


def in_three(values):
    high = values.astype(BF16).astype(F32)
    rest = values - high
    middle = rest.astype(BF16).astype(F32)
    return high, middle, rest - middle


def three_columns(values, place):
    high, middle, low = in_three(values)
    return jnp.where(
        place == 0, high, jnp.where(place == 1, middle, jnp.where(place == 2, low, 0.0))
    )


def forward_kernel(
    block,
    scalars,
    q_ref,
    prev_k_ref,
    prev_v_ref,
    own_k_ref,
    own_v_ref,
    out_ref,
    lse_ref,
    values_one,
    query_parts,
    keys_both,
    total,
    top,
):
    rows = q_ref.shape[0]
    has_prev, own_prefix = scalars[0], scalars[1]
    lane = lane_index(rows)
    first = lane < HEAD_DIM
    zero = jnp.zeros((rows, LANES), BF16)
    one = jnp.ones((rows, LANES), BF16)
    own_values, prev_values = own_v_ref[...], prev_v_ref[...]
    values_one[0, 0] = jnp.where(first, prev_values, one)
    values_one[1, 0] = jnp.where(first, one, prev_values)
    values_one[0, 1] = jnp.where(first, own_values, one)
    values_one[1, 1] = jnp.where(first, one, own_values)
    scaled = q_ref[...].astype(F32) * LOG2E
    high = scaled.astype(BF16)
    low = (scaled - high.astype(F32)).astype(BF16)
    query_parts[0, :, :LANES] = jnp.where(first, high, zero)
    query_parts[0, :, LANES:] = jnp.where(first, low, zero)
    query_parts[1, :, :LANES] = jnp.where(first, zero, high)
    query_parts[1, :, LANES:] = jnp.where(first, zero, low)

    same_head = (
        lax.broadcasted_iota(jnp.int32, (LANES, LANES), 0) < HEAD_DIM
    ) == (lax.broadcasted_iota(jnp.int32, (LANES, LANES), 1) < HEAD_DIM)
    same_head = jnp.where(same_head, 1.0, 0.0).astype(BF16)

    def longest(ref):
        values = ref[...].astype(F32)
        return jnp.max(nn((values * values).astype(BF16), same_head), axis=0, keepdims=True)

    keys_longest = jnp.maximum(longest(own_k_ref), longest(prev_k_ref))
    small = jnp.max(longest(q_ref) * keys_longest) < (SAFE_LOG2 / LOG2E) ** 2
    keys_both[0] = prev_k_ref[...]
    keys_both[1] = own_k_ref[...]
    first_part = jnp.where(has_prev > 0, 0, 1)
    total[...] = jnp.zeros_like(total)

    def scores_of(h, keys, queries_at, size_q, part, at, size_k):
        scores = nt(query_parts[h, queries_at, :], keys)
        key_pos = at + (part - 1) * rows + lax.broadcasted_iota(jnp.int32, (1, size_k), 1)
        query_pos = queries_at.start + lax.broadcasted_iota(jnp.int32, (size_q, 1), 0)
        visible = key_pos <= jnp.maximum(query_pos, own_prefix - 1)
        return jnp.where(visible, scores, MASK_FILL)

    def keys_twice(part, at, size):
        keys = keys_both[part, pl.ds(at, size), :]
        return jnp.concatenate([keys, keys], axis=1)

    @pl.when(small)
    def _():
        top[...] = jnp.zeros_like(top)

        def add_up(part, carried):
            keys = keys_twice(part, 0, rows)
            for h in range(2):
                scores = scores_of(h, keys, pl.ds(0, rows), rows, part, 0, rows)
                total[h] += nn(jnp.exp2(scores).astype(BF16), values_one[h, part])
            return carried

        lax.fori_loop(first_part, 2, add_up, 0)

    @pl.when(jnp.logical_not(small))
    def _():
        size = block
        blocks = rows // size
        lane = lane_index(size)
        place = lane & (HEAD_DIM - 1)
        three = jnp.where(place < 3, 1.0, 0.0).astype(BF16)

        def queries_block(i, carried):
            here = pl.ds(pl.multiple_of(i * size, size), size)

            def over_keys(visit):
                def one(n, carried):
                    part = n // blocks
                    visit(part, pl.multiple_of(lax.rem(n, blocks) * size, size))
                    return carried

                lax.fori_loop(first_part * blocks, 2 * blocks, one, 0)

            for h in range(2):
                top[h, here, :] = jnp.full((size, LANES), MASK_FILL, F32)

                def find_top(part, at):
                    keys = keys_twice(part, at, size)
                    scores = scores_of(h, keys, here, size, part, at, size)
                    largest = top[h, here, :]
                    for t in range(size // LANES):
                        largest = jnp.maximum(largest, scores[:, t * LANES : (t + 1) * LANES])
                    top[h, here, :] = largest

                over_keys(find_top)
                maximum = jnp.max(top[h, here, :], axis=1, keepdims=True)
                maximum = jnp.broadcast_to(maximum, (size, LANES))
                top[h, here, :] = maximum
                mine = (lane < HEAD_DIM) == (h == 0)
                less = jnp.where(mine, three_columns(-maximum, place), 0.0).astype(BF16)

                def add_up(part, at):
                    keys = keys_twice(part, at, size)
                    scores = scores_of(h, keys, here, size, part, at, size) + nt(less, three)
                    weights = jnp.exp2(scores).astype(BF16)
                    total[h, here, :] += nn(weights, values_one[h, part, pl.ds(at, size), :])

                over_keys(add_up)
            return carried

        lax.fori_loop(0, blocks, queries_block, 0)

    sum_a, sum_b = total[0], total[1]
    weight = jnp.where(first, pltpu.roll(sum_a, HEAD_DIM, 1), pltpu.roll(sum_b, HEAD_DIM, 1))
    out_ref[...] = (jnp.where(first, sum_a, sum_b) / weight).astype(BF16)
    lse_ref[...] = jnp.where(first, top[0], top[1]) * (1.0 / LOG2E) + jnp.log(weight)


def attention_forward(scalars, queries, prev, own, block=512):
    rows, width = queries.shape
    pairs = width // LANES

    def spec(offset):
        return pl.BlockSpec((rows, LANES), lambda h, scalars: (0, h + offset))

    return pl.pallas_call(
        partial(forward_kernel, block),
        grid_spec=pltpu.PrefetchScalarGridSpec(
            num_scalar_prefetch=1,
            grid=(pairs,),
            in_specs=[spec(0), spec(0), spec(pairs), spec(0), spec(pairs)],
            out_specs=[spec(0), spec(0)],
            scratch_shapes=[
                pltpu.VMEM((2, 2, rows, LANES), BF16),
                pltpu.VMEM((2, rows, 2 * LANES), BF16),
                pltpu.VMEM((2, rows, LANES), BF16),
                pltpu.VMEM((2, rows, LANES), F32),
                pltpu.VMEM((2, rows, LANES), F32),
            ],
        ),
        out_shape=[
            jax.ShapeDtypeStruct((rows, width), BF16),
            jax.ShapeDtypeStruct((rows, width), F32),
        ],
        compiler_params=pltpu.CompilerParams(vmem_limit_bytes=VMEM_LIMIT),
        cost_estimate=pl.CostEstimate(
            flops=4 * rows * rows * width,
            bytes_accessed=16 * rows * width,
            transcendentals=rows * rows,
        ),
        name="attention_forward",
    )(scalars, queries, prev, prev, own, own)


def over_visible(has_prev, own_prefix, rows, block_q, block_k, begin, visit, end):
    query_blocks, key_blocks = rows // block_q, rows // block_k

    def one_block(j, carried):
        line = pl.multiple_of(j * block_k, block_k)
        at = line - rows
        begin()
        seen_by_all = (at < 0) | (own_prefix > at)
        first_seen = jnp.where(seen_by_all, 0, jnp.maximum(at, 0) // block_q)

        def step(i, carried):
            visit(line, pl.multiple_of(i * block_q, block_q))
            return carried

        lax.fori_loop(first_seen, query_blocks, step, 0)
        end(line)
        return carried

    lax.fori_loop(jnp.where(has_prev > 0, 0, key_blocks), 2 * key_blocks, one_block, 0)


def weights_kernel(
    block_q, block_k, scalars, q_ref, prev_k_ref, own_k_ref, lse_ref, weights_ref, query_aug, keys_both
):
    rows = q_ref.shape[0]
    has_prev, own_prefix = scalars[0], scalars[1]
    lane = lane_index(rows)
    first = lane < HEAD_DIM
    zero = jnp.zeros((rows, LANES), BF16)
    queries = q_ref[...]
    less = three_columns(-lse_ref[...], lane & (HEAD_DIM - 1)).astype(BF16)
    query_aug[0, :, :LANES] = jnp.where(first, queries, zero)
    query_aug[0, :, LANES:] = jnp.where(first, less, zero)
    query_aug[1, :, :LANES] = jnp.where(first, zero, queries)
    query_aug[1, :, LANES:] = jnp.where(first, zero, less)
    ones = jnp.where((lane_index(block_k) & (HEAD_DIM - 1)) < 3, 1.0, 0.0).astype(BF16)

    keys_both[:rows] = prev_k_ref[...]
    keys_both[rows:] = own_k_ref[...]

    def visit(line, start):
        keys_aug = jnp.concatenate([keys_both[pl.ds(line, block_k), :], ones], axis=1)
        key_pos = line - rows + lax.broadcasted_iota(jnp.int32, (block_k, 1), 0)
        query_pos = start + lax.broadcasted_iota(jnp.int32, (1, block_q), 1)
        visible = key_pos <= jnp.maximum(query_pos, own_prefix - 1)
        for h in range(2):
            scores = nt(keys_aug, query_aug[h, pl.ds(start, block_q), :]) * LOG2E
            scores = jnp.where(visible, scores, MASK_FILL)
            weights_ref[h, pl.ds(line, block_k), pl.ds(start, block_q)] = jnp.exp2(
                scores
            ).astype(BF16)

    def nothing(*unused):
        return None

    over_visible(has_prev, own_prefix, rows, block_q, block_k, nothing, visit, nothing)


def attention_weights(scalars, queries, prev, own, lse, block_q=1024, block_k=512):
    rows, width = queries.shape
    pairs = width // LANES
    spec = pl.BlockSpec((rows, LANES), lambda h, scalars: (0, h))
    return pl.pallas_call(
        partial(weights_kernel, block_q, block_k),
        grid_spec=pltpu.PrefetchScalarGridSpec(
            num_scalar_prefetch=1,
            grid=(pairs,),
            in_specs=[spec] * 4,
            out_specs=pl.BlockSpec((None, 2, 2 * rows, rows), lambda h, scalars: (h, 0, 0, 0)),
            scratch_shapes=[
                pltpu.VMEM((2, rows, 2 * LANES), BF16),
                pltpu.VMEM((2 * rows, LANES), BF16),
            ],
        ),
        out_shape=jax.ShapeDtypeStruct((pairs, 2, 2 * rows, rows), BF16),
        compiler_params=pltpu.CompilerParams(vmem_limit_bytes=VMEM_LIMIT),
        cost_estimate=pl.CostEstimate(
            flops=8 * rows * rows * width,
            bytes_accessed=4 * pairs * rows * rows * 2 + 10 * rows * width,
            transcendentals=2 * rows * rows * width // HEAD_DIM,
        ),
        name="attention_weights",
    )(scalars, queries, prev, own, lse)


def backward_kernel(
    block_q,
    block_k,
    scalars,
    q_ref,
    prev_k_ref,
    prev_v_ref,
    own_k_ref,
    own_v_ref,
    out_ref,
    grad_ref,
    weights_ref,
    dq_ref,
    prev_grad_ref,
    own_grad_ref,
    grad_aug,
    keys_turned,
    values_both,
    dq_total,
    dk_total,
    dv_total,
):
    rows = q_ref.shape[0]
    has_prev, own_prefix = scalars[0], scalars[1]
    lane = lane_index(rows)
    first = lane < HEAD_DIM
    zero = jnp.zeros((rows, LANES), BF16)
    grads = grad_ref[...]
    products = grads.astype(F32) * out_ref[...].astype(F32)
    delta_a = jnp.sum(jnp.where(first, products, 0.0), axis=1, keepdims=True)
    delta_b = jnp.sum(jnp.where(first, 0.0, products), axis=1, keepdims=True)
    less = three_columns(-jnp.where(first, delta_a, delta_b), lane & (HEAD_DIM - 1)).astype(BF16)
    grad_aug[0, :, :LANES] = jnp.where(first, grads, zero)
    grad_aug[0, :, LANES:] = jnp.where(first, less, zero)
    grad_aug[1, :, :LANES] = jnp.where(first, zero, grads)
    grad_aug[1, :, LANES:] = jnp.where(first, zero, less)
    ones = jnp.where((lane_index(block_k) & (HEAD_DIM - 1)) < 3, 1.0, 0.0).astype(BF16)
    keys_first = lane_index(block_k) < HEAD_DIM
    dq_total[...] = jnp.zeros_like(dq_total)

    keys_turned[:, :rows] = prev_k_ref[...].T
    keys_turned[:, rows:] = own_k_ref[...].T
    values_both[:rows] = prev_v_ref[...]
    values_both[rows:] = own_v_ref[...]

    def visit(line, start):
        lines, queries_at = pl.ds(line, block_k), pl.ds(start, block_q)
        values_aug = jnp.concatenate([values_both[lines, :], ones], axis=1)
        probs, d_scores = [], []
        for h in range(2):
            part = weights_ref[h, lines, queries_at]
            centered = nt(values_aug, grad_aug[h, queries_at, :])
            d_scores.append((part.astype(F32) * centered).astype(BF16))
            probs.append(part)
        here_grads, here_queries = grad_ref[queries_at, :], q_ref[queries_at, :]
        dv_total[...] += jnp.where(keys_first, nn(probs[0], here_grads), nn(probs[1], here_grads))
        dk_total[...] += jnp.where(
            keys_first, nn(d_scores[0], here_queries), nn(d_scores[1], here_queries)
        )
        for h in range(2):
            head = slice(h * HEAD_DIM, (h + 1) * HEAD_DIM)
            dq_total[head, queries_at] += nn(keys_turned[head, lines], d_scores[h])

    @pl.when(has_prev == 0)
    def _():
        prev_grad_ref[0] = zero
        prev_grad_ref[1] = zero

    def clear():
        dk_total[...] = jnp.zeros_like(dk_total)
        dv_total[...] = jnp.zeros_like(dv_total)

    def put(line):
        @pl.when(line < rows)
        def _():
            prev_grad_ref[0, pl.ds(line, block_k), :] = dk_total[...].astype(BF16)
            prev_grad_ref[1, pl.ds(line, block_k), :] = dv_total[...].astype(BF16)

        @pl.when(line >= rows)
        def _():
            at = pl.multiple_of(line - rows, block_k)
            own_grad_ref[0, pl.ds(at, block_k), :] = dk_total[...].astype(BF16)
            own_grad_ref[1, pl.ds(at, block_k), :] = dv_total[...].astype(BF16)

    over_visible(has_prev, own_prefix, rows, block_q, block_k, clear, visit, put)
    dq_ref[...] = (dq_total[...].T * (HEAD_DIM**-0.5)).astype(BF16)


def attention_backward(
    scalars, queries, prev, own, out, grads, weights, begin, count, block_q=BWD_Q, block_k=BWD_K
):
    rows, width = queries.shape
    pairs = width // LANES

    def spec(offset):
        return pl.BlockSpec((rows, LANES), lambda h, scalars: (0, h + begin + offset))

    both = pl.BlockSpec((2, rows, LANES), lambda h, scalars: (0, 0, h))
    share = count * LANES
    return pl.pallas_call(
        partial(backward_kernel, block_q, block_k),
        grid_spec=pltpu.PrefetchScalarGridSpec(
            num_scalar_prefetch=1,
            grid=(count,),
            in_specs=[spec(0), spec(0), spec(pairs), spec(0), spec(pairs), spec(0), spec(0)]
            + [pl.BlockSpec((None, 2, 2 * rows, rows), lambda h, scalars: (h + begin, 0, 0, 0))],
            out_specs=[pl.BlockSpec((rows, LANES), lambda h, scalars: (0, h)), both, both],
            scratch_shapes=[
                pltpu.VMEM((2, rows, 2 * LANES), BF16),
                pltpu.VMEM((LANES, 2 * rows), BF16),
                pltpu.VMEM((2 * rows, LANES), BF16),
                pltpu.VMEM((LANES, rows), F32),
                pltpu.VMEM((block_k, LANES), F32),
                pltpu.VMEM((block_k, LANES), F32),
            ],
        ),
        out_shape=[
            jax.ShapeDtypeStruct((rows, share), BF16),
            jax.ShapeDtypeStruct((2, rows, share), BF16),
            jax.ShapeDtypeStruct((2, rows, share), BF16),
        ],
        compiler_params=pltpu.CompilerParams(vmem_limit_bytes=VMEM_LIMIT),
        cost_estimate=pl.CostEstimate(
            flops=60 * rows * rows * share,
            bytes_accessed=26 * rows * share,
            transcendentals=2 * rows * rows * share // HEAD_DIM,
        ),
        name="attention_backward",
    )(scalars, queries, prev, prev, own, own, out, grads, weights)


def expert_kernel(
    experts,
    block_r,
    scalars,
    rows_ref,
    cot_ref,
    w_in_ref,
    w_down_ref,
    router_ref,
    y_before_ref,
    y_ref,
    dm_ref,
    act_ref,
    du_ref,
    dy_ref,
    dz_ref,
    y_total,
    dm_total,
    probs,
):
    step = pl.program_id(0)
    slots, width = cot_ref.shape[1], cot_ref.shape[2]
    sources = block_r // slots
    lane = lane_index(block_r)
    is_mine = lane == scalars[0]

    def over_rows(work):
        for b in range(rows_ref.shape[0] // block_r):
            work(slice(b * block_r, (b + 1) * block_r), slice(b * sources, (b + 1) * sources))

    def cots(source):
        return cot_ref[source].reshape(block_r, width).astype(F32)

    @pl.when(step == 0)
    def _():
        def gate(here, source):
            logits = nt(rows_ref[here, :], router_ref[...])
            logits = jnp.where(lane < experts, logits, MASK_FILL)
            spread = jnp.exp(logits - jnp.max(logits, axis=1, keepdims=True))
            part = spread / jnp.sum(spread, axis=1, keepdims=True)
            probs[here, :] = part
            mine = jnp.sum(jnp.where(is_mine, part, 0.0), axis=1, keepdims=True)
            dy_ref[here, :] = (mine * cots(source)).astype(BF16)
            y_total[here, :] = jnp.zeros((block_r, y_total.shape[1]), F32)
            dm_total[here, :] = jnp.zeros((block_r, dm_total.shape[1]), F32)

        over_rows(gate)

    def hidden_block(here, source):
        u = nn(rows_ref[here, :], w_in_ref[...])
        d_act = nt(dy_ref[here, :], w_down_ref[...])
        square = u * u
        bend = jnp.tanh(u * (GELU_A + (GELU_A * GELU_B) * square))
        half = 0.5 + 0.5 * bend
        act = (u * half).astype(BF16)
        slope = half + (0.5 * u) * (1.0 - bend * bend) * (
            GELU_A + (3.0 * GELU_A * GELU_B) * square
        )
        du = (d_act * slope).astype(BF16)
        act_ref[here, :] = act
        du_ref[here, :] = du
        y_total[here, :] += nn(act, w_down_ref[...])
        dm_total[here, :] += nt(du, w_in_ref[...])

    over_rows(hidden_block)

    @pl.when(step == pl.num_programs(0) - 1)
    def _():
        def finish(here, source):
            y = y_total[here, :].astype(BF16)
            y_ref[source] = y.reshape(sources, slots, width)
            d_gate = jnp.sum(cots(source) * y.astype(F32), axis=1, keepdims=True)
            part = probs[here, :]
            mine = jnp.sum(jnp.where(is_mine, part, 0.0), axis=1, keepdims=True)
            dz = ((d_gate * mine) * (jnp.where(is_mine, 1.0, 0.0) - part)).astype(BF16)
            dz = jnp.where(lane < experts, dz, jnp.zeros_like(dz))
            dz_ref[here, :] = dz
            dm_ref[here, :] = (dm_total[here, :] + nn(dz, router_ref[...])).astype(BF16)

        over_rows(finish)


def run_expert(
    scalars, rows_in, cots, w_in, w_down, router, y_before, chunk, experts, block_h=512, block_r=1024
):
    rows, width = rows_in.shape
    half = w_in.shape[2]
    per_half = half // block_h
    whole = pl.BlockSpec((rows, width), lambda j, s: (0, 0))
    hidden = pl.BlockSpec((rows, block_h), lambda j, s: (0, j))
    mine = pl.BlockSpec(
        (cots.shape[0], None, cots.shape[2], width), lambda j, s: (0, chunk, 0, 0)
    )

    def which(j, s):
        return lax.rem(j // per_half + s[1], 2)

    first = y_before is None
    return pl.pallas_call(
        partial(expert_kernel, experts, block_r),
        grid_spec=pltpu.PrefetchScalarGridSpec(
            num_scalar_prefetch=1,
            grid=(2 * per_half,),
            in_specs=[
                whole,
                mine,
                pl.BlockSpec(
                    (None, width, block_h), lambda j, s: (which(j, s), 0, lax.rem(j, per_half))
                ),
                pl.BlockSpec(
                    (None, block_h, width), lambda j, s: (which(j, s), lax.rem(j, per_half), 0)
                ),
                pl.BlockSpec((LANES, width), lambda j, s: (0, 0)),
                pl.BlockSpec(memory_space=pl.ANY),
            ],
            out_specs=[
                mine,
                whole,
                hidden,
                hidden,
                whole,
                pl.BlockSpec((rows, LANES), lambda j, s: (0, 0)),
            ],
            scratch_shapes=[
                pltpu.VMEM((rows, width), F32),
                pltpu.VMEM((rows, width), F32),
                pltpu.VMEM((rows, LANES), F32),
            ],
        ),
        out_shape=[
            jax.ShapeDtypeStruct(cots.shape, BF16),
            jax.ShapeDtypeStruct((rows, width), BF16),
            jax.ShapeDtypeStruct((rows, 2 * half), BF16),
            jax.ShapeDtypeStruct((rows, 2 * half), BF16),
            jax.ShapeDtypeStruct((rows, width), BF16),
            jax.ShapeDtypeStruct((rows, LANES), BF16),
        ],
        input_output_aliases={} if first else {6: 0},
        compiler_params=pltpu.CompilerParams(vmem_limit_bytes=VMEM_LIMIT),
        cost_estimate=pl.CostEstimate(
            flops=16 * rows * width * half,
            bytes_accessed=8 * width * half + 12 * rows * width + 8 * rows * half,
            transcendentals=2 * rows * half,
        ),
        name="expert_rows",
    )(scalars, rows_in, cots, w_in, w_down, router, scalars if first else y_before)


def expert_weights_kernel(chunks, add, *refs):
    rows_refs, dy_refs, act_refs, du_refs = (
        refs[i * chunks : (i + 1) * chunks] for i in range(4)
    )
    rest = refs[4 * chunks :]
    d_in_ref, d_down_ref, turned = rest[-3:]
    rows = rows_refs[0].shape[0]

    @pl.when(pl.program_id(0) == 0)
    def _():
        for c in range(chunks):
            turned[:, c * rows : (c + 1) * rows] = rows_refs[c][...].T

    d_in, d_down = None, None
    for c in range(chunks):
        part = nn(turned[:, c * rows : (c + 1) * rows], du_refs[c][...])
        d_in = part if d_in is None else d_in + part
        part = tn(act_refs[c][...], dy_refs[c][...])
        d_down = part if d_down is None else d_down + part
    if add:
        d_in = d_in + rest[0][...].astype(F32)
        d_down = d_down + rest[1][...].astype(F32)
    d_in_ref[...] = d_in.astype(d_in_ref.dtype)
    d_down_ref[...] = d_down.astype(d_down_ref.dtype)


def expert_weights(rows_in, dy, act, du, half_index, got, block_h=512):
    chunks = len(rows_in)
    rows, width = rows_in[0].shape
    half = du[0].shape[1] // 2
    steps = half // block_h
    whole = pl.BlockSpec((rows, width), lambda j: (0, 0))
    hidden = pl.BlockSpec((rows, block_h), lambda j: (0, j + half_index * steps))
    columns = pl.BlockSpec((width, block_h), lambda j: (0, j))
    lines = pl.BlockSpec((block_h, width), lambda j: (j, 0))
    dtype = BF16 if got is None else F32
    extra = () if got is None else tuple(got)
    return pl.pallas_call(
        partial(expert_weights_kernel, chunks, got is not None),
        grid=(steps,),
        in_specs=[whole] * (2 * chunks) + [hidden] * (2 * chunks) + [columns, lines][: len(extra)],
        out_specs=[columns, lines],
        out_shape=[
            jax.ShapeDtypeStruct((width, half), dtype),
            jax.ShapeDtypeStruct((half, width), dtype),
        ],
        scratch_shapes=[pltpu.VMEM((width, chunks * rows), BF16)],
        compiler_params=pltpu.CompilerParams(vmem_limit_bytes=VMEM_LIMIT),
        cost_estimate=pl.CostEstimate(
            flops=4 * chunks * rows * width * half,
            bytes_accessed=4 * chunks * rows * (width + half) + 8 * width * half,
            transcendentals=0,
        ),
        name="expert_weights",
    )(*rows_in, *dy, *act, *du, *extra)


def both_sums(own_ref, back_ref, i):
    return (own_ref[i].astype(F32) + back_ref[i].astype(F32)).astype(BF16)


def pair_weights_kernel(with_context, scalars, *refs):
    in_ref, dq_ref, own_ref, back_ref, vectors_ref = refs[:5]
    outs = refs[-2:]
    is_first = scalars[0] == 0
    half = outs[0].shape[0]
    column = 0

    def put(top, bottom):
        nonlocal column
        here = slice(column, column + top.shape[1])
        column += top.shape[1]
        top, bottom = top.astype(BF16), bottom.astype(BF16)
        outs[0][:, here] = jnp.where(is_first, top, bottom)
        outs[1][:, here] = jnp.where(is_first, bottom, top)

    def products(left, rights):
        turned = left[...].T
        for right in rights:
            put(nn(turned[:half], right), nn(turned[half:], right))

    products(in_ref, [dq_ref[...]] + [both_sums(own_ref, back_ref, i) for i in range(2)])
    if with_context:
        products(refs[5], [refs[6][...]])
    turned = vectors_ref[...].T
    put(turned[:half], turned[half:])


def pair_weights(half_index, attn_in, grads, vectors, context_side=()):
    d_query, own_grad, back_grad = grads
    rows, width = attn_in.shape
    columns = 3 * d_query.shape[1] + vectors.shape[0]
    if context_side:
        columns += context_side[1].shape[1]

    def full(shape):
        return pl.BlockSpec(shape, lambda i, s: (0,) * len(shape))

    arrays = [attn_in, d_query, own_grad, back_grad, vectors] + list(context_side)
    out = full((width // 2, columns))
    return pl.pallas_call(
        partial(pair_weights_kernel, bool(context_side)),
        grid_spec=pltpu.PrefetchScalarGridSpec(
            num_scalar_prefetch=1,
            grid=(1,),
            in_specs=[full(x.shape) for x in arrays],
            out_specs=[out, out],
        ),
        out_shape=[jax.ShapeDtypeStruct((width // 2, columns), BF16)] * 2,
        compiler_params=pltpu.CompilerParams(vmem_limit_bytes=VMEM_LIMIT),
        cost_estimate=pl.CostEstimate(
            flops=2 * rows * width * columns,
            bytes_accessed=4 * (rows + width) * columns,
            transcendentals=0,
        ),
        name="pair_weights",
    )(half_index, *arrays)


def normalized(values):
    center = values - jnp.mean(values, axis=1, keepdims=True)
    inv_std = lax.rsqrt(jnp.mean(center * center, axis=1, keepdims=True) + NORM_EPSILON)
    return center * inv_std, inv_std


def rows_in_order(is_first, own_ref, other_ref):
    own, other = own_ref[...], other_ref[...]
    return jnp.concatenate(
        [jnp.where(is_first, own, other), jnp.where(is_first, other, own)], axis=0
    )


def key_value_kernel(scalars, tokens_ref, norm_ref, own_ref, other_ref, add_ref, out_ref, in_ref):
    @pl.when(pl.program_id(0) == 0)
    def _():
        normed, inv_std = normalized(tokens_ref[...].astype(F32))
        in_ref[...] = (normed * norm_ref[0:1, :] + norm_ref[1:2, :]).astype(BF16)

    weight = rows_in_order(scalars[0] == 0, own_ref, other_ref)
    out_ref[...] = (nn(in_ref[...], weight) + add_ref[...]).astype(BF16)


def query_kernel(scalars, in_ref, own_ref, other_ref, add_ref, out_ref):
    weight = rows_in_order(scalars[0] == 0, own_ref, other_ref)
    out_ref[...] = ((nn(in_ref[...], weight) + add_ref[...]) * (HEAD_DIM**-0.5)).astype(BF16)


def project(half_index, rows_in, w_own, w_other, bias, norm=None, block_n=512):
    rows, width = rows_in.shape
    columns = bias.shape[0]
    begin = 0 if norm is None else width // block_n
    half = pl.BlockSpec((width // 2, block_n), lambda j, s: (0, begin + j))
    whole = pl.BlockSpec((rows, width), lambda j, s: (0, 0))
    line = pl.BlockSpec((1, block_n), lambda j, s: (0, j))
    block = pl.BlockSpec((rows, block_n), lambda j, s: (0, j))
    shape = jax.ShapeDtypeStruct((rows, columns), BF16)
    if norm is None:
        in_specs, out_specs, out_shape = [whole, half, half, line], block, shape
        arrays = (rows_in, w_own, w_other, bias[None, :])
    else:
        in_specs = [whole, pl.BlockSpec((2, width), lambda j, s: (0, 0)), half, half, line]
        out_specs = [block, whole]
        out_shape = [shape, jax.ShapeDtypeStruct((rows, width), BF16)]
        arrays = (rows_in, norm, w_own, w_other, bias[None, :])
    return pl.pallas_call(
        query_kernel if norm is None else key_value_kernel,
        grid_spec=pltpu.PrefetchScalarGridSpec(
            num_scalar_prefetch=1,
            grid=(columns // block_n,),
            in_specs=in_specs,
            out_specs=out_specs,
        ),
        out_shape=out_shape,
        compiler_params=pltpu.CompilerParams(vmem_limit_bytes=VMEM_LIMIT),
        cost_estimate=pl.CostEstimate(
            flops=2 * rows * width * columns,
            bytes_accessed=2 * (rows * width + width * columns + rows * columns),
            transcendentals=0,
        ),
        name="project",
    )(half_index, *arrays)


def first_norm_kernel(
    shares, scalars, tokens_ref, dh_ref, gain_ref, w_own_ref, w_other_ref, *refs
):
    parts = len(shares)
    out_ref, sums_ref = refs[3 * parts], refs[3 * parts + 1]
    width = tokens_ref.shape[1]
    d_own, d_other = None, None
    query_sums, value_sums = [], []
    begin = 0
    for p, share in enumerate(shares):
        dq, own_grad, back_grad = refs[3 * p : 3 * p + 3]
        for i in range(3):
            grads = dq[...] if i == 0 else both_sums(own_grad, back_grad, i - 1)
            at = i * width + begin
            part = nt(grads, w_own_ref[:, at : at + share])
            d_own = part if d_own is None else d_own + part
            part = nt(grads, w_other_ref[:, at : at + share])
            d_other = part if d_other is None else d_other + part
            if i != 1:
                sums = jnp.sum(grads.astype(F32), axis=0, keepdims=True)
                (query_sums if i == 0 else value_sums).append(sums)
        begin += share
    is_first = scalars[0] == 0
    d_norm = jnp.concatenate(
        [jnp.where(is_first, d_own, d_other), jnp.where(is_first, d_other, d_own)], axis=1
    )
    normed, inv_std = normalized(tokens_ref[...].astype(F32))
    scaled = d_norm * gain_ref[...]
    back = inv_std * (
        scaled
        - jnp.mean(scaled, axis=1, keepdims=True)
        - normed * jnp.mean(scaled * normed, axis=1, keepdims=True)
    )
    out_ref[...] = (dh_ref[...] + back).astype(BF16)
    sums = jnp.concatenate(
        [
            jnp.sum(d_norm * normed, axis=0, keepdims=True),
            jnp.sum(d_norm, axis=0, keepdims=True),
            jnp.concatenate(query_sums, axis=1),
            jnp.concatenate(value_sums, axis=1),
        ],
        axis=0,
    )

    @pl.when(pl.program_id(0) == 0)
    def _():
        sums_ref[...] = jnp.zeros_like(sums_ref)

    sums_ref[0:4, :] += sums


def first_norm(half_index, tokens, d_hidden, gain, w_own, w_other, grads, block_r=256):
    rows, width = tokens.shape
    shares = tuple(g[0].shape[1] for g in grads)
    lines = pl.BlockSpec((block_r, width), lambda i, s: (i, 0))
    weight = pl.BlockSpec((width // 2, 3 * width), lambda i, s: (0, 0))
    specs, arrays = [], []
    for three, share in zip(grads, shares):
        both = pl.BlockSpec((2, block_r, share), lambda i, s: (0, i, 0))
        specs += [pl.BlockSpec((block_r, share), lambda i, s: (i, 0)), both, both]
        arrays += list(three)
    return pl.pallas_call(
        partial(first_norm_kernel, shares),
        grid_spec=pltpu.PrefetchScalarGridSpec(
            num_scalar_prefetch=1,
            grid=(rows // block_r,),
            in_specs=[lines, lines, pl.BlockSpec((1, width), lambda i, s: (0, 0)), weight, weight]
            + specs,
            out_specs=[lines, pl.BlockSpec((LANES, width), lambda i, s: (0, 0))],
        ),
        out_shape=[
            jax.ShapeDtypeStruct((rows, width), BF16),
            jax.ShapeDtypeStruct((LANES, width), F32),
        ],
        compiler_params=pltpu.CompilerParams(vmem_limit_bytes=VMEM_LIMIT),
        cost_estimate=pl.CostEstimate(
            flops=6 * rows * width * width,
            bytes_accessed=14 * rows * width + 6 * width * width,
            transcendentals=rows,
        ),
        name="first_norm",
    )(half_index, tokens, d_hidden, gain[None, :], w_own, w_other, *arrays)


def layer_norm(values, norm_gain, norm_bias):
    center = values - jnp.mean(values, axis=-1, keepdims=True)
    inv_std = lax.rsqrt(jnp.mean(center * center, axis=-1, keepdims=True) + NORM_EPSILON)
    normed = center * inv_std
    return (normed * norm_gain + norm_bias, normed, inv_std)


def norm_backward(grad_out, normed, inv_std, norm_gain):
    scaled = grad_out * norm_gain
    return inv_std * (
        scaled
        - jnp.mean(scaled, axis=-1, keepdims=True)
        - normed * jnp.mean(scaled * normed, axis=-1, keepdims=True)
    )


def swapped(array):
    return lax.ppermute(array, "fsdp", [(0, 1), (1, 0)])


def exchanged(array):
    return lax.all_to_all(array, "expert", split_axis=0, concat_axis=0, tiled=True)


def body(
    tokens,
    out_grad,
    routes,
    prefix,
    ln1_gain,
    ln1_bias,
    w_qkv,
    q_bias,
    v_bias,
    attention_output_weight,
    attention_output_bias,
    ln2_gain,
    ln2_bias,
    w_router,
    moe_bias,
    w_in,
    w_down,
):
    experts = lax.axis_size("expert")
    my_expert = lax.axis_index("expert")
    my_half = lax.axis_index("fsdp")
    is_first = my_half == 0
    rows, width = tokens.shape[1], tokens.shape[2]
    half_width = width // 2
    slots = max(2, 2 * rows // experts) // CHUNKS
    chunk_rows = experts * slots

    def in_order(own, other, axis):
        return jnp.where(
            is_first,
            jnp.concatenate([own, other], axis=axis),
            jnp.concatenate([other, own], axis=axis),
        )

    small = jnp.concatenate(
        [
            jnp.stack(
                [
                    ln1_gain,
                    ln1_bias,
                    q_bias,
                    v_bias,
                    attention_output_bias,
                    ln2_gain,
                    ln2_bias,
                    moe_bias,
                ]
            ),
            w_router.T,
        ],
        axis=0,
    )
    small = in_order(small, swapped(small), 1)
    vectors = small[:8].astype(F32)
    norm1_gain, norm1_bias, query_bias, value_bias = (vectors[i] for i in range(4))
    output_bias, norm2_gain, norm2_bias, expert_bias = (vectors[i] for i in range(4, 8))
    router_t = small[8:]
    w_qkv_other = swapped(w_qkv)
    own_index = my_half[None].astype(jnp.int32)
    out_weight = lax.all_gather(attention_output_weight, "fsdp", axis=0, tiled=True)
    w_in_both = lax.all_gather(w_in[0], "fsdp", axis=0, tiled=False)
    w_down_both = lax.all_gather(w_down[0], "fsdp", axis=0, tiled=False)

    token_route = routes[0, :, 0]
    one_hot = token_route[:, None] == jnp.arange(experts, dtype=jnp.int32)[None, :]
    row_ids = jnp.arange(rows, dtype=jnp.int32)
    earlier_same = nn(
        (row_ids[None, :] < row_ids[:, None]).astype(BF16), one_hot.astype(BF16)
    )
    slot_index = jnp.sum(jnp.where(one_hot, earlier_same, 0.0), axis=-1).astype(jnp.int32)
    chunk_of = slot_index // slots
    place_in = token_route * slots + slot_index % slots
    buffer_ids = jnp.arange(chunk_rows, dtype=jnp.int32)

    def place_of(chunk):
        return jnp.where(chunk_of == chunk, place_in, -1)

    def picked(row_values, chunk):
        return nn(
            (buffer_ids[:, None] == place_of(chunk)[None, :]).astype(BF16), row_values
        ).astype(BF16)

    def sent(buffer):
        return exchanged(buffer.reshape(experts, slots, width)).reshape(chunk_rows, width)

    def picked_up(got):
        total = None
        for chunk in range(CHUNKS):
            part = nn((place_of(chunk)[:, None] == buffer_ids[None, :]).astype(BF16), got[chunk])
            total = part if total is None else total + part
        return total

    full_place = token_route * (CHUNKS * slots) + slot_index
    full_ids = jnp.arange(CHUNKS * chunk_rows, dtype=jnp.int32)
    cot_rows = nn((full_ids[:, None] == full_place[None, :]).astype(BF16), out_grad[0])
    cot_rows, tokens_in = lax.optimization_barrier((cot_rows.astype(BF16), tokens[0]))
    cot_rows = exchanged(cot_rows.reshape(experts, CHUNKS * slots, width)).reshape(
        experts, CHUNKS, slots, width
    )

    key_value, attn_in = project(
        own_index,
        tokens_in,
        w_qkv,
        w_qkv_other,
        jnp.concatenate([jnp.zeros_like(value_bias), value_bias]),
        vectors[0:2],
    )
    prev_key_value = lax.ppermute(key_value, "fsdp", [(0, 1)])
    queries = project(own_index, attn_in, w_qkv, w_qkv_other, query_bias)
    residual = tokens[0].astype(F32)
    scalars = jnp.stack([my_half, prefix[0] - my_half * rows]).astype(jnp.int32)
    context, lse = attention_forward(scalars, queries, prev_key_value, key_value)
    hidden = residual + (nn(context, out_weight) + output_bias)
    norm2_out, normed2, inv_std2 = layer_norm(hidden, norm2_gain, norm2_bias)
    mixed = norm2_out.astype(BF16)

    leaving = [picked(mixed, chunk) for chunk in range(CHUNKS)]
    weights = attention_weights(scalars, queries, prev_key_value, key_value, lse)
    leaving[-1], weights = lax.optimization_barrier((leaving[-1], weights))
    mixed_rows = [sent(rows_out) for rows_out in leaving]
    router_pad = jnp.pad(router_t, ((0, LANES - experts), (0, 0)))
    expert_scalars = jnp.stack([my_expert, my_half]).astype(jnp.int32)
    done, y_rows = [], None
    for c in range(CHUNKS):
        y_rows, *rest = run_expert(
            expert_scalars,
            mixed_rows[c],
            cot_rows,
            w_in_both,
            w_down_both,
            router_pad,
            y_rows,
            c,
            experts,
        )
        done.append(rest)
    d_mixed_chunks, act, du, dy, dz = ([d[i] for d in done] for i in range(5))
    back = [sent(d) for d in d_mixed_chunks]
    others = expert_weights(mixed_rows, dy, act, du, 1, None)
    d_router_t = None
    for c in range(CHUNKS):
        part = tn(dz[c], mixed_rows[c])
        d_router_t = part if d_router_t is None else d_router_t + part
    d_expert_bias = jnp.sum(out_grad[0].astype(F32), axis=0)
    back[-1], others, d_router_t, d_expert_bias = lax.optimization_barrier(
        (back[-1], others, d_router_t, d_expert_bias)
    )
    d_mixed = picked_up(back)
    got = [swapped(o) for o in others]
    out_cot = out_grad[0].astype(F32)
    d_norm2_gain = jnp.sum(d_mixed * normed2, axis=0)
    d_norm2_bias = jnp.sum(d_mixed, axis=0)
    d_hidden = out_cot + norm_backward(d_mixed, normed2, inv_std2, norm2_gain)
    d_attn = d_hidden.astype(BF16)
    d_output_bias = jnp.sum(d_attn.astype(F32), axis=0)
    d_context = nt(d_attn, out_weight).astype(BF16)

    logits = nt(mixed, router_t)
    router_probs = jax.nn.softmax(logits, axis=-1)
    gate_value = jnp.sum(jnp.where(one_hot, router_probs, 0.0), axis=-1)
    y_back = exchanged(y_rows.reshape(experts, CHUNKS * slots, width)).reshape(-1, width)
    early, line = d_router_t, jnp.arange(LANES, dtype=jnp.int32)[:, None]
    for i, vector in enumerate([d_expert_bias, d_norm2_gain, d_norm2_bias, d_output_bias]):
        early = early + jnp.where(line == experts + i, vector[None, :], 0.0)

    pairs = width // LANES
    groups = ((0, FIRST_PAIRS), (FIRST_PAIRS, pairs - FIRST_PAIRS))
    grads, sums = [], []
    for number, (begin, count) in enumerate(groups):
        d_query, prev_grad, own_grad = attention_backward(
            scalars,
            queries,
            prev_key_value,
            key_value,
            context,
            d_context,
            weights,
            begin,
            count,
        )
        returned = lax.ppermute(prev_grad, "fsdp", [(1, 0)])
        group = (d_query, own_grad, returned)
        grads.append(group)
        if number == 0:
            vectors_in, context_side = early, (context, d_attn)
        else:
            d_tokens, norm_sums = first_norm(
                own_index, tokens[0], d_hidden, norm1_gain, w_qkv, w_qkv_other, grads
            )
            norm_sums, sums[0] = lax.optimization_barrier((norm_sums, sums[0]))
            vectors_in, context_side = norm_sums, ()
        own_part, other_part = pair_weights(own_index, attn_in, group, vectors_in, context_side)
        own_part = (own_part.astype(F32) + swapped(other_part).astype(F32)).astype(BF16)
        blocks = own_part.reshape(experts, half_width // experts, own_part.shape[1])
        if number < len(groups) - 1:
            d_context, blocks, y_back = lax.optimization_barrier((d_context, blocks, y_back))
        sums.append(jnp.sum(exchanged(blocks).astype(F32), axis=0))
    d_w_in, d_w_down = expert_weights(mixed_rows, dy, act, du, 0, got)
    expert_value = nn((full_place[:, None] == full_ids[None, :]).astype(BF16), y_back)
    output = hidden + gate_value[:, None] * expert_value + expert_bias

    sum_qkv = jnp.concatenate(
        [
            sums[g][:, i * count * LANES : (i + 1) * count * LANES]
            for i in range(3)
            for g, (begin, count) in enumerate(groups)
        ],
        axis=1,
    )
    sum_out = sums[0][:, 3 * groups[0][1] * LANES :]
    sum_last = sums[-1][:, 3 * groups[-1][1] * LANES :]
    return (
        output.astype(BF16)[None],
        d_tokens[None],
        sum_last[:, 0],
        sum_last[:, 1],
        sum_qkv,
        sum_last[:, 2],
        sum_last[:, 3],
        sum_out[:, :width],
        sum_out[:, width + experts + 3],
        sum_out[:, width + experts + 1],
        sum_out[:, width + experts + 2],
        sum_out[:, width : width + experts],
        sum_out[:, width + experts],
        d_w_in[None],
        d_w_down[None],
    )


def solution(mesh):
    vector = P(("fsdp", "expert"))
    matrix = P(("fsdp", "expert"), None)
    tokens = P("expert", "fsdp", None)
    return jax.shard_map(
        body,
        mesh=mesh,
        in_specs=(
            tokens,
            tokens,
            tokens,
            P("expert"),
            P("fsdp"),
            P("fsdp"),
            P("fsdp", None),
            P("fsdp"),
            P("fsdp"),
            P("fsdp", None),
            P("fsdp"),
            P("fsdp"),
            P("fsdp"),
            P("fsdp", None),
            P("fsdp"),
            P("expert", None, "fsdp"),
            P("expert", "fsdp", None),
        ),
        out_specs=(
            tokens,
            tokens,
            vector,
            vector,
            matrix,
            vector,
            vector,
            matrix,
            vector,
            vector,
            vector,
            matrix,
            vector,
            P("expert", None, "fsdp"),
            P("expert", "fsdp", None),
        ),
        check_vma=False,
    )
```

```python
from functools import partial

import jax
import jax.numpy as jnp
from jax import lax
from jax.experimental import pallas as pl
from jax.experimental.pallas import tpu as pltpu
from jax.sharding import PartitionSpec as P

HEAD_DIM = 64
NORM_EPSILON = 1e-05
MASK_FILL = -1e30
LOG2E = 1.4426950408889634
SAFE_LOG2 = 90.0
GELU_A = 0.7978845608028654
GELU_B = 0.044715
CHUNKS = 2
BWD_Q = 512
BWD_K = 512
FIRST_PAIRS = 4
LANES = 128
BF16 = jnp.bfloat16
F32 = jnp.float32
VMEM_LIMIT = 56 << 20


def nn(left, right):
    return lax.dot_general(left, right, (((1,), (0,)), ((), ())), preferred_element_type=F32)


def nt(left, right):
    return lax.dot_general(left, right, (((1,), (1,)), ((), ())), preferred_element_type=F32)


def tn(left, right):
    return lax.dot_general(left, right, (((0,), (0,)), ((), ())), preferred_element_type=F32)


def lane_index(rows):
    return lax.broadcasted_iota(jnp.int32, (rows, LANES), 1)


def in_three(values):
    high = values.astype(BF16).astype(F32)
    rest = values - high
    middle = rest.astype(BF16).astype(F32)
    return high, middle, rest - middle


def three_columns(values, place):
    high, middle, low = in_three(values)
    return jnp.where(
        place == 0, high, jnp.where(place == 1, middle, jnp.where(place == 2, low, 0.0))
    )


def forward_kernel(
    block,
    scalars,
    q_ref,
    prev_k_ref,
    prev_v_ref,
    own_k_ref,
    own_v_ref,
    out_ref,
    lse_ref,
    values_one,
    query_parts,
    keys_both,
    total,
    top,
):
    rows = q_ref.shape[0]
    has_prev, own_prefix = scalars[0], scalars[1]
    lane = lane_index(rows)
    first = lane < HEAD_DIM
    zero = jnp.zeros((rows, LANES), BF16)
    one = jnp.ones((rows, LANES), BF16)
    own_values, prev_values = own_v_ref[...], prev_v_ref[...]
    values_one[0, 0] = jnp.where(first, prev_values, one)
    values_one[1, 0] = jnp.where(first, one, prev_values)
    values_one[0, 1] = jnp.where(first, own_values, one)
    values_one[1, 1] = jnp.where(first, one, own_values)
    scaled = q_ref[...].astype(F32) * LOG2E
    high = scaled.astype(BF16)
    low = (scaled - high.astype(F32)).astype(BF16)
    query_parts[0, :, :LANES] = jnp.where(first, high, zero)
    query_parts[0, :, LANES:] = jnp.where(first, low, zero)
    query_parts[1, :, :LANES] = jnp.where(first, zero, high)
    query_parts[1, :, LANES:] = jnp.where(first, zero, low)

    same_head = (
        lax.broadcasted_iota(jnp.int32, (LANES, LANES), 0) < HEAD_DIM
    ) == (lax.broadcasted_iota(jnp.int32, (LANES, LANES), 1) < HEAD_DIM)
    same_head = jnp.where(same_head, 1.0, 0.0).astype(BF16)

    def longest(ref):
        values = ref[...].astype(F32)
        return jnp.max(nn((values * values).astype(BF16), same_head), axis=0, keepdims=True)

    keys_longest = jnp.maximum(longest(own_k_ref), longest(prev_k_ref))
    small = jnp.max(longest(q_ref) * keys_longest) < (SAFE_LOG2 / LOG2E) ** 2
    keys_both[0] = prev_k_ref[...]
    keys_both[1] = own_k_ref[...]
    first_part = jnp.where(has_prev > 0, 0, 1)
    total[...] = jnp.zeros_like(total)

    def scores_of(h, keys, queries_at, size_q, part, at, size_k):
        scores = nt(query_parts[h, queries_at, :], keys)
        key_pos = at + (part - 1) * rows + lax.broadcasted_iota(jnp.int32, (1, size_k), 1)
        query_pos = queries_at.start + lax.broadcasted_iota(jnp.int32, (size_q, 1), 0)
        visible = key_pos <= jnp.maximum(query_pos, own_prefix - 1)
        return jnp.where(visible, scores, MASK_FILL)

    def keys_twice(part, at, size):
        keys = keys_both[part, pl.ds(at, size), :]
        return jnp.concatenate([keys, keys], axis=1)

    @pl.when(small)
    def _():
        top[...] = jnp.zeros_like(top)

        def add_up(part, carried):
            keys = keys_twice(part, 0, rows)
            for h in range(2):
                scores = scores_of(h, keys, pl.ds(0, rows), rows, part, 0, rows)
                total[h] += nn(jnp.exp2(scores).astype(BF16), values_one[h, part])
            return carried

        lax.fori_loop(first_part, 2, add_up, 0)

    @pl.when(jnp.logical_not(small))
    def _():
        size = block
        blocks = rows // size
        lane = lane_index(size)
        place = lane & (HEAD_DIM - 1)
        three = jnp.where(place < 3, 1.0, 0.0).astype(BF16)

        def queries_block(i, carried):
            here = pl.ds(pl.multiple_of(i * size, size), size)

            def over_keys(visit):
                def one(n, carried):
                    part = n // blocks
                    visit(part, pl.multiple_of(lax.rem(n, blocks) * size, size))
                    return carried

                lax.fori_loop(first_part * blocks, 2 * blocks, one, 0)

            for h in range(2):
                top[h, here, :] = jnp.full((size, LANES), MASK_FILL, F32)

                def find_top(part, at):
                    keys = keys_twice(part, at, size)
                    scores = scores_of(h, keys, here, size, part, at, size)
                    largest = top[h, here, :]
                    for t in range(size // LANES):
                        largest = jnp.maximum(largest, scores[:, t * LANES : (t + 1) * LANES])
                    top[h, here, :] = largest

                over_keys(find_top)
                maximum = jnp.max(top[h, here, :], axis=1, keepdims=True)
                maximum = jnp.broadcast_to(maximum, (size, LANES))
                top[h, here, :] = maximum
                mine = (lane < HEAD_DIM) == (h == 0)
                less = jnp.where(mine, three_columns(-maximum, place), 0.0).astype(BF16)

                def add_up(part, at):
                    keys = keys_twice(part, at, size)
                    scores = scores_of(h, keys, here, size, part, at, size) + nt(less, three)
                    weights = jnp.exp2(scores).astype(BF16)
                    total[h, here, :] += nn(weights, values_one[h, part, pl.ds(at, size), :])

                over_keys(add_up)
            return carried

        lax.fori_loop(0, blocks, queries_block, 0)

    sum_a, sum_b = total[0], total[1]
    weight = jnp.where(first, pltpu.roll(sum_a, HEAD_DIM, 1), pltpu.roll(sum_b, HEAD_DIM, 1))
    out_ref[...] = (jnp.where(first, sum_a, sum_b) / weight).astype(BF16)
    lse_ref[...] = jnp.where(first, top[0], top[1]) * (1.0 / LOG2E) + jnp.log(weight)


def attention_forward(scalars, queries, prev, own, block=512):
    rows, width = queries.shape
    pairs = width // LANES

    def spec(offset):
        return pl.BlockSpec((rows, LANES), lambda h, scalars: (0, h + offset))

    return pl.pallas_call(
        partial(forward_kernel, block),
        grid_spec=pltpu.PrefetchScalarGridSpec(
            num_scalar_prefetch=1,
            grid=(pairs,),
            in_specs=[spec(0), spec(0), spec(pairs), spec(0), spec(pairs)],
            out_specs=[spec(0), spec(0)],
            scratch_shapes=[
                pltpu.VMEM((2, 2, rows, LANES), BF16),
                pltpu.VMEM((2, rows, 2 * LANES), BF16),
                pltpu.VMEM((2, rows, LANES), BF16),
                pltpu.VMEM((2, rows, LANES), F32),
                pltpu.VMEM((2, rows, LANES), F32),
            ],
        ),
        out_shape=[
            jax.ShapeDtypeStruct((rows, width), BF16),
            jax.ShapeDtypeStruct((rows, width), F32),
        ],
        compiler_params=pltpu.CompilerParams(vmem_limit_bytes=VMEM_LIMIT),
        cost_estimate=pl.CostEstimate(
            flops=4 * rows * rows * width,
            bytes_accessed=16 * rows * width,
            transcendentals=rows * rows,
        ),
        name="attention_forward",
    )(scalars, queries, prev, prev, own, own)


def over_visible(has_prev, own_prefix, rows, block_q, block_k, begin, visit, end):
    query_blocks, key_blocks = rows // block_q, rows // block_k

    def one_block(j, carried):
        line = pl.multiple_of(j * block_k, block_k)
        at = line - rows
        begin()
        seen_by_all = (at < 0) | (own_prefix > at)
        first_seen = jnp.where(seen_by_all, 0, jnp.maximum(at, 0) // block_q)

        def step(i, carried):
            visit(line, pl.multiple_of(i * block_q, block_q))
            return carried

        lax.fori_loop(first_seen, query_blocks, step, 0)
        end(line)
        return carried

    lax.fori_loop(jnp.where(has_prev > 0, 0, key_blocks), 2 * key_blocks, one_block, 0)


def weights_kernel(
    block_q, block_k, scalars, q_ref, prev_k_ref, own_k_ref, lse_ref, weights_ref, query_aug, keys_both
):
    rows = q_ref.shape[0]
    has_prev, own_prefix = scalars[0], scalars[1]
    lane = lane_index(rows)
    first = lane < HEAD_DIM
    zero = jnp.zeros((rows, LANES), BF16)
    queries = q_ref[...]
    less = three_columns(-lse_ref[...], lane & (HEAD_DIM - 1)).astype(BF16)
    query_aug[0, :, :LANES] = jnp.where(first, queries, zero)
    query_aug[0, :, LANES:] = jnp.where(first, less, zero)
    query_aug[1, :, :LANES] = jnp.where(first, zero, queries)
    query_aug[1, :, LANES:] = jnp.where(first, zero, less)
    ones = jnp.where((lane_index(block_k) & (HEAD_DIM - 1)) < 3, 1.0, 0.0).astype(BF16)

    keys_both[:rows] = prev_k_ref[...]
    keys_both[rows:] = own_k_ref[...]

    def visit(line, start):
        keys_aug = jnp.concatenate([keys_both[pl.ds(line, block_k), :], ones], axis=1)
        key_pos = line - rows + lax.broadcasted_iota(jnp.int32, (block_k, 1), 0)
        query_pos = start + lax.broadcasted_iota(jnp.int32, (1, block_q), 1)
        visible = key_pos <= jnp.maximum(query_pos, own_prefix - 1)
        for h in range(2):
            scores = nt(keys_aug, query_aug[h, pl.ds(start, block_q), :]) * LOG2E
            scores = jnp.where(visible, scores, MASK_FILL)
            weights_ref[h, pl.ds(line, block_k), pl.ds(start, block_q)] = jnp.exp2(
                scores
            ).astype(BF16)

    def nothing(*unused):
        return None

    over_visible(has_prev, own_prefix, rows, block_q, block_k, nothing, visit, nothing)


def attention_weights(scalars, queries, prev, own, lse, block_q=1024, block_k=512):
    rows, width = queries.shape
    pairs = width // LANES
    spec = pl.BlockSpec((rows, LANES), lambda h, scalars: (0, h))
    return pl.pallas_call(
        partial(weights_kernel, block_q, block_k),
        grid_spec=pltpu.PrefetchScalarGridSpec(
            num_scalar_prefetch=1,
            grid=(pairs,),
            in_specs=[spec] * 4,
            out_specs=pl.BlockSpec((None, 2, 2 * rows, rows), lambda h, scalars: (h, 0, 0, 0)),
            scratch_shapes=[
                pltpu.VMEM((2, rows, 2 * LANES), BF16),
                pltpu.VMEM((2 * rows, LANES), BF16),
            ],
        ),
        out_shape=jax.ShapeDtypeStruct((pairs, 2, 2 * rows, rows), BF16),
        compiler_params=pltpu.CompilerParams(vmem_limit_bytes=VMEM_LIMIT),
        cost_estimate=pl.CostEstimate(
            flops=8 * rows * rows * width,
            bytes_accessed=4 * pairs * rows * rows * 2 + 10 * rows * width,
            transcendentals=2 * rows * rows * width // HEAD_DIM,
        ),
        name="attention_weights",
    )(scalars, queries, prev, own, lse)


def backward_kernel(
    block_q,
    block_k,
    scalars,
    q_ref,
    prev_k_ref,
    prev_v_ref,
    own_k_ref,
    own_v_ref,
    out_ref,
    grad_ref,
    weights_ref,
    dq_ref,
    prev_grad_ref,
    own_grad_ref,
    grad_aug,
    keys_turned,
    values_both,
    dq_total,
    dk_total,
    dv_total,
):
    rows = q_ref.shape[0]
    has_prev, own_prefix = scalars[0], scalars[1]
    lane = lane_index(rows)
    first = lane < HEAD_DIM
    zero = jnp.zeros((rows, LANES), BF16)
    grads = grad_ref[...]
    products = grads.astype(F32) * out_ref[...].astype(F32)
    delta_a = jnp.sum(jnp.where(first, products, 0.0), axis=1, keepdims=True)
    delta_b = jnp.sum(jnp.where(first, 0.0, products), axis=1, keepdims=True)
    less = three_columns(-jnp.where(first, delta_a, delta_b), lane & (HEAD_DIM - 1)).astype(BF16)
    grad_aug[0, :, :LANES] = jnp.where(first, grads, zero)
    grad_aug[0, :, LANES:] = jnp.where(first, less, zero)
    grad_aug[1, :, :LANES] = jnp.where(first, zero, grads)
    grad_aug[1, :, LANES:] = jnp.where(first, zero, less)
    ones = jnp.where((lane_index(block_k) & (HEAD_DIM - 1)) < 3, 1.0, 0.0).astype(BF16)
    keys_first = lane_index(block_k) < HEAD_DIM
    dq_total[...] = jnp.zeros_like(dq_total)

    keys_turned[:, :rows] = prev_k_ref[...].T
    keys_turned[:, rows:] = own_k_ref[...].T
    values_both[:rows] = prev_v_ref[...]
    values_both[rows:] = own_v_ref[...]

    def visit(line, start):
        lines, queries_at = pl.ds(line, block_k), pl.ds(start, block_q)
        values_aug = jnp.concatenate([values_both[lines, :], ones], axis=1)
        probs, d_scores = [], []
        for h in range(2):
            part = weights_ref[h, lines, queries_at]
            centered = nt(values_aug, grad_aug[h, queries_at, :])
            d_scores.append((part.astype(F32) * centered).astype(BF16))
            probs.append(part)
        here_grads, here_queries = grad_ref[queries_at, :], q_ref[queries_at, :]
        dv_total[...] += jnp.where(keys_first, nn(probs[0], here_grads), nn(probs[1], here_grads))
        dk_total[...] += jnp.where(
            keys_first, nn(d_scores[0], here_queries), nn(d_scores[1], here_queries)
        )
        for h in range(2):
            head = slice(h * HEAD_DIM, (h + 1) * HEAD_DIM)
            dq_total[head, queries_at] += nn(keys_turned[head, lines], d_scores[h])

    @pl.when(has_prev == 0)
    def _():
        prev_grad_ref[0] = zero
        prev_grad_ref[1] = zero

    def clear():
        dk_total[...] = jnp.zeros_like(dk_total)
        dv_total[...] = jnp.zeros_like(dv_total)

    def put(line):
        @pl.when(line < rows)
        def _():
            prev_grad_ref[0, pl.ds(line, block_k), :] = dk_total[...].astype(BF16)
            prev_grad_ref[1, pl.ds(line, block_k), :] = dv_total[...].astype(BF16)

        @pl.when(line >= rows)
        def _():
            at = pl.multiple_of(line - rows, block_k)
            own_grad_ref[0, pl.ds(at, block_k), :] = dk_total[...].astype(BF16)
            own_grad_ref[1, pl.ds(at, block_k), :] = dv_total[...].astype(BF16)

    over_visible(has_prev, own_prefix, rows, block_q, block_k, clear, visit, put)
    dq_ref[...] = (dq_total[...].T * (HEAD_DIM**-0.5)).astype(BF16)


def attention_backward(
    scalars, queries, prev, own, out, grads, weights, begin, count, block_q=BWD_Q, block_k=BWD_K
):
    rows, width = queries.shape
    pairs = width // LANES

    def spec(offset):
        return pl.BlockSpec((rows, LANES), lambda h, scalars: (0, h + begin + offset))

    both = pl.BlockSpec((2, rows, LANES), lambda h, scalars: (0, 0, h))
    share = count * LANES
    return pl.pallas_call(
        partial(backward_kernel, block_q, block_k),
        grid_spec=pltpu.PrefetchScalarGridSpec(
            num_scalar_prefetch=1,
            grid=(count,),
            in_specs=[spec(0), spec(0), spec(pairs), spec(0), spec(pairs), spec(0), spec(0)]
            + [pl.BlockSpec((None, 2, 2 * rows, rows), lambda h, scalars: (h + begin, 0, 0, 0))],
            out_specs=[pl.BlockSpec((rows, LANES), lambda h, scalars: (0, h)), both, both],
            scratch_shapes=[
                pltpu.VMEM((2, rows, 2 * LANES), BF16),
                pltpu.VMEM((LANES, 2 * rows), BF16),
                pltpu.VMEM((2 * rows, LANES), BF16),
                pltpu.VMEM((LANES, rows), F32),
                pltpu.VMEM((block_k, LANES), F32),
                pltpu.VMEM((block_k, LANES), F32),
            ],
        ),
        out_shape=[
            jax.ShapeDtypeStruct((rows, share), BF16),
            jax.ShapeDtypeStruct((2, rows, share), BF16),
            jax.ShapeDtypeStruct((2, rows, share), BF16),
        ],
        compiler_params=pltpu.CompilerParams(vmem_limit_bytes=VMEM_LIMIT),
        cost_estimate=pl.CostEstimate(
            flops=60 * rows * rows * share,
            bytes_accessed=26 * rows * share,
            transcendentals=2 * rows * rows * share // HEAD_DIM,
        ),
        name="attention_backward",
    )(scalars, queries, prev, prev, own, own, out, grads, weights)


def expert_kernel(
    experts,
    block_r,
    scalars,
    rows_ref,
    cot_ref,
    w_in_ref,
    w_down_ref,
    router_ref,
    y_before_ref,
    y_ref,
    dm_ref,
    act_ref,
    du_ref,
    dy_ref,
    dz_ref,
    y_total,
    dm_total,
    probs,
):
    step = pl.program_id(0)
    slots, width = cot_ref.shape[1], cot_ref.shape[2]
    sources = block_r // slots
    lane = lane_index(block_r)
    is_mine = lane == scalars[0]

    def over_rows(work):
        for b in range(rows_ref.shape[0] // block_r):
            work(slice(b * block_r, (b + 1) * block_r), slice(b * sources, (b + 1) * sources))

    def cots(source):
        return cot_ref[source].reshape(block_r, width).astype(F32)

    @pl.when(step == 0)
    def _():
        def gate(here, source):
            logits = nt(rows_ref[here, :], router_ref[...])
            logits = jnp.where(lane < experts, logits, MASK_FILL)
            spread = jnp.exp(logits - jnp.max(logits, axis=1, keepdims=True))
            part = spread / jnp.sum(spread, axis=1, keepdims=True)
            probs[here, :] = part
            mine = jnp.sum(jnp.where(is_mine, part, 0.0), axis=1, keepdims=True)
            dy_ref[here, :] = (mine * cots(source)).astype(BF16)
            y_total[here, :] = jnp.zeros((block_r, y_total.shape[1]), F32)
            dm_total[here, :] = jnp.zeros((block_r, dm_total.shape[1]), F32)

        over_rows(gate)

    def hidden_block(here, source):
        u = nn(rows_ref[here, :], w_in_ref[...])
        d_act = nt(dy_ref[here, :], w_down_ref[...])
        square = u * u
        bend = jnp.tanh(u * (GELU_A + (GELU_A * GELU_B) * square))
        half = 0.5 + 0.5 * bend
        act = (u * half).astype(BF16)
        slope = half + (0.5 * u) * (1.0 - bend * bend) * (
            GELU_A + (3.0 * GELU_A * GELU_B) * square
        )
        du = (d_act * slope).astype(BF16)
        act_ref[here, :] = act
        du_ref[here, :] = du
        y_total[here, :] += nn(act, w_down_ref[...])
        dm_total[here, :] += nt(du, w_in_ref[...])

    over_rows(hidden_block)

    @pl.when(step == pl.num_programs(0) - 1)
    def _():
        def finish(here, source):
            y = y_total[here, :].astype(BF16)
            y_ref[source] = y.reshape(sources, slots, width)
            d_gate = jnp.sum(cots(source) * y.astype(F32), axis=1, keepdims=True)
            part = probs[here, :]
            mine = jnp.sum(jnp.where(is_mine, part, 0.0), axis=1, keepdims=True)
            dz = ((d_gate * mine) * (jnp.where(is_mine, 1.0, 0.0) - part)).astype(BF16)
            dz = jnp.where(lane < experts, dz, jnp.zeros_like(dz))
            dz_ref[here, :] = dz
            dm_ref[here, :] = (dm_total[here, :] + nn(dz, router_ref[...])).astype(BF16)

        over_rows(finish)


def run_expert(
    scalars, rows_in, cots, w_in, w_down, router, y_before, chunk, experts, block_h=512, block_r=1024
):
    rows, width = rows_in.shape
    half = w_in.shape[2]
    per_half = half // block_h
    whole = pl.BlockSpec((rows, width), lambda j, s: (0, 0))
    hidden = pl.BlockSpec((rows, block_h), lambda j, s: (0, j))
    mine = pl.BlockSpec(
        (cots.shape[0], None, cots.shape[2], width), lambda j, s: (0, chunk, 0, 0)
    )

    def which(j, s):
        return lax.rem(j // per_half + s[1], 2)

    first = y_before is None
    return pl.pallas_call(
        partial(expert_kernel, experts, block_r),
        grid_spec=pltpu.PrefetchScalarGridSpec(
            num_scalar_prefetch=1,
            grid=(2 * per_half,),
            in_specs=[
                whole,
                mine,
                pl.BlockSpec(
                    (None, width, block_h), lambda j, s: (which(j, s), 0, lax.rem(j, per_half))
                ),
                pl.BlockSpec(
                    (None, block_h, width), lambda j, s: (which(j, s), lax.rem(j, per_half), 0)
                ),
                pl.BlockSpec((LANES, width), lambda j, s: (0, 0)),
                pl.BlockSpec(memory_space=pl.ANY),
            ],
            out_specs=[
                mine,
                whole,
                hidden,
                hidden,
                whole,
                pl.BlockSpec((rows, LANES), lambda j, s: (0, 0)),
            ],
            scratch_shapes=[
                pltpu.VMEM((rows, width), F32),
                pltpu.VMEM((rows, width), F32),
                pltpu.VMEM((rows, LANES), F32),
            ],
        ),
        out_shape=[
            jax.ShapeDtypeStruct(cots.shape, BF16),
            jax.ShapeDtypeStruct((rows, width), BF16),
            jax.ShapeDtypeStruct((rows, 2 * half), BF16),
            jax.ShapeDtypeStruct((rows, 2 * half), BF16),
            jax.ShapeDtypeStruct((rows, width), BF16),
            jax.ShapeDtypeStruct((rows, LANES), BF16),
        ],
        input_output_aliases={} if first else {6: 0},
        compiler_params=pltpu.CompilerParams(vmem_limit_bytes=VMEM_LIMIT),
        cost_estimate=pl.CostEstimate(
            flops=16 * rows * width * half,
            bytes_accessed=8 * width * half + 12 * rows * width + 8 * rows * half,
            transcendentals=2 * rows * half,
        ),
        name="expert_rows",
    )(scalars, rows_in, cots, w_in, w_down, router, scalars if first else y_before)


def expert_weights_kernel(chunks, add, *refs):
    rows_refs, dy_refs, act_refs, du_refs = (
        refs[i * chunks : (i + 1) * chunks] for i in range(4)
    )
    rest = refs[4 * chunks :]
    d_in_ref, d_down_ref, turned = rest[-3:]
    rows = rows_refs[0].shape[0]

    @pl.when(pl.program_id(0) == 0)
    def _():
        for c in range(chunks):
            turned[:, c * rows : (c + 1) * rows] = rows_refs[c][...].T

    d_in, d_down = None, None
    for c in range(chunks):
        part = nn(turned[:, c * rows : (c + 1) * rows], du_refs[c][...])
        d_in = part if d_in is None else d_in + part
        part = tn(act_refs[c][...], dy_refs[c][...])
        d_down = part if d_down is None else d_down + part
    if add:
        d_in = d_in + rest[0][...].astype(F32)
        d_down = d_down + rest[1][...].astype(F32)
    d_in_ref[...] = d_in.astype(d_in_ref.dtype)
    d_down_ref[...] = d_down.astype(d_down_ref.dtype)


def expert_weights(rows_in, dy, act, du, half_index, got, block_h=512):
    chunks = len(rows_in)
    rows, width = rows_in[0].shape
    half = du[0].shape[1] // 2
    steps = half // block_h
    whole = pl.BlockSpec((rows, width), lambda j: (0, 0))
    hidden = pl.BlockSpec((rows, block_h), lambda j: (0, j + half_index * steps))
    columns = pl.BlockSpec((width, block_h), lambda j: (0, j))
    lines = pl.BlockSpec((block_h, width), lambda j: (j, 0))
    dtype = BF16 if got is None else F32
    extra = () if got is None else tuple(got)
    return pl.pallas_call(
        partial(expert_weights_kernel, chunks, got is not None),
        grid=(steps,),
        in_specs=[whole] * (2 * chunks) + [hidden] * (2 * chunks) + [columns, lines][: len(extra)],
        out_specs=[columns, lines],
        out_shape=[
            jax.ShapeDtypeStruct((width, half), dtype),
            jax.ShapeDtypeStruct((half, width), dtype),
        ],
        scratch_shapes=[pltpu.VMEM((width, chunks * rows), BF16)],
        compiler_params=pltpu.CompilerParams(vmem_limit_bytes=VMEM_LIMIT),
        cost_estimate=pl.CostEstimate(
            flops=4 * chunks * rows * width * half,
            bytes_accessed=4 * chunks * rows * (width + half) + 8 * width * half,
            transcendentals=0,
        ),
        name="expert_weights",
    )(*rows_in, *dy, *act, *du, *extra)


def both_sums(own_ref, back_ref, i):
    return (own_ref[i].astype(F32) + back_ref[i].astype(F32)).astype(BF16)


def pair_weights_kernel(with_context, scalars, *refs):
    in_ref, dq_ref, own_ref, back_ref, vectors_ref = refs[:5]
    outs = refs[-2:]
    is_first = scalars[0] == 0
    half = outs[0].shape[0]
    column = 0

    def put(top, bottom):
        nonlocal column
        here = slice(column, column + top.shape[1])
        column += top.shape[1]
        top, bottom = top.astype(BF16), bottom.astype(BF16)
        outs[0][:, here] = jnp.where(is_first, top, bottom)
        outs[1][:, here] = jnp.where(is_first, bottom, top)

    def products(left, rights):
        turned = left[...].T
        for right in rights:
            put(nn(turned[:half], right), nn(turned[half:], right))

    products(in_ref, [dq_ref[...]] + [both_sums(own_ref, back_ref, i) for i in range(2)])
    if with_context:
        products(refs[5], [refs[6][...]])
    turned = vectors_ref[...].T
    put(turned[:half], turned[half:])


def pair_weights(half_index, attn_in, grads, vectors, context_side=()):
    d_query, own_grad, back_grad = grads
    rows, width = attn_in.shape
    columns = 3 * d_query.shape[1] + vectors.shape[0]
    if context_side:
        columns += context_side[1].shape[1]

    def full(shape):
        return pl.BlockSpec(shape, lambda i, s: (0,) * len(shape))

    arrays = [attn_in, d_query, own_grad, back_grad, vectors] + list(context_side)
    out = full((width // 2, columns))
    return pl.pallas_call(
        partial(pair_weights_kernel, bool(context_side)),
        grid_spec=pltpu.PrefetchScalarGridSpec(
            num_scalar_prefetch=1,
            grid=(1,),
            in_specs=[full(x.shape) for x in arrays],
            out_specs=[out, out],
        ),
        out_shape=[jax.ShapeDtypeStruct((width // 2, columns), BF16)] * 2,
        compiler_params=pltpu.CompilerParams(vmem_limit_bytes=40 << 20),
        cost_estimate=pl.CostEstimate(
            flops=2 * rows * width * columns,
            bytes_accessed=4 * (rows + width) * columns,
            transcendentals=0,
        ),
        name="pair_weights",
    )(half_index, *arrays)


def normalized(values):
    center = values - jnp.mean(values, axis=1, keepdims=True)
    inv_std = lax.rsqrt(jnp.mean(center * center, axis=1, keepdims=True) + NORM_EPSILON)
    return center * inv_std, inv_std


def rows_in_order(is_first, own_ref, other_ref):
    own, other = own_ref[...], other_ref[...]
    return jnp.concatenate(
        [jnp.where(is_first, own, other), jnp.where(is_first, other, own)], axis=0
    )


def key_value_kernel(scalars, tokens_ref, norm_ref, own_ref, other_ref, add_ref, out_ref, in_ref):
    @pl.when(pl.program_id(0) == 0)
    def _():
        normed, inv_std = normalized(tokens_ref[...].astype(F32))
        in_ref[...] = (normed * norm_ref[0:1, :] + norm_ref[1:2, :]).astype(BF16)

    weight = rows_in_order(scalars[0] == 0, own_ref, other_ref)
    out_ref[...] = (nn(in_ref[...], weight) + add_ref[...]).astype(BF16)


def query_kernel(scalars, in_ref, own_ref, other_ref, add_ref, out_ref):
    weight = rows_in_order(scalars[0] == 0, own_ref, other_ref)
    out_ref[...] = ((nn(in_ref[...], weight) + add_ref[...]) * (HEAD_DIM**-0.5)).astype(BF16)


def project(half_index, rows_in, w_own, w_other, bias, norm=None, block_n=512):
    rows, width = rows_in.shape
    columns = bias.shape[0]
    begin = 0 if norm is None else width // block_n
    half = pl.BlockSpec((width // 2, block_n), lambda j, s: (0, begin + j))
    whole = pl.BlockSpec((rows, width), lambda j, s: (0, 0))
    line = pl.BlockSpec((1, block_n), lambda j, s: (0, j))
    block = pl.BlockSpec((rows, block_n), lambda j, s: (0, j))
    shape = jax.ShapeDtypeStruct((rows, columns), BF16)
    if norm is None:
        in_specs, out_specs, out_shape = [whole, half, half, line], block, shape
        arrays = (rows_in, w_own, w_other, bias[None, :])
    else:
        in_specs = [whole, pl.BlockSpec((2, width), lambda j, s: (0, 0)), half, half, line]
        out_specs = [block, whole]
        out_shape = [shape, jax.ShapeDtypeStruct((rows, width), BF16)]
        arrays = (rows_in, norm, w_own, w_other, bias[None, :])
    return pl.pallas_call(
        query_kernel if norm is None else key_value_kernel,
        grid_spec=pltpu.PrefetchScalarGridSpec(
            num_scalar_prefetch=1,
            grid=(columns // block_n,),
            in_specs=in_specs,
            out_specs=out_specs,
        ),
        out_shape=out_shape,
        compiler_params=pltpu.CompilerParams(vmem_limit_bytes=VMEM_LIMIT),
        cost_estimate=pl.CostEstimate(
            flops=2 * rows * width * columns,
            bytes_accessed=2 * (rows * width + width * columns + rows * columns),
            transcendentals=0,
        ),
        name="project",
    )(half_index, *arrays)


def first_norm_kernel(
    shares, scalars, tokens_ref, dh_ref, gain_ref, w_own_ref, w_other_ref, *refs
):
    parts = len(shares)
    out_ref, sums_ref = refs[3 * parts], refs[3 * parts + 1]
    width = tokens_ref.shape[1]
    d_own, d_other = None, None
    query_sums, value_sums = [], []
    begin = 0
    for p, share in enumerate(shares):
        dq, own_grad, back_grad = refs[3 * p : 3 * p + 3]
        for i in range(3):
            grads = dq[...] if i == 0 else both_sums(own_grad, back_grad, i - 1)
            at = i * width + begin
            part = nt(grads, w_own_ref[:, at : at + share])
            d_own = part if d_own is None else d_own + part
            part = nt(grads, w_other_ref[:, at : at + share])
            d_other = part if d_other is None else d_other + part
            if i != 1:
                sums = jnp.sum(grads.astype(F32), axis=0, keepdims=True)
                (query_sums if i == 0 else value_sums).append(sums)
        begin += share
    is_first = scalars[0] == 0
    d_norm = jnp.concatenate(
        [jnp.where(is_first, d_own, d_other), jnp.where(is_first, d_other, d_own)], axis=1
    )
    normed, inv_std = normalized(tokens_ref[...].astype(F32))
    scaled = d_norm * gain_ref[...]
    back = inv_std * (
        scaled
        - jnp.mean(scaled, axis=1, keepdims=True)
        - normed * jnp.mean(scaled * normed, axis=1, keepdims=True)
    )
    out_ref[...] = (dh_ref[...] + back).astype(BF16)
    sums = jnp.concatenate(
        [
            jnp.sum(d_norm * normed, axis=0, keepdims=True),
            jnp.sum(d_norm, axis=0, keepdims=True),
            jnp.concatenate(query_sums, axis=1),
            jnp.concatenate(value_sums, axis=1),
        ],
        axis=0,
    )

    @pl.when(pl.program_id(0) == 0)
    def _():
        sums_ref[...] = jnp.zeros_like(sums_ref)

    sums_ref[0:4, :] += sums


def first_norm(half_index, tokens, d_hidden, gain, w_own, w_other, grads, block_r=256):
    rows, width = tokens.shape
    shares = tuple(g[0].shape[1] for g in grads)
    lines = pl.BlockSpec((block_r, width), lambda i, s: (i, 0))
    weight = pl.BlockSpec((width // 2, 3 * width), lambda i, s: (0, 0))
    specs, arrays = [], []
    for three, share in zip(grads, shares):
        both = pl.BlockSpec((2, block_r, share), lambda i, s: (0, i, 0))
        specs += [pl.BlockSpec((block_r, share), lambda i, s: (i, 0)), both, both]
        arrays += list(three)
    return pl.pallas_call(
        partial(first_norm_kernel, shares),
        grid_spec=pltpu.PrefetchScalarGridSpec(
            num_scalar_prefetch=1,
            grid=(rows // block_r,),
            in_specs=[lines, lines, pl.BlockSpec((1, width), lambda i, s: (0, 0)), weight, weight]
            + specs,
            out_specs=[lines, pl.BlockSpec((LANES, width), lambda i, s: (0, 0))],
        ),
        out_shape=[
            jax.ShapeDtypeStruct((rows, width), BF16),
            jax.ShapeDtypeStruct((LANES, width), F32),
        ],
        compiler_params=pltpu.CompilerParams(vmem_limit_bytes=40 << 20),
        cost_estimate=pl.CostEstimate(
            flops=6 * rows * width * width,
            bytes_accessed=14 * rows * width + 6 * width * width,
            transcendentals=rows,
        ),
        name="first_norm",
    )(half_index, tokens, d_hidden, gain[None, :], w_own, w_other, *arrays)


def layer_norm(values, norm_gain, norm_bias):
    center = values - jnp.mean(values, axis=-1, keepdims=True)
    inv_std = lax.rsqrt(jnp.mean(center * center, axis=-1, keepdims=True) + NORM_EPSILON)
    normed = center * inv_std
    return (normed * norm_gain + norm_bias, normed, inv_std)


def norm_backward(grad_out, normed, inv_std, norm_gain):
    scaled = grad_out * norm_gain
    return inv_std * (
        scaled
        - jnp.mean(scaled, axis=-1, keepdims=True)
        - normed * jnp.mean(scaled * normed, axis=-1, keepdims=True)
    )


def swapped(array):
    return lax.ppermute(array, "fsdp", [(0, 1), (1, 0)])


def exchanged(array):
    return lax.all_to_all(array, "expert", split_axis=0, concat_axis=0, tiled=True)


def body(
    tokens,
    out_grad,
    routes,
    prefix,
    ln1_gain,
    ln1_bias,
    w_qkv,
    q_bias,
    v_bias,
    attention_output_weight,
    attention_output_bias,
    ln2_gain,
    ln2_bias,
    w_router,
    moe_bias,
    w_in,
    w_down,
):
    experts = lax.axis_size("expert")
    my_expert = lax.axis_index("expert")
    my_half = lax.axis_index("fsdp")
    is_first = my_half == 0
    rows, width = tokens.shape[1], tokens.shape[2]
    half_width = width // 2
    slots = max(2, 2 * rows // experts) // CHUNKS
    chunk_rows = experts * slots

    def in_order(own, other, axis):
        return jnp.where(
            is_first,
            jnp.concatenate([own, other], axis=axis),
            jnp.concatenate([other, own], axis=axis),
        )

    small = jnp.concatenate(
        [
            jnp.stack(
                [
                    ln1_gain,
                    ln1_bias,
                    q_bias,
                    v_bias,
                    attention_output_bias,
                    ln2_gain,
                    ln2_bias,
                    moe_bias,
                ]
            ),
            w_router.T,
        ],
        axis=0,
    )
    small = in_order(small, swapped(small), 1)
    vectors = small[:8].astype(F32)
    norm1_gain, norm1_bias, query_bias, value_bias = (vectors[i] for i in range(4))
    output_bias, norm2_gain, norm2_bias, expert_bias = (vectors[i] for i in range(4, 8))
    router_t = small[8:]
    w_qkv_other = swapped(w_qkv)
    own_index = my_half[None].astype(jnp.int32)
    out_weight = lax.all_gather(attention_output_weight, "fsdp", axis=0, tiled=True)
    w_in_both = lax.all_gather(w_in[0], "fsdp", axis=0, tiled=False)
    w_down_both = lax.all_gather(w_down[0], "fsdp", axis=0, tiled=False)

    token_route = routes[0, :, 0]
    one_hot = token_route[:, None] == jnp.arange(experts, dtype=jnp.int32)[None, :]
    row_ids = jnp.arange(rows, dtype=jnp.int32)
    earlier_same = nn(
        (row_ids[None, :] < row_ids[:, None]).astype(BF16), one_hot.astype(BF16)
    )
    slot_index = jnp.sum(jnp.where(one_hot, earlier_same, 0.0), axis=-1).astype(jnp.int32)
    chunk_of = slot_index // slots
    place_in = token_route * slots + slot_index % slots
    buffer_ids = jnp.arange(chunk_rows, dtype=jnp.int32)

    def place_of(chunk):
        return jnp.where(chunk_of == chunk, place_in, -1)

    def picked(row_values, chunk):
        return nn(
            (buffer_ids[:, None] == place_of(chunk)[None, :]).astype(BF16), row_values
        ).astype(BF16)

    def sent(buffer):
        return exchanged(buffer.reshape(experts, slots, width)).reshape(chunk_rows, width)

    def picked_up(got):
        total = None
        for chunk in range(CHUNKS):
            part = nn((place_of(chunk)[:, None] == buffer_ids[None, :]).astype(BF16), got[chunk])
            total = part if total is None else total + part
        return total

    full_place = token_route * (CHUNKS * slots) + slot_index
    full_ids = jnp.arange(CHUNKS * chunk_rows, dtype=jnp.int32)
    cot_rows = nn((full_ids[:, None] == full_place[None, :]).astype(BF16), out_grad[0])
    cot_rows, tokens_in = lax.optimization_barrier((cot_rows.astype(BF16), tokens[0]))
    cot_rows = exchanged(cot_rows.reshape(experts, CHUNKS * slots, width)).reshape(
        experts, CHUNKS, slots, width
    )

    key_value, attn_in = project(
        own_index,
        tokens_in,
        w_qkv,
        w_qkv_other,
        jnp.concatenate([jnp.zeros_like(value_bias), value_bias]),
        vectors[0:2],
    )
    prev_key_value = lax.ppermute(key_value, "fsdp", [(0, 1)])
    queries = project(own_index, attn_in, w_qkv, w_qkv_other, query_bias)
    residual = tokens[0].astype(F32)
    scalars = jnp.stack([my_half, prefix[0] - my_half * rows]).astype(jnp.int32)
    context, lse = attention_forward(scalars, queries, prev_key_value, key_value)
    hidden = residual + (nn(context, out_weight) + output_bias)
    norm2_out, normed2, inv_std2 = layer_norm(hidden, norm2_gain, norm2_bias)
    mixed = norm2_out.astype(BF16)

    leaving = [picked(mixed, chunk) for chunk in range(CHUNKS)]
    weights = attention_weights(scalars, queries, prev_key_value, key_value, lse)
    leaving[-1], weights = lax.optimization_barrier((leaving[-1], weights))
    mixed_rows = [sent(rows_out) for rows_out in leaving]
    router_pad = jnp.pad(router_t, ((0, LANES - experts), (0, 0)))
    expert_scalars = jnp.stack([my_expert, my_half]).astype(jnp.int32)
    done, y_rows = [], None
    for c in range(CHUNKS):
        y_rows, *rest = run_expert(
            expert_scalars,
            mixed_rows[c],
            cot_rows,
            w_in_both,
            w_down_both,
            router_pad,
            y_rows,
            c,
            experts,
        )
        done.append(rest)
    d_mixed_chunks, act, du, dy, dz = ([d[i] for d in done] for i in range(5))
    back = [sent(d) for d in d_mixed_chunks]
    others = expert_weights(mixed_rows, dy, act, du, 1, None)
    d_router_t = None
    for c in range(CHUNKS):
        part = tn(dz[c], mixed_rows[c])
        d_router_t = part if d_router_t is None else d_router_t + part
    d_expert_bias = jnp.sum(out_grad[0].astype(F32), axis=0)
    back[-1], others, d_router_t, d_expert_bias = lax.optimization_barrier(
        (back[-1], others, d_router_t, d_expert_bias)
    )
    d_mixed = picked_up(back)
    got = [swapped(o) for o in others]
    out_cot = out_grad[0].astype(F32)
    d_norm2_gain = jnp.sum(d_mixed * normed2, axis=0)
    d_norm2_bias = jnp.sum(d_mixed, axis=0)
    d_hidden = out_cot + norm_backward(d_mixed, normed2, inv_std2, norm2_gain)
    d_attn = d_hidden.astype(BF16)
    d_output_bias = jnp.sum(d_attn.astype(F32), axis=0)
    d_context = nt(d_attn, out_weight).astype(BF16)

    logits = nt(mixed, router_t)
    router_probs = jax.nn.softmax(logits, axis=-1)
    gate_value = jnp.sum(jnp.where(one_hot, router_probs, 0.0), axis=-1)
    y_back = exchanged(y_rows.reshape(experts, CHUNKS * slots, width)).reshape(-1, width)
    early, line = d_router_t, jnp.arange(LANES, dtype=jnp.int32)[:, None]
    for i, vector in enumerate([d_expert_bias, d_norm2_gain, d_norm2_bias, d_output_bias]):
        early = early + jnp.where(line == experts + i, vector[None, :], 0.0)

    pairs = width // LANES
    groups = ((0, FIRST_PAIRS), (FIRST_PAIRS, pairs - FIRST_PAIRS))
    grads, sums = [], []
    for number, (begin, count) in enumerate(groups):
        d_query, prev_grad, own_grad = attention_backward(
            scalars,
            queries,
            prev_key_value,
            key_value,
            context,
            d_context,
            weights,
            begin,
            count,
        )
        returned = lax.ppermute(prev_grad, "fsdp", [(1, 0)])
        group = (d_query, own_grad, returned)
        grads.append(group)
        if number == 0:
            vectors_in, context_side = early, (context, d_attn)
        else:
            d_tokens, norm_sums = first_norm(
                own_index, tokens[0], d_hidden, norm1_gain, w_qkv, w_qkv_other, grads
            )
            norm_sums, sums[0] = lax.optimization_barrier((norm_sums, sums[0]))
            vectors_in, context_side = norm_sums, ()
        own_part, other_part = pair_weights(own_index, attn_in, group, vectors_in, context_side)
        own_part = (own_part.astype(F32) + swapped(other_part).astype(F32)).astype(BF16)
        blocks = own_part.reshape(experts, half_width // experts, own_part.shape[1])
        if number < len(groups) - 1:
            d_context, blocks, y_back = lax.optimization_barrier((d_context, blocks, y_back))
        sums.append(jnp.sum(exchanged(blocks).astype(F32), axis=0))
    d_w_in, d_w_down = expert_weights(mixed_rows, dy, act, du, 0, got)
    expert_value = nn((full_place[:, None] == full_ids[None, :]).astype(BF16), y_back)
    output = hidden + gate_value[:, None] * expert_value + expert_bias

    sum_qkv = jnp.concatenate(
        [
            sums[g][:, i * count * LANES : (i + 1) * count * LANES]
            for i in range(3)
            for g, (begin, count) in enumerate(groups)
        ],
        axis=1,
    )
    sum_out = sums[0][:, 3 * groups[0][1] * LANES :]
    sum_last = sums[-1][:, 3 * groups[-1][1] * LANES :]
    return (
        output.astype(BF16)[None],
        d_tokens[None],
        sum_last[:, 0],
        sum_last[:, 1],
        sum_qkv,
        sum_last[:, 2],
        sum_last[:, 3],
        sum_out[:, :width],
        sum_out[:, width + experts + 3],
        sum_out[:, width + experts + 1],
        sum_out[:, width + experts + 2],
        sum_out[:, width : width + experts],
        sum_out[:, width + experts],
        d_w_in[None],
        d_w_down[None],
    )


def solution(mesh):
    vector = P(("fsdp", "expert"))
    matrix = P(("fsdp", "expert"), None)
    tokens = P("expert", "fsdp", None)
    return jax.shard_map(
        body,
        mesh=mesh,
        in_specs=(
            tokens,
            tokens,
            tokens,
            P("expert"),
            P("fsdp"),
            P("fsdp"),
            P("fsdp", None),
            P("fsdp"),
            P("fsdp"),
            P("fsdp", None),
            P("fsdp"),
            P("fsdp"),
            P("fsdp"),
            P("fsdp", None),
            P("fsdp"),
            P("expert", None, "fsdp"),
            P("expert", "fsdp", None),
        ),
        out_specs=(
            tokens,
            tokens,
            vector,
            vector,
            matrix,
            vector,
            vector,
            matrix,
            vector,
            vector,
            vector,
            matrix,
            vector,
            P("expert", None, "fsdp"),
            P("expert", "fsdp", None),
        ),
        check_vma=False,
    )
```
